32 devices in a mesh: dp: 8 (over z, x), tensor: 4 (over y, core).
Axes of the slice: x: 2, y: 2, z: 4, core: 2. Of those that a mesh axis runs over, the one named last changes fastest.
Arguments:
- tokens: bfloat16 [16384, 768], P(('dp', 'tensor')), may hold values from -6 to 6
- seq_counts: int32 [8], P('dp'), may hold values from 1 to 2, as said below
- seq_lengths: int32 [8, 2], P('dp'), may hold values from 512 to 1024, as said below
- norm1_gain: float32 [768], replicated, may hold values from 0.5 to 1.5
- norm1_bias: float32 [768], replicated, may hold values from -1.75 to 1.75
- in_weight: bfloat16 [3, 768, 768], P(None, 'tensor'), may hold values from -0.21875 to 0.21875
- in_bias: float32 [3, 768], P(None, 'tensor'), may hold values from -1.75 to 1.75
- conv_weight: float32 [3, 3, 768], P(None, None, 'tensor'), may hold values from -3 to 3
- conv_bias: float32 [3, 768], P(None, 'tensor'), may hold values from -1.75 to 1.75
- filter_w1: float32 [33, 64], replicated, may hold values from -1 to 1
- filter_b1: float32 [64], replicated, may hold values from -3 to 3
- filter_freq1: float32 [64], replicated, may hold values from 0.6 to 1.6
- filter_w2: float32 [64, 64], replicated, may hold values from -0.75 to 0.75
- filter_b2: float32 [64], replicated, may hold values from -3 to 3
- filter_freq2: float32 [64], replicated, may hold values from 0.6 to 1.6
- filter_w3: float32 [64, 768], P(None, 'tensor'), may hold values from -0.0625 to 0.0625
- filter_bias: float32 [768], P('tensor'), may hold values from -6 to 6
- out_weight: bfloat16 [768, 768], P('tensor'), may hold values from -0.21875 to 0.21875
- out_bias: float32 [768], replicated, may hold values from -1.75 to 1.75
- norm2_gain: float32 [768], replicated, may hold values from 0.5 to 1.5
- norm2_bias: float32 [768], replicated, may hold values from -1.75 to 1.75
- up_weight: bfloat16 [768, 3072], P(None, 'tensor'), may hold values from -0.21875 to 0.21875
- up_bias: float32 [3072], P('tensor'), may hold values from -1.75 to 1.75
- down_weight: bfloat16 [3072, 768], P('tensor'), may hold values from -0.109375 to 0.109375
- down_bias: float32 [768], replicated, may hold values from -1.75 to 1.75
- cotangent: bfloat16 [16384, 768], P(('dp', 'tensor')), may hold values from -6 to 6
Outputs:
- activations: bfloat16 [16384, 768], P(('dp', 'tensor'))
- input_grad: float32 [16384, 768], P(('dp', 'tensor'))
- grad_norm1_gain: float32 [768], replicated
- grad_norm1_bias: float32 [768], replicated
- grad_in_weight: float32 [3, 768, 768], P(None, 'tensor', 'dp')
- grad_in_bias: float32 [3, 768], P(None, 'tensor')
- grad_conv_weight: float32 [3, 3, 768], P(None, None, 'tensor')
- grad_conv_bias: float32 [3, 768], P(None, 'tensor')
- grad_filter_w1: float32 [33, 64], replicated
- grad_filter_b1: float32 [64], replicated
- grad_filter_freq1: float32 [64], replicated
- grad_filter_w2: float32 [64, 64], replicated
- grad_filter_b2: float32 [64], replicated
- grad_filter_freq2: float32 [64], replicated
- grad_filter_w3: float32 [64, 768], P('dp', 'tensor')
- grad_filter_bias: float32 [768], P('tensor')
- grad_out_weight: float32 [768, 768], P('tensor', 'dp')
- grad_out_bias: float32 [768], replicated
- grad_norm2_gain: float32 [768], replicated
- grad_norm2_bias: float32 [768], replicated
- grad_up_weight: float32 [768, 3072], P('dp', 'tensor')
- grad_up_bias: float32 [3072], P('tensor')
- grad_down_weight: float32 [3072, 768], P('tensor', 'dp')
- grad_down_bias: float32 [768], replicated
The draws below stay inside these ranges and needn't reach their ends.
Inputs may be any that keep to these rules, and one draw needn't show every extreme that they name: `seq_counts`: half of the dp indices hold 2 sequences and the others 1, in their first slots. `seq_lengths`: only the slots that seq_counts marks as used carry a sequence; the others' entries are ignored. Every draw has a used slot of length 1024.
All inputs are finite; a program needn't handle non-finite values.
Results may differ from the reference program's by a relative error of at most 0.012.
Values may be sent and summed in bfloat16 or wider, within the bound.
A program may use at most 256 MiB of HBM per device.

```python
import math
import jax
import jax.numpy as jnp
from jax import lax

D = 768
FF = 3072
FILTER_HIDDEN = 64
BANDS = 16
SHORT = 3
SEQ_LEN = 1024
SLOTS = 2
GROUPS = 8
TOKENS = 16384


def draw_seq_counts(key, part):
    order = jax.random.permutation(key, GROUPS)
    return (1 + (order < GROUPS // 2)).astype(jnp.int32)


def draw_seq_lengths(key, part):
    first_key, second_key = jax.random.split(key)
    drawn = jax.random.randint(first_key, (GROUPS, SLOTS), SEQ_LEN // 2, SEQ_LEN + 1)
    chosen = jax.random.randint(second_key, (), 0, GROUPS)
    group_index = lax.broadcasted_iota(jnp.int32, (GROUPS, SLOTS), 0)
    slot_index = lax.broadcasted_iota(jnp.int32, (GROUPS, SLOTS), 1)
    full_slot = (group_index == chosen) & (slot_index == 0)
    return jnp.where(full_slot, SEQ_LEN, drawn).astype(jnp.int32)


def level_of(key, dims, cuts, smallest, largest):
    level = 1.0
    for dim, shards_of in cuts:
        heights = jax.random.uniform(jax.random.fold_in(jax.random.fold_in(key, 6), dim), (shards_of,), jnp.float32, smallest / len(cuts), largest / len(cuts))
        level = level * jnp.repeat(jnp.exp(heights), dims[dim] // shards_of).reshape((-1,) + (1,) * (len(dims) - 1 - dim))
    return level


def scatter_about(stream_key, shape, spread, most, shards=(), held_as=jnp.bfloat16):
    entries = jax.random.normal(stream_key, shape, jnp.float32) * spread
    if len(shards) > 0:
        entries = level_of(stream_key, shape, shards, -0.22, 0.18) * entries
    return jnp.clip(entries, min=-most, max=most).astype(held_as)


def setup_inputs(seed: int = 0) -> dict:
    key_of = jax.random.split(jax.random.key(seed), 27)
    return {
        "tokens": scatter_about(key_of[0], (TOKENS, D), 1.0, 6.0, ((0, 32),)),
        "seq_counts": draw_seq_counts(jax.random.fold_in(key_of[26], 71), 0),
        "seq_lengths": draw_seq_lengths(jax.random.fold_in(key_of[26], 71), 0),
        "norm1_gain": jnp.clip(1.0 + 0.1 * jax.random.normal(key_of[3], (D,), jnp.float32), 0.5, 1.5),
        "norm1_bias": scatter_about(key_of[4], (D,), 0.3, 1.75, (), jnp.float32),
        "in_weight": scatter_about(key_of[5], (3, D, D), D ** -0.5, 0.21875, ((1, 4),)),
        "in_bias": scatter_about(key_of[6], (3, D), 0.3, 1.75, ((1, 4),), jnp.float32),
        "conv_weight": scatter_about(key_of[7], (SHORT, 3, D), 0.5, 3.0, ((2, 4),), jnp.float32),
        "conv_bias": scatter_about(key_of[8], (3, D), 0.3, 1.75, ((1, 4),), jnp.float32),
        "filter_w1": scatter_about(key_of[9], (2 * BANDS + 1, FILTER_HIDDEN), (2 * BANDS + 1) ** -0.5, 1.0, (), jnp.float32),
        "filter_b1": scatter_about(key_of[10], (FILTER_HIDDEN,), 0.5, 3.0, (), jnp.float32),
        "filter_freq1": jnp.clip(jnp.exp(jax.random.uniform(key_of[11], (FILTER_HIDDEN,), jnp.float32, math.log(0.6), math.log(1.6))), 0.6, 1.6),
        "filter_w2": scatter_about(key_of[12], (FILTER_HIDDEN, FILTER_HIDDEN), FILTER_HIDDEN ** -0.5, 0.75, (), jnp.float32),
        "filter_b2": scatter_about(key_of[13], (FILTER_HIDDEN,), 0.5, 3.0, (), jnp.float32),
        "filter_freq2": jnp.clip(jnp.exp(jax.random.uniform(key_of[14], (FILTER_HIDDEN,), jnp.float32, math.log(0.6), math.log(1.6))), 0.6, 1.6),
        "filter_w3": scatter_about(key_of[15], (FILTER_HIDDEN, D), (FILTER_HIDDEN * SEQ_LEN // 8) ** -0.5, 0.0625, ((1, 4),), jnp.float32),
        "filter_bias": scatter_about(key_of[16], (D,), 1.0, 6.0, ((0, 4),), jnp.float32),
        "out_weight": scatter_about(key_of[17], (D, D), D ** -0.5, 0.21875, ((0, 4),)),
        "out_bias": scatter_about(key_of[18], (D,), 0.3, 1.75, (), jnp.float32),
        "norm2_gain": jnp.clip(1.0 + 0.1 * jax.random.normal(key_of[19], (D,), jnp.float32), 0.5, 1.5),
        "norm2_bias": scatter_about(key_of[20], (D,), 0.3, 1.75, (), jnp.float32),
        "up_weight": scatter_about(key_of[21], (D, FF), D ** -0.5, 0.21875, ((1, 4),)),
        "up_bias": scatter_about(key_of[22], (FF,), 0.3, 1.75, ((0, 4),), jnp.float32),
        "down_weight": scatter_about(key_of[23], (FF, D), FF ** -0.5, 0.109375, ((0, 4),)),
        "down_bias": scatter_about(key_of[24], (D,), 0.3, 1.75, (), jnp.float32),
        "cotangent": scatter_about(key_of[25], (TOKENS, D), 1.0, 6.0, ((0, 32),)),
    }


@jax.custom_vjp
def low(v):
    return lax.optimization_barrier(v.astype(jnp.bfloat16)).astype(jnp.float32)

@jax.custom_vjp
def low_back(v):
    return v

def low_keep(v):
    return (low(v), None)

def low_pass(kept, grad):
    return (grad,)

def back_keep(v):
    return (v, None)

def back_low(kept, grad):
    return (low(grad),)
low.defvjp(low_keep, low_pass)
low_back.defvjp(back_keep, back_low)
highest = lax.Precision.HIGHEST
norm_epsilon = 1e-05
slow_rate = math.log(100.0) / 1.5
fast_rate = math.log(100.0) / 0.3

def matmul_high(left, right):
    return jnp.dot(left, right, precision=highest, preferred_element_type=jnp.float32)

def layer_norm(values, gain, shift):
    centred = values - lax.optimization_barrier(jnp.mean(values, axis=-1, keepdims=True))
    variance = lax.optimization_barrier(jnp.mean(centred * centred, axis=-1, keepdims=True))
    return centred * lax.rsqrt(variance + norm_epsilon) * gain + shift

def positions(length, bands):
    steps = jnp.arange(length).astype(jnp.float32)
    levels = (jnp.arange(bands) + 1).astype(jnp.float32)
    angle = 2.0 * math.pi / length * steps[:, None] * levels[None, :]
    return jnp.concatenate([steps[:, None] / (length - 1), jnp.cos(angle), -jnp.sin(angle)], axis=1)

def window(length, channels, offset, total):
    steps = jnp.arange(length).astype(jnp.float32)[:, None] / (length - 1)
    channel = (jnp.arange(channels) + offset).astype(jnp.float32)
    rates = slow_rate + (fast_rate - slow_rate) * channel / (total - 1)
    return jnp.exp(-steps * rates[None, :])

def filter_taps(filter_w1, filter_b1, filter_freq1, filter_w2, filter_b2, filter_freq2, filter_w3, length, offset, total):
    bands = (filter_w1.shape[0] - 1) // 2
    hidden_one = jnp.sin(filter_freq1 * (matmul_high(positions(length, bands), filter_w1) + filter_b1))
    hidden_two = jnp.sin(filter_freq2 * (matmul_high(hidden_one, filter_w2) + filter_b2))
    return matmul_high(hidden_two, filter_w3) * window(length, filter_w3.shape[1], offset, total)

def short_conv(projected, conv_weight, conv_bias):
    taps_count = conv_weight.shape[0]
    length = projected.shape[1]
    padded = jnp.pad(projected, ((0, 0), (taps_count - 1, 0), (0, 0), (0, 0)))
    result = conv_bias + jnp.zeros_like(projected)
    for tap_index in range(taps_count):
        first_row = taps_count - 1 - tap_index
        result = result + conv_weight[tap_index] * padded[:, first_row:first_row + length]
    return result

def long_conv(signal, taps):
    padded_size = 2 * signal.shape[1]
    spectrum = jnp.fft.rfft(signal, n=padded_size, axis=1) * jnp.fft.rfft(taps, n=padded_size, axis=0)[None]
    return jnp.fft.irfft(spectrum, n=padded_size, axis=1)[:, :signal.shape[1]]

def block(inputs, mask, norm1_gain, norm1_bias, in_weight, in_bias, conv_weight, conv_bias, filter_w1, filter_b1, filter_freq1, filter_w2, filter_b2, filter_freq2, filter_w3, filter_bias, out_weight, out_bias, norm2_gain, norm2_bias, up_weight, up_bias, down_weight, down_bias):
    token_count = inputs.shape[0]
    normed_in = low(layer_norm(inputs, norm1_gain, norm1_bias))
    flat_weight = jnp.transpose(in_weight, (2, 0, 1)).reshape(D, 3 * D)
    projected = low_back(matmul_high(normed_in, flat_weight).reshape(token_count, 3, D) + in_bias)
    streams = short_conv(projected.reshape(SLOTS, SEQ_LEN, 3, D), conv_weight, conv_bias)
    gate_out = streams[:, :, 0]
    gate_in = streams[:, :, 1]
    values = streams[:, :, 2]
    mixed_in = values * gate_in
    taps = filter_taps(filter_w1, filter_b1, filter_freq1, filter_w2, filter_b2, filter_freq2, filter_w3, SEQ_LEN, 0, D)
    conv_out = long_conv(mixed_in, taps) + mixed_in * filter_bias
    mixed = low((conv_out * gate_out).reshape(token_count, D))
    branch = low_back(matmul_high(mixed, out_weight) + out_bias)
    residual = inputs + branch
    normed_mid = low(layer_norm(residual, norm2_gain, norm2_bias))
    pre_act = low_back(matmul_high(normed_mid, up_weight) + up_bias)
    hidden = low(jax.nn.gelu(pre_act, approximate=False))
    return mask[:, None] * (residual + matmul_high(hidden, down_weight) + down_bias)

def reference(tokens, seq_counts, seq_lengths, norm1_gain, norm1_bias, in_weight, in_bias, conv_weight, conv_bias, filter_w1, filter_b1, filter_freq1, filter_w2, filter_b2, filter_freq2, filter_w3, filter_bias, out_weight, out_bias, norm2_gain, norm2_bias, up_weight, up_bias, down_weight, down_bias, cotangent):
    params = tuple((item.astype(jnp.float32) for item in (norm1_gain, norm1_bias, in_weight, in_bias, conv_weight, conv_bias, filter_w1, filter_b1, filter_freq1, filter_w2, filter_b2, filter_freq2, filter_w3, filter_bias, out_weight, out_bias, norm2_gain, norm2_bias, up_weight, up_bias, down_weight, down_bias)))
    inputs_all = tokens.astype(jnp.float32).reshape(GROUPS, SLOTS * SEQ_LEN, D)
    cots_all = cotangent.astype(jnp.float32).reshape(GROUPS, SLOTS * SEQ_LEN, D)
    position = jnp.arange(SEQ_LEN)
    live = jnp.arange(SLOTS)[None, :] < seq_counts[:, None]
    masks = (live[:, :, None] & (position[None, None, :] < seq_lengths[:, :, None])).astype(jnp.float32).reshape(GROUPS, SLOTS * SEQ_LEN)

    def one_group(totals, inputs):
        group_in, group_mask, group_cot = inputs

        def forward(values, *weights):
            return block(values, group_mask, *weights)
        result, pull = jax.vjp(forward, group_in, *params)
        grads = pull(group_cot)
        totals = tuple((total + grad for total, grad in zip(totals, grads[1:])))
        return (totals, (result.astype(jnp.bfloat16), grads[0]))
    starts = tuple((jnp.zeros_like(item) for item in params))
    totals, (results, input_grads) = lax.scan(one_group, starts, (inputs_all, masks, cots_all))
    return (results.reshape(TOKENS, D), input_grads.reshape(TOKENS, D), totals[0], totals[1], totals[2], totals[3], totals[4], totals[5], totals[6], totals[7], totals[8], totals[9], totals[10], totals[11], totals[12], totals[13], totals[14], totals[15], totals[16], totals[17], totals[18], totals[19], totals[20], totals[21])
```

```python
import math

import jax
import jax.numpy as jnp
from jax import lax
from jax.sharding import PartitionSpec as P

highest = lax.Precision.HIGHEST
norm_epsilon = 1e-05
slow_rate = math.log(100.0) / 1.5
fast_rate = math.log(100.0) / 0.3


def matmul_high(left, right):
    return jnp.dot(left, right, precision=highest, preferred_element_type=jnp.float32)


def norm_stats(values):
    centred = values - jnp.mean(values, axis=-1, keepdims=True)
    inv_scale = lax.rsqrt(jnp.mean(centred * centred, axis=-1, keepdims=True) + norm_epsilon)
    return (centred * inv_scale, inv_scale)


def norm_back(grad_out, normed, inv_scale, gain):
    scaled = grad_out * gain
    return inv_scale * (
        scaled
        - jnp.mean(scaled, axis=-1, keepdims=True)
        - normed * jnp.mean(scaled * normed, axis=-1, keepdims=True)
    )


def gelu_both(values):
    cdf = 0.5 * (1.0 + lax.erf(values * (1.0 / math.sqrt(2.0))))
    density = jnp.exp(-0.5 * values * values) * (1.0 / math.sqrt(2.0 * math.pi))
    return (values * cdf, cdf + values * density)


def positions(length, bands):
    steps = jnp.arange(length).astype(jnp.float32)
    levels = (jnp.arange(bands) + 1).astype(jnp.float32)
    angle = 2.0 * math.pi / length * steps[:, None] * levels[None, :]
    return jnp.concatenate([steps[:, None] / (length - 1), jnp.cos(angle), -jnp.sin(angle)], axis=1)


def decay(length, channel, total):
    steps = jnp.arange(length).astype(jnp.float32)[None, :] / (length - 1)
    rates = slow_rate + (fast_rate - slow_rate) * channel / (total - 1)
    return jnp.exp(-steps * rates[:, None])


def fourier_table(length):
    period = 2 * length
    low = 1 << (length.bit_length() // 2)
    high = length // low
    step = jnp.arange(length)[None, :]

    def turn(level):
        angle = (level[:, None] * step % period).astype(jnp.float32) * (2.0 * math.pi / period)
        return (jnp.cos(angle), jnp.sin(angle))

    cos_high, sin_high, cos_low, sin_low = lax.optimization_barrier(
        turn(jnp.arange(high) * low) + turn(jnp.arange(low))
    )
    cos_high, sin_high = cos_high[:, None], sin_high[:, None]
    cos_low, sin_low = cos_low[None], sin_low[None]
    cosines = (cos_high * cos_low - sin_high * sin_low).reshape(length, length)
    sines = (sin_high * cos_low + cos_high * sin_low).reshape(length, length)
    alternating = (1 - 2 * (step % 2)).astype(jnp.float32)
    first = lax.broadcasted_iota(jnp.int32, (length, length), 0) == 0
    sines = jnp.where(first, alternating, sines)
    return (cosines.astype(jnp.bfloat16), sines.astype(jnp.bfloat16))


def spectrum(signal, table):
    low = signal.astype(jnp.bfloat16)
    return tuple(
        jnp.einsum("ct,kt->ck", low, part, preferred_element_type=jnp.float32) for part in table
    )


def from_spectrum(parts, table):
    return sum(
        jnp.einsum("ck,kt->ct", part.astype(jnp.bfloat16), basis, preferred_element_type=jnp.float32)
        for part, basis in zip(parts, table)
    )


def split_factor(parts, scale):
    cos_part, sin_part = parts
    first = lax.broadcasted_iota(jnp.int32, cos_part.shape, 1) == 0
    weight = jnp.where(first, 0.5 * scale, scale)
    return (
        cos_part * weight,
        jnp.where(first, 0.0, sin_part) * weight,
        jnp.where(first, sin_part, cos_part) * weight,
    )


def times(parts, factor):
    return (
        parts[0] * factor[0] - parts[1] * factor[1],
        parts[0] * factor[1] + parts[1] * factor[2],
    )


def times_conj(parts, factor):
    return (
        parts[0] * factor[0] + parts[1] * factor[1],
        parts[1] * factor[2] - parts[0] * factor[1],
    )


def later(values, shift):
    if shift == 0:
        return values
    pads = [(0, 0)] * (values.ndim - 1) + [(shift, 0)]
    return jnp.pad(values, pads)[..., : values.shape[-1]]


def earlier(values, shift):
    if shift == 0:
        return values
    pads = [(0, 0)] * (values.ndim - 1) + [(0, shift)]
    return jnp.pad(values, pads)[..., shift:]


def local(
    tokens,
    seq_counts,
    seq_lengths,
    norm1_gain,
    norm1_bias,
    in_weight,
    in_bias,
    conv_weight,
    conv_bias,
    filter_w1,
    filter_b1,
    filter_freq1,
    filter_w2,
    filter_b2,
    filter_freq2,
    filter_w3,
    filter_bias,
    out_weight,
    out_bias,
    norm2_gain,
    norm2_bias,
    up_weight,
    up_bias,
    down_weight,
    down_bias,
    cotangent,
):
    low = jnp.bfloat16
    full = jnp.float32
    tensor_count = lax.axis_size("tensor")
    dp_count = lax.axis_size("dp")
    row_share, model_width = tokens.shape
    local_width = in_weight.shape[1]
    slot_count = seq_lengths.shape[1]
    seq_length = row_share * tensor_count // slot_count
    part = lax.axis_index("tensor")
    side = part % 2
    group = lax.axis_index("dp")
    across = [(i, i ^ 1) for i in range(tensor_count)]
    over = [(i, i ^ 2) for i in range(tensor_count)]

    def swap(values):
        return lax.ppermute(values, "tensor", across)

    def cross(values):
        return lax.ppermute(values, "tensor", over)

    def pair(own, other):
        return jnp.concatenate(
            [jnp.where(side == 0, own, other), jnp.where(side == 0, other, own)], axis=0
        )

    def halves(rows):
        own = lax.dynamic_slice_in_dim(rows, side * row_share, row_share, 0)
        other = lax.dynamic_slice_in_dim(rows, (1 - side) * row_share, row_share, 0)
        return (own, other)

    def pair_sum(rows):
        own, other = halves(rows)
        return own + swap(other.astype(low)).astype(full)

    def dp_scatter(grad):
        blocks, width = dp_count, grad.shape[1]
        kept = grad.reshape(blocks, model_width // blocks, width)
        for bit_index in range(dp_count.bit_length() - 1):
            bit = (group >> bit_index) & 1
            blocks //= 2
            kept = kept.reshape(blocks, 2, model_width // dp_count, width)
            mine = lax.dynamic_index_in_dim(kept, bit, 1, keepdims=False)
            sent = lax.dynamic_index_in_dim(kept, 1 - bit, 1, keepdims=False)
            flips = [(i, i ^ (1 << bit_index)) for i in range(dp_count)]
            kept = mine + lax.ppermute(sent.astype(low), "dp", flips).astype(full)
        return kept.reshape(model_width // dp_count, width)

    def dp_sum(values):
        for bit_index in range(dp_count.bit_length() - 1):
            flips = [(i, i ^ (1 << bit_index)) for i in range(dp_count)]
            values = values + lax.ppermute(values, "dp", flips)
        return values

    first_row = part * row_share
    slot = first_row // seq_length
    position = first_row % seq_length + lax.broadcasted_iota(jnp.int32, (row_share, 1), 0)
    live = (slot < seq_counts[0]) & (position < lax.dynamic_index_in_dim(seq_lengths[0], slot, 0))
    mask_rows = live.astype(full)
    inputs = tokens.astype(full)
    normed_one, inv_one = norm_stats(inputs)
    normed_in_own = (normed_one * norm1_gain + norm1_bias).astype(low)
    normed_in = pair(normed_in_own, swap(normed_in_own))
    cot_rows = cotangent.astype(full) * mask_rows
    cot_own = cot_rows.astype(low)

    flat_in = in_weight.reshape(3 * local_width, model_width)
    peer_weights = cross(jnp.concatenate([flat_in, out_weight], axis=0))
    peer_in = peer_weights[: 3 * local_width].reshape(3, local_width, model_width)
    peer_out = peer_weights[3 * local_width :]
    chan = jnp.concatenate(
        [conv_weight.reshape(9, local_width), in_bias, conv_bias, filter_bias[None], filter_w3], axis=0
    )
    chan = jnp.concatenate([chan, cross(chan)], axis=1)
    conv_w = chan[:9].reshape(3, 3, -1)
    in_b, conv_b, filter_b, w_three = chan[9:12], chan[12:15], chan[15], chan[16:]
    in_w = jnp.concatenate([in_weight, peer_in], axis=1)
    out_w = jnp.concatenate([out_weight, peer_out], axis=0)

    table = fourier_table(seq_length)
    offsets = jnp.arange(local_width)
    channel = jnp.concatenate(
        [part * local_width + offsets, (part ^ 2) * local_width + offsets]
    ).astype(full)

    def make_taps(w_one, b_one, q_one, w_two, b_two, q_two, w_last):
        bands = (w_one.shape[0] - 1) // 2
        features = lax.optimization_barrier(positions(seq_length, bands))
        hidden_one = jnp.sin(q_one * (matmul_high(features, w_one) + b_one))
        hidden_two = jnp.sin(q_two * (matmul_high(hidden_one, w_two) + b_two))
        raw = jnp.einsum(
            "hc,th->ct", w_last, hidden_two, precision=highest, preferred_element_type=full
        )
        return raw * decay(seq_length, channel, model_width)

    taps, taps_pull = jax.vjp(
        make_taps, filter_w1, filter_b1, filter_freq1, filter_w2, filter_b2, filter_freq2, w_three
    )
    scale = 1.0 / seq_length
    taps_factor = split_factor(spectrum(taps, table), scale)

    projected = (
        jnp.einsum("icd,td->ict", in_w, normed_in, preferred_element_type=full) + in_b[:, :, None]
    )
    streams = conv_b[:, :, None] + sum(conv_w[j][:, :, None] * later(projected, j) for j in range(3))
    gate_out, gate_in, values = streams[0], streams[1], streams[2]
    mixed_in = values * gate_in
    signal = spectrum(mixed_in, table)
    conv_out = from_spectrum(times(signal, taps_factor), table) + mixed_in * filter_b[:, None]
    mixed = (conv_out * gate_out).astype(low)
    branch = pair_sum(jnp.einsum("ct,cd->td", mixed, out_w, preferred_element_type=full))
    residual = inputs + branch + out_bias
    normed_two, inv_two = norm_stats(residual)
    mid_own = (normed_two * norm2_gain + norm2_bias).astype(low)

    far_mid_own = cross(mid_own)
    far_cot_own = cross(cot_own)
    mid_near = pair(mid_own, swap(mid_own))
    cot_near = pair(cot_own, swap(cot_own))
    mid_far = pair(far_mid_own, swap(far_mid_own))
    cot_far = pair(far_cot_own, swap(far_cot_own))

    def mlp(mid, cot):
        pre_act = jnp.dot(mid, up_weight, preferred_element_type=full) + up_bias
        act, slope = gelu_both(pre_act)
        hidden = act.astype(low)
        hidden_grad = jnp.einsum("td,fd->tf", cot, down_weight, preferred_element_type=full)
        pre_grad = (hidden_grad * slope).astype(low)
        mid_part = jnp.einsum("tf,df->td", pre_grad, up_weight, preferred_element_type=full)
        down_part = jnp.dot(hidden, down_weight, preferred_element_type=full)
        return (hidden, pre_grad, mid_part, down_part)

    hidden_far, pre_grad_far, mid_part_far, down_part_far = mlp(mid_far, cot_far)
    hidden_near, pre_grad_near, mid_part_near, down_part_near = mlp(mid_near, cot_near)
    mid_back = cross(pair_sum(mid_part_far).astype(low)).astype(full)
    down_back = cross(pair_sum(down_part_far).astype(low)).astype(full)
    mid_rows = pair_sum(mid_part_near) + mid_back
    block_sum = pair_sum(down_part_near) + down_back
    activations = (mask_rows * (residual + block_sum + down_bias)).astype(low)

    def both(form, left, right):
        return jnp.einsum(form, left[0], right[0], preferred_element_type=full) + jnp.einsum(
            form, left[1], right[1], preferred_element_type=full
        )

    down_grad = both("td,tf->df", (cot_near, cot_far), (hidden_near, hidden_far))
    up_grad = both("td,tf->df", (mid_near, mid_far), (pre_grad_near, pre_grad_far))
    up_bias_grad = jnp.sum(pre_grad_near.astype(full), axis=0) + jnp.sum(
        pre_grad_far.astype(full), axis=0
    )
    mlp_grads = dp_scatter(jnp.concatenate([up_grad, down_grad], axis=1))

    residual_grad = cot_rows + norm_back(mid_rows, normed_two, inv_two, norm2_gain)
    gain_two_grad = jnp.sum(mid_rows * normed_two, axis=0)
    shift_two_grad = jnp.sum(mid_rows, axis=0)
    residual_low_own = residual_grad.astype(low)
    out_bias_grad = jnp.sum(residual_low_own.astype(full), axis=0)
    down_bias_grad = jnp.sum(cot_rows, axis=0)
    residual_low = pair(residual_low_own, swap(residual_low_own))

    out_grad = jnp.einsum("td,ct->dc", residual_low, mixed, preferred_element_type=full)
    mixed_grad = jnp.einsum("cd,td->ct", out_w, residual_low, preferred_element_type=full)
    conv_grad = mixed_grad * gate_out
    gate_out_grad = mixed_grad * conv_out
    filter_bias_grad = jnp.sum(conv_grad * mixed_in, axis=1)
    grad_parts = spectrum(conv_grad, table)
    taps_grad = from_spectrum(times_conj(grad_parts, split_factor(signal, scale)), table)
    mixed_in_grad = (
        from_spectrum(times_conj(grad_parts, taps_factor), table) + conv_grad * filter_b[:, None]
    )
    stream_grad = jnp.stack([gate_out_grad, mixed_in_grad * values, mixed_in_grad * gate_in], axis=0)
    conv_bias_grad = jnp.sum(stream_grad, axis=2)
    conv_weight_grad = jnp.stack(
        [jnp.sum(stream_grad * later(projected, j), axis=2) for j in range(3)], axis=0
    )
    proj_low = sum(conv_w[j][:, :, None] * earlier(stream_grad, j) for j in range(3)).astype(low)
    in_bias_grad = jnp.sum(proj_low.astype(full), axis=2)
    in_grad = jnp.einsum("td,ict->dic", normed_in, proj_low, preferred_element_type=full)
    first_rows = pair_sum(jnp.einsum("ict,icd->td", proj_low, in_w, preferred_element_type=full))
    input_grad = residual_grad + norm_back(first_rows, normed_one, inv_one, norm1_gain)
    gain_one_grad = jnp.sum(first_rows * normed_one, axis=0)
    shift_one_grad = jnp.sum(first_rows, axis=0)
    filter_grads = taps_pull(taps_grad)

    own_in, peer_in_grad = in_grad[:, :, :local_width], in_grad[:, :, local_width:]
    own = jnp.concatenate(
        [own_in.reshape(model_width, 3 * local_width), out_grad[:, :local_width]], axis=1
    )
    peer = jnp.concatenate(
        [peer_in_grad.reshape(model_width, 3 * local_width), out_grad[:, local_width:]], axis=1
    )
    operator_grads = dp_scatter(own + cross(peer.astype(low)).astype(full))

    chan_grads = jnp.concatenate(
        [
            in_bias_grad,
            conv_weight_grad.reshape(9, -1),
            conv_bias_grad,
            filter_bias_grad[None],
            filter_grads[6],
        ],
        axis=0,
    )
    chan_grads = chan_grads[:, :local_width] + cross(chan_grads[:, local_width:])
    chan_grads = jnp.concatenate([chan_grads, up_bias_grad.reshape(-1, local_width)], axis=0)
    chan_grads = dp_sum(chan_grads)

    wide = jnp.stack(
        [gain_one_grad, shift_one_grad, out_bias_grad, gain_two_grad, shift_two_grad, down_bias_grad]
    )
    narrow = jnp.concatenate(
        [
            filter_grads[0],
            filter_grads[3],
            jnp.stack([filter_grads[1], filter_grads[2], filter_grads[4], filter_grads[5]]),
        ],
        axis=0,
    )
    wide = wide + swap(wide)
    wide = dp_sum(wide + cross(wide))
    narrow = narrow + swap(narrow)
    narrow = dp_sum(narrow + cross(narrow))
    inputs_count = filter_w1.shape[0]
    units = filter_w2.shape[0]
    tail = inputs_count + units
    share = units // dp_count
    block = model_width // dp_count
    grad_in = operator_grads[:, : 3 * local_width].reshape(block, 3, local_width)
    return (
        activations,
        input_grad,
        wide[0],
        wide[1],
        jnp.transpose(grad_in, (1, 2, 0)),
        chan_grads[0:3],
        chan_grads[3:12].reshape(3, 3, local_width),
        chan_grads[12:15],
        narrow[:inputs_count],
        narrow[tail],
        narrow[tail + 1],
        narrow[inputs_count:tail],
        narrow[tail + 2],
        narrow[tail + 3],
        lax.dynamic_slice_in_dim(chan_grads[16 : 16 + units], group * share, share, 0),
        chan_grads[15],
        jnp.transpose(operator_grads[:, 3 * local_width :]),
        wide[2],
        wide[3],
        wide[4],
        mlp_grads[:, : up_weight.shape[1]],
        chan_grads[16 + units :].reshape(-1),
        jnp.transpose(mlp_grads[:, up_weight.shape[1] :]),
        wide[5],
    )

def solution(mesh):
    in_specs = (
        P(("dp", "tensor"), None),
        P("dp"),
        P("dp", None),
        P(),
        P(),
        P(None, "tensor", None),
        P(None, "tensor"),
        P(None, None, "tensor"),
        P(None, "tensor"),
        P(),
        P(),
        P(),
        P(),
        P(),
        P(),
        P(None, "tensor"),
        P("tensor"),
        P("tensor", None),
        P(),
        P(),
        P(),
        P(None, "tensor"),
        P("tensor"),
        P("tensor", None),
        P(),
        P(("dp", "tensor"), None),
    )
    out_specs = (
        P(("dp", "tensor"), None),
        P(("dp", "tensor"), None),
        P(),
        P(),
        P(None, "tensor", "dp"),
        P(None, "tensor"),
        P(None, None, "tensor"),
        P(None, "tensor"),
        P(),
        P(),
        P(),
        P(),
        P(),
        P(),
        P("dp", "tensor"),
        P("tensor"),
        P("tensor", "dp"),
        P(),
        P(),
        P(),
        P("dp", "tensor"),
        P("tensor"),
        P("tensor", "dp"),
        P(),
    )
    return jax.shard_map(local, mesh=mesh, in_specs=in_specs, out_specs=out_specs, check_vma=False)
```

```python
import functools
import math

import jax
import jax.numpy as jnp
from jax import lax
from jax.experimental import pallas as pl
from jax.experimental.pallas import tpu as pltpu
from jax.sharding import PartitionSpec as P

highest = lax.Precision.HIGHEST
norm_epsilon = 1e-05
slow_rate = math.log(100.0) / 1.5
fast_rate = math.log(100.0) / 0.3


def matmul_high(left, right):
    return jnp.dot(left, right, precision=highest, preferred_element_type=jnp.float32)


def norm_stats(values):
    centred = values - jnp.mean(values, axis=-1, keepdims=True)
    inv_scale = lax.rsqrt(jnp.mean(centred * centred, axis=-1, keepdims=True) + norm_epsilon)
    return (centred * inv_scale, inv_scale)


def norm_back(grad_out, normed, inv_scale, gain):
    scaled = grad_out * gain
    return inv_scale * (
        scaled
        - jnp.mean(scaled, axis=-1, keepdims=True)
        - normed * jnp.mean(scaled * normed, axis=-1, keepdims=True)
    )


def gelu_both(values):
    cdf = 0.5 * (1.0 + lax.erf(values * (1.0 / math.sqrt(2.0))))
    density = jnp.exp(-0.5 * values * values) * (1.0 / math.sqrt(2.0 * math.pi))
    return (values * cdf, cdf + values * density)


def positions(length, bands):
    steps = jnp.arange(length).astype(jnp.float32)
    levels = (jnp.arange(bands) + 1).astype(jnp.float32)
    angle = 2.0 * math.pi / length * steps[:, None] * levels[None, :]
    return jnp.concatenate([steps[:, None] / (length - 1), jnp.cos(angle), -jnp.sin(angle)], axis=1)


def decay(length, channel, total):
    steps = jnp.arange(length).astype(jnp.float32)[None, :] / (length - 1)
    rates = slow_rate + (fast_rate - slow_rate) * channel / (total - 1)
    return jnp.exp(-steps * rates[:, None])


def fourier_table(length):
    period = 2 * length
    low = 1 << (length.bit_length() // 2)
    high = length // low
    step = jnp.arange(length)[None, :]

    def turn(level):
        angle = (level[:, None] * step % period).astype(jnp.float32) * (2.0 * math.pi / period)
        return (jnp.cos(angle), jnp.sin(angle))

    cos_high, sin_high, cos_low, sin_low = lax.optimization_barrier(
        turn(jnp.arange(high) * low) + turn(jnp.arange(low))
    )
    cos_high, sin_high = cos_high[:, None], sin_high[:, None]
    cos_low, sin_low = cos_low[None], sin_low[None]
    cosines = (cos_high * cos_low - sin_high * sin_low).reshape(length, length)
    sines = (sin_high * cos_low + cos_high * sin_low).reshape(length, length)
    alternating = (1 - 2 * (step % 2)).astype(jnp.float32)
    first = lax.broadcasted_iota(jnp.int32, (length, length), 0) == 0
    sines = jnp.where(first, alternating, sines)
    return (cosines.astype(jnp.bfloat16), sines.astype(jnp.bfloat16))


def spectrum(signal, table):
    low = signal.astype(jnp.bfloat16)
    return tuple(
        jnp.einsum("ct,kt->ck", low, part, preferred_element_type=jnp.float32) for part in table
    )


def from_spectrum(parts, table):
    return sum(
        jnp.einsum("ck,kt->ct", part.astype(jnp.bfloat16), basis, preferred_element_type=jnp.float32)
        for part, basis in zip(parts, table)
    )


def split_factor(parts, scale):
    cos_part, sin_part = parts
    first = lax.broadcasted_iota(jnp.int32, cos_part.shape, 1) == 0
    weight = jnp.where(first, 0.5 * scale, scale)
    return (
        cos_part * weight,
        jnp.where(first, 0.0, sin_part) * weight,
        jnp.where(first, sin_part, cos_part) * weight,
    )


def times(parts, factor):
    return (
        parts[0] * factor[0] - parts[1] * factor[1],
        parts[0] * factor[1] + parts[1] * factor[2],
    )


def times_conj(parts, factor):
    return (
        parts[0] * factor[0] + parts[1] * factor[1],
        parts[1] * factor[2] - parts[0] * factor[1],
    )


def later(values, shift):
    if shift == 0:
        return values
    pads = [(0, 0)] * (values.ndim - 1) + [(shift, 0)]
    return jnp.pad(values, pads)[..., : values.shape[-1]]


def earlier(values, shift):
    if shift == 0:
        return values
    pads = [(0, 0)] * (values.ndim - 1) + [(0, shift)]
    return jnp.pad(values, pads)[..., shift:]


def dot_nt(left, right):
    return lax.dot_general(
        left, right, (((1,), (1,)), ((), ())), preferred_element_type=jnp.float32
    )


def dot_nn(left, right):
    return jnp.dot(left, right, preferred_element_type=jnp.float32)


def dot_tn(left, right):
    return lax.dot_general(
        left, right, (((0,), (0,)), ((), ())), preferred_element_type=jnp.float32
    )


def shifted(values, shift, lanes):
    length = values.shape[1]
    if shift == 0:
        return values
    if shift > 0:
        return jnp.where(lanes >= shift, pltpu.roll(values, shift, 1), 0.0)
    return jnp.where(lanes < length + shift, pltpu.roll(values, length + shift, 1), 0.0)


def column(params, index):
    return params[:, index : index + 1]


def pack_columns(columns, rows):
    lanes = lax.broadcasted_iota(jnp.int32, (rows, 128), 1)
    packed = jnp.zeros((rows, 128), jnp.float32)
    for index, values in columns:
        packed = jnp.where(lanes == index, values, packed)
    return packed


CHUNK = 16


BLOCKS = 8
PLAN = ("resid", "up1", "down1", "up2", "down2", "up3", "down3", "grads", "chan", "first") + tuple(
    f"{name}{hop}" for name in ("a", "b", "c") for hop in (1, 2, 3)
) + tuple(f"s{hop}" for hop in range(5))
LOADS = ("resid", "w_peer", "w_own", "proj", "conv", "par", "table", "factor", "signal", "normed",
         "filt", "w_last", "up", "down", "w_mid", "feat", "freq", "tokens", "gain", "residual", "extra", "upb")


def other_of(index, step):
    return index + step * (1 - 2 * ((index // step) % 2))


def operator_back(dp_step, *refs):
    sizes = len(LOADS)
    source = dict(zip(LOADS, refs[:sizes]))
    input_grad, op_out, up_out, down_out, shared_out, chan_out = refs[sizes : sizes + 6]
    refs = refs[sizes + 6 :]
    held = dict(zip(LOADS, refs[: len(LOADS)]))
    refs = refs[len(LOADS) :]
    (grad, real, imag, pair_a, pair_b, pair_c, pair_d, stack, proj_low, h_grad, first, first_send, first_recv,
     g_peer, g_recv, g_sum, sums, chan_peer, chan_recv, chan, chan_hops, shared, shared_hops) = refs[:23]
    hops = dict(zip(("up", "down", "a", "b"), (refs[23 + 5 * i : 28 + 5 * i] for i in range(4))))
    load_sem, send_sem, recv_sem = refs[43:]
    full, low = jnp.float32, jnp.bfloat16

    part = lax.axis_index("tensor")
    group = lax.axis_index("dp")
    side = part % 2
    bits = [(group // (dp_step << b)) % 2 for b in range(3)]
    across = {"tensor": other_of(part, 1)}
    over = {"tensor": other_of(part, 2)}
    flips = [{"dp": other_of(group, dp_step << b)} for b in range(3)]

    def remote(name, src, dst, target):
        index = PLAN.index(name)
        return pltpu.make_async_remote_copy(
            src_ref=src,
            dst_ref=dst,
            send_sem=send_sem.at[index],
            recv_sem=recv_sem.at[index],
            device_id=target,
            device_id_type=pl.DeviceIdType.MESH,
        )

    width, length = grad.shape
    model_width = first.shape[1]
    half_rows = length // 2
    block_rows = model_width // BLOCKS
    mine = pl.ds(pl.multiple_of(side * half_rows, half_rows), half_rows)
    theirs = pl.ds(pl.multiple_of((1 - side) * half_rows, half_rows), half_rows)

    loads = {
        name: pltpu.make_async_copy(
            source[name],
            held[name].at[mine] if name == "resid" else held[name],
            load_sem.at[index],
        )
        for index, name in enumerate(LOADS)
    }
    for name in LOADS:
        loads[name].start()

    barrier = pltpu.get_barrier_semaphore()
    for target in [across, over] + flips:
        pl.semaphore_signal(barrier, inc=1, device_id=target, device_id_type=pl.DeviceIdType.MESH)
    pl.semaphore_wait(barrier, 5)

    resid = held["resid"]
    resid_copy = remote("resid", source["resid"], resid.at[mine], across)
    resid_copy.start()
    loads["resid"].wait()
    loads["w_peer"].wait()
    loads["w_own"].wait()
    resid_copy.wait()

    def hop_one(name, grads, bit):
        if bit == 0:
            src = grads.at[:, :, 1 - bits[0]]
        else:
            src = grads.at[:, 1 - bits[1]]
        copy = remote(name + "1", src, hops[name][0], flips[bit])
        copy.start()
        return copy

    def hop_two(name, grads, bit, copy):
        recv_one, send_two, keep_two, recv_two, _ = hops[name]
        copy.wait()
        for top in range(2):
            if bit == 0:
                sent = grads[top, 1 - bits[1], bits[0]].astype(full) + recv_one[top, 1 - bits[1]].astype(full)
                kept = grads[top, bits[1], bits[0]].astype(full) + recv_one[top, bits[1]].astype(full)
            else:
                sent = grads[top, bits[1], 1 - bits[0]].astype(full) + recv_one[top, 1 - bits[0]].astype(full)
                kept = grads[top, bits[1], bits[0]].astype(full) + recv_one[top, bits[0]].astype(full)
            send_two[top] = sent.astype(low)
            keep_two[top] = kept
        copy = remote(name + "2", send_two, recv_two, flips[1 - bit])
        copy.start()
        return copy

    def hop_three(name, copy):
        recv_one, send_two, keep_two, recv_two, recv_three = hops[name]
        copy.wait()
        send_two[0] = (keep_two[1 - bits[2]] + recv_two[1 - bits[2]].astype(full)).astype(low)
        copy = remote(name + "3", send_two.at[0], recv_three, flips[2])
        copy.start()
        return copy

    def hop_last(name, copy):
        recv_one, send_two, keep_two, recv_two, recv_three = hops[name]
        copy.wait()
        return keep_two[bits[2]] + recv_two[bits[2]].astype(full) + recv_three[...].astype(full)

    loads["up"].wait()
    loads["down"].wait()
    up_copy = hop_one("up", held["up"], 0)
    down_copy = hop_one("down", held["down"], 1)

    lanes = lax.broadcasted_iota(jnp.int32, (CHUNK, length), 1)
    par, proj, conv = held["par"], held["proj"], held["conv"]
    cos, sin = held["table"].at[0], held["table"].at[1]
    factor, signal, normed = held["factor"], held["signal"], held["normed"]
    filt = held["filt"]
    weights = (held["w_own"], held["w_peer"])

    def half_pass(half, loaded, middle):
        base = half * width
        weight = weights[half]
        own_w = 3 * width

        def at(index):
            return pl.ds(pl.multiple_of(index * CHUNK, CHUNK), CHUNK)

        def far(index):
            return pl.ds(pl.multiple_of(base + index * CHUNK, CHUNK), CHUNK)

        def stream(i, rows, params):
            line = proj[i, rows, :]
            lines = [line, shifted(line, 1, lanes), shifted(line, 2, lanes)]
            total = column(params, 12 + i) + sum(column(params, 3 * j + i) * lines[j] for j in range(3))
            return (lines, total)

        def stream_back(i, index, params, back, lines):
            out = sum(column(params, 3 * j + i) * shifted(back, -j, lanes) for j in range(3)).astype(low)
            start = pl.multiple_of(i * width + index * CHUNK, CHUNK)
            proj_low[pl.ds(start, CHUNK), :] = out
            found = [(3 * j + i, jnp.sum(back * lines[j], axis=1, keepdims=True)) for j in range(3)]
            found.append((9 + i, jnp.sum(out.astype(full), axis=1, keepdims=True)))
            found.append((12 + i, jnp.sum(back, axis=1, keepdims=True)))
            return found

        grad[...] = dot_nt(weight[own_w:, :], resid[...])
        if not loaded:
            for name in ("proj", "conv", "par"):
                loads[name].wait()

        def before(index, carry):
            rows = far(index)
            params = par[rows, :]
            lines, gate_out = stream(0, rows, params)
            gate_in = stream(1, rows, params)[1]
            values = stream(2, rows, params)[1]
            mixed_grad = grad[at(index), :]
            conv_part = conv[rows, :]
            conv_grad = mixed_grad * gate_out
            grad[at(index), :] = conv_grad
            pair_a[at(index), :] = conv_grad.astype(low)
            pair_b[at(index), :] = (conv_part * gate_out).astype(low)
            found = stream_back(0, index, params, mixed_grad * conv_part, lines)
            found.append((15, jnp.sum(conv_grad * values * gate_in, axis=1, keepdims=True)))
            sums[at(index), :] = pack_columns(found, CHUNK)
            return carry

        lax.fori_loop(0, width // CHUNK, before, 0)
        stack[3 * width :, :] = dot_nn(pair_b[...], resid[...])
        if not loaded:
            loads["table"].wait()
        real[...] = dot_nt(pair_a[...], cos[...])
        imag[...] = dot_nt(pair_a[...], sin[...])
        if not loaded:
            loads["factor"].wait()
            loads["signal"].wait()
        first_lane = lanes == 0
        scale = jnp.where(first_lane, 0.5 / length, 1.0 / length)

        def between(index, carry):
            rows, place = far(index), at(index)
            cos_part, sin_part = real[place, :], imag[place, :]
            f_cos, f_sin, f_last = factor[0, rows, :], factor[1, rows, :], factor[2, rows, :]
            pair_a[place, :] = (cos_part * f_cos + sin_part * f_sin).astype(low)
            pair_b[place, :] = (sin_part * f_last - cos_part * f_sin).astype(low)
            s_cos, s_sin = signal[0, rows, :], signal[1, rows, :]
            cos_part, sin_part = cos_part * scale, sin_part * scale
            s_last = jnp.where(first_lane, s_sin, s_cos)
            s_sin = jnp.where(first_lane, 0.0, s_sin)
            pair_c[place, :] = (cos_part * s_cos + sin_part * s_sin).astype(low)
            pair_d[place, :] = (sin_part * s_last - cos_part * s_sin).astype(low)
            return carry

        lax.fori_loop(0, width // CHUNK, between, 0)
        middle()
        real[...] = dot_nn(pair_a[...], cos[...]) + dot_nn(pair_b[...], sin[...])
        imag[...] = dot_nn(pair_c[...], cos[...]) + dot_nn(pair_d[...], sin[...])

        def after(index, carry):
            rows = far(index)
            params = par[rows, :]
            lines_in, gate_in = stream(1, rows, params)
            lines_value, values = stream(2, rows, params)
            back = real[at(index), :] + grad[at(index), :] * column(params, 15)
            found = stream_back(1, index, params, back * values, lines_in)
            found += stream_back(2, index, params, back * gate_in, lines_value)
            sums[at(index), :] = sums[at(index), :] + pack_columns(found, CHUNK)
            window = jnp.exp(-lanes.astype(full) * column(params, 16))
            pair_a[at(index), :] = (imag[at(index), :] * window).astype(low)
            return carry

        lax.fori_loop(0, width // CHUNK, after, 0)
        if not loaded:
            for name in ("normed", "filt", "w_last"):
                loads[name].wait()
        stack[: 3 * width, :] = dot_nn(proj_low[...], normed[...])
        target = chan_peer if half == 1 else chan
        target[0:16, :] = jnp.transpose(sums[...])[0:16, :]
        target[16:80, :] = dot_nt(filt[1].astype(low), pair_a[...])
        h_part = dot_nn(held["w_last"][half].astype(low), pair_a[...])
        if half == 1:
            h_grad[...] = h_part
        else:
            h_grad[...] += h_part

    def turned(store):
        for piece in range(model_width // 128):
            block = jnp.transpose(stack[:, piece * 128 : (piece + 1) * 128])
            start = piece * 128
            while start < (piece + 1) * 128:
                index, offset = start // block_rows, start % block_rows
                size = min(block_rows - offset, (piece + 1) * 128 - start)
                begin = start - piece * 128
                place = (index // 4, (index // 2) % 2, index % 2, pl.ds(offset, size))
                store(place, block[begin : begin + size, :])
                start += size

    def store_peer(place, values):
        g_peer[place] = values.astype(low)

    def first_part(half):
        for start in range(0, length, 256):
            product = dot_tn(proj_low[:, start : start + 256], weights[half][: 3 * width, :])
            if half == 1:
                first[start : start + 256, :] = product
            else:
                first[start : start + 256, :] += product

    half_pass(1, False, lambda: None)
    turned(store_peer)
    chan_peer[80:88, :] = jnp.zeros((8, width), full)
    grads_copy = remote("grads", g_peer, g_recv, over)
    grads_copy.start()
    chan_copy = remote("chan", chan_peer, chan_recv, over)
    chan_copy.start()
    first_part(1)
    copies = {"up": hop_two("up", held["up"], 0, up_copy)}
    copies["down"] = hop_two("down", held["down"], 1, down_copy)

    def last_hops():
        copies["up"] = hop_three("up", copies["up"])
        copies["down"] = hop_three("down", copies["down"])

    half_pass(0, True, last_hops)
    first_part(0)
    first_send[...] = first[theirs, :].astype(low)
    first_copy = remote("first", first_send, first_recv, across)
    first_copy.start()
    grads_copy.wait()

    def store_sum(place, values):
        total = (values + g_recv[place].astype(full)).astype(low)
        middle = model_width // 2
        g_sum[(0,) + place] = total[:, :middle]
        g_sum[(1,) + place] = total[:, middle:]

    turned(store_sum)
    a_copy = hop_one("a", g_sum.at[0], 0)
    b_copy = hop_one("b", g_sum.at[1], 1)

    chan_copy.wait()
    loads["upb"].wait()
    chan[0:80, :] = chan[0:80, :] + chan_recv[0:80, :]
    chan[80:88, :] = held["upb"][...]
    chan_copy = remote("c1", chan, chan_hops.at[0], flips[0])
    chan_copy.start()

    for name in ("w_mid", "feat", "freq"):
        loads[name].wait()
    freq, w_mid = held["freq"], held["w_mid"]
    shared[...] = jnp.zeros_like(shared)
    units = w_mid.shape[0]
    feats = held["feat"].shape[0]
    slope = h_grad[...] * filt[3]
    q_two = jnp.sum(slope * filt[5], axis=1, keepdims=True)
    slope = slope * column(freq[...], 1)
    b_two = jnp.sum(slope, axis=1, keepdims=True)
    slope_low = slope.astype(low)
    shared[80 : 80 + units, 0:units] = dot_nt(filt[0].astype(low), slope_low)
    slope = dot_nn(w_mid[...].astype(low), slope_low) * filt[2]
    q_one = jnp.sum(slope * filt[4], axis=1, keepdims=True)
    slope = slope * column(freq[...], 0)
    b_one = jnp.sum(slope, axis=1, keepdims=True)
    shared[40 : 40 + feats, 0:units] = dot_nt(held["feat"][...].astype(low), slope.astype(low))
    vectors = pack_columns([(0, b_one), (1, q_one), (2, b_two), (3, q_two)], units)
    shared[144:152, 0:units] = jnp.transpose(vectors)[0:8, :]

    for name in ("tokens", "gain", "residual", "extra"):
        loads[name].wait()
    first_copy.wait()
    gain = held["gain"][0:1, :]

    def norm_rows(index, carry):
        rows = pl.ds(pl.multiple_of(index * CHUNK, CHUNK), CHUNK)
        own = pl.ds(pl.multiple_of(side * half_rows + index * CHUNK, CHUNK), CHUNK)
        values = held["tokens"][rows, :].astype(full)
        centred = values - jnp.mean(values, axis=-1, keepdims=True)
        inverse = lax.rsqrt(jnp.mean(centred * centred, axis=-1, keepdims=True) + norm_epsilon)
        normed_rows = centred * inverse
        back = first[own, :] + first_recv[rows, :].astype(full)
        scaled = back * gain
        grad_rows = inverse * (
            scaled
            - jnp.mean(scaled, axis=-1, keepdims=True)
            - normed_rows * jnp.mean(scaled * normed_rows, axis=-1, keepdims=True)
        )
        input_grad[rows, :] = held["residual"][rows, :] + grad_rows
        return (
            carry[0] + jnp.sum(back * normed_rows, axis=0, keepdims=True),
            carry[1] + jnp.sum(back, axis=0, keepdims=True),
        )

    zero = jnp.zeros((1, model_width), full)
    found = lax.fori_loop(0, half_rows // CHUNK, norm_rows, (zero, zero))
    extra = held["extra"]
    vectors = list(found) + [extra[i : i + 1, :] for i in range(4)]
    for index, vector in enumerate(vectors):
        for piece in range(model_width // 128):
            row = index * (model_width // 128) + piece
            shared[row : row + 1, :] = vector[:, piece * 128 : (piece + 1) * 128]

    shared_targets = [across, over] + flips

    def share(hop):
        copy = remote("s" + str(hop), shared, shared_hops.at[hop], shared_targets[hop])
        copy.start()
        return copy

    def shared_next(hop, copy):
        copy.wait()
        shared[...] = shared[...] + shared_hops[hop]
        return share(hop + 1) if hop < 4 else None

    def chan_next(hop, copy):
        copy.wait()
        chan[...] = chan[...] + chan_hops[hop]
        if hop == 2:
            return None
        copy = remote("c" + str(hop + 2), chan, chan_hops.at[hop + 1], flips[hop + 1])
        copy.start()
        return copy

    shared_copy = share(0)
    a_copy = hop_two("a", g_sum.at[0], 0, a_copy)
    b_copy = hop_two("b", g_sum.at[1], 1, b_copy)
    shared_copy = shared_next(0, shared_copy)
    chan_copy = chan_next(0, chan_copy)
    up_out[...] = hop_last("up", copies["up"])
    shared_copy = shared_next(1, shared_copy)
    a_copy = hop_three("a", a_copy)
    b_copy = hop_three("b", b_copy)
    chan_copy = chan_next(1, chan_copy)
    shared_copy = shared_next(2, shared_copy)
    down_out[...] = hop_last("down", copies["down"])
    chan_next(2, chan_copy)
    shared_copy = shared_next(3, shared_copy)
    op_out[:, : model_width // 2] = hop_last("a", a_copy)
    op_out[:, model_width // 2 :] = hop_last("b", b_copy)
    shared_next(4, shared_copy)
    shared_out[...] = shared[...]
    chan_out[...] = chan[...]


def call_operator_back(operands, width, length, model_width, dp_count):
    full, low = jnp.float32, jnp.bfloat16
    units = operands["w_mid"].shape[0]
    half_rows = length // 2
    block = model_width // BLOCKS
    grads = (2, 2, 2, block, model_width)
    held = []
    for name in LOADS:
        shape = operands[name].shape
        if name == "resid":
            shape = (length, model_width)
        held.append(pltpu.VMEM(shape, operands[name].dtype))
    wide, thin = pltpu.VMEM((width, length), full), pltpu.VMEM((width, length), low)
    chan = pltpu.VMEM((88, width), full)
    shared = pltpu.VMEM((152, 128), full)
    scratch = held + [wide] * 3 + [thin] * 4
    scratch += [
        pltpu.VMEM((4 * width, model_width), full),
        pltpu.VMEM((3 * width, length), low),
        pltpu.VMEM((units, length), full),
        pltpu.VMEM((length, model_width), full),
        pltpu.VMEM((half_rows, model_width), low),
        pltpu.VMEM((half_rows, model_width), low),
        pltpu.VMEM(grads, low),
        pltpu.VMEM(grads, low),
        pltpu.VMEM((2, 2, 2, 2, block, model_width // 2), low),
        pltpu.VMEM((width, 128), full),
        chan,
        chan,
        chan,
        pltpu.VMEM((3, 88, width), full),
        shared,
        pltpu.VMEM((5, 152, 128), full),
    ]
    for columns in (model_width, model_width, model_width // 2, model_width // 2):
        scratch += [
            pltpu.VMEM((2, 2, block, columns), low),
            pltpu.VMEM((2, block, columns), low),
            pltpu.VMEM((2, block, columns), full),
            pltpu.VMEM((2, block, columns), low),
            pltpu.VMEM((block, columns), low),
        ]
    scratch += [
        pltpu.SemaphoreType.DMA((len(LOADS),)),
        pltpu.SemaphoreType.DMA((len(PLAN),)),
        pltpu.SemaphoreType.DMA((len(PLAN),)),
    ]
    outs = (
        (half_rows, model_width),
        (block, model_width),
        (block, model_width),
        (block, model_width),
        (152, 128),
        (88, width),
    )
    return pl.pallas_call(
        functools.partial(operator_back, dp_count // BLOCKS),
        out_shape=tuple(jax.ShapeDtypeStruct(out, full) for out in outs),
        in_specs=[pl.BlockSpec(memory_space=pl.ANY)] * len(LOADS),
        out_specs=tuple(pl.BlockSpec(memory_space=pltpu.VMEM) for out in outs),
        scratch_shapes=scratch,
        compiler_params=pltpu.CompilerParams(
            vmem_limit_bytes=60 * 1024 * 1024, collective_id=0, has_side_effects=True
        ),
        cost_estimate=pl.CostEstimate(
            flops=4 * width * length * (10 * length + 8 * model_width),
            bytes_accessed=40 * 1024 * 1024,
            transcendentals=0,
        ),
        name="operator_back",
    )(*(operands[name] for name in LOADS))


def local(
    tokens,
    seq_counts,
    seq_lengths,
    norm1_gain,
    norm1_bias,
    in_weight,
    in_bias,
    conv_weight,
    conv_bias,
    filter_w1,
    filter_b1,
    filter_freq1,
    filter_w2,
    filter_b2,
    filter_freq2,
    filter_w3,
    filter_bias,
    out_weight,
    out_bias,
    norm2_gain,
    norm2_bias,
    up_weight,
    up_bias,
    down_weight,
    down_bias,
    cotangent,
):
    low = jnp.bfloat16
    full = jnp.float32
    tensor_count = lax.axis_size("tensor")
    dp_count = lax.axis_size("dp")
    row_share, model_width = tokens.shape
    local_width = in_weight.shape[1]
    slot_count = seq_lengths.shape[1]
    seq_length = row_share * tensor_count // slot_count
    part = lax.axis_index("tensor")
    side = part % 2
    group = lax.axis_index("dp")
    across = [(i, i ^ 1) for i in range(tensor_count)]
    over = [(i, i ^ 2) for i in range(tensor_count)]

    def behind(value, *others):
        return lax.optimization_barrier((value,) + others)[0]

    def swap(values):
        return lax.ppermute(values, "tensor", across)

    def cross(values):
        return lax.ppermute(values, "tensor", over)

    def pair(own, other):
        return jnp.concatenate(
            [jnp.where(side == 0, own, other), jnp.where(side == 0, other, own)], axis=0
        )

    def halves(rows):
        own = lax.dynamic_slice_in_dim(rows, side * row_share, row_share, 0)
        other = lax.dynamic_slice_in_dim(rows, (1 - side) * row_share, row_share, 0)
        return (own, other)

    def pair_sum(rows):
        own, other = halves(rows)
        return own + swap(other.astype(low)).astype(full)

    def dp_scatter(grad):
        blocks, width = dp_count, grad.shape[1]
        kept = grad.reshape(blocks, model_width // blocks, width)
        for bit_index in range(dp_count.bit_length() - 1):
            bit = (group >> bit_index) & 1
            blocks //= 2
            kept = kept.reshape(blocks, 2, model_width // dp_count, width)
            mine = lax.dynamic_index_in_dim(kept, bit, 1, keepdims=False)
            sent = lax.dynamic_index_in_dim(kept, 1 - bit, 1, keepdims=False)
            flips = [(i, i ^ (1 << bit_index)) for i in range(dp_count)]
            kept = mine + lax.ppermute(sent.astype(low), "dp", flips).astype(full)
        return kept.reshape(model_width // dp_count, width)

    def dp_sum(values):
        for bit_index in range(dp_count.bit_length() - 1):
            flips = [(i, i ^ (1 << bit_index)) for i in range(dp_count)]
            values = values + lax.ppermute(values, "dp", flips)
        return values

    first_row = part * row_share
    slot = first_row // seq_length
    position = first_row % seq_length + lax.broadcasted_iota(jnp.int32, (row_share, 1), 0)
    live = (slot < seq_counts[0]) & (position < lax.dynamic_index_in_dim(seq_lengths[0], slot, 0))
    mask_rows = live.astype(full)
    inputs = tokens.astype(full)
    normed_one, inv_one = norm_stats(inputs)
    normed_in_own = (normed_one * norm1_gain + norm1_bias).astype(low)
    normed_in = pair(normed_in_own, swap(normed_in_own))
    cot_rows = cotangent.astype(full) * mask_rows
    cot_own = cot_rows.astype(low)

    flat_in = in_weight.reshape(3 * local_width, model_width)
    own_weights = jnp.concatenate([flat_in, out_weight], axis=0)
    peer_weights = cross(own_weights)
    peer_in = peer_weights[: 3 * local_width].reshape(3, local_width, model_width)
    peer_out = peer_weights[3 * local_width :]
    chan = jnp.concatenate(
        [conv_weight.reshape(9, local_width), in_bias, conv_bias, filter_bias[None], filter_w3], axis=0
    )
    chan = jnp.concatenate([chan, cross(chan)], axis=1)
    conv_w = chan[:9].reshape(3, 3, -1)
    in_b, conv_b, filter_b, w_three = chan[9:12], chan[12:15], chan[15], chan[16:]
    in_w = jnp.concatenate([in_weight, peer_in], axis=1)
    out_w = jnp.concatenate([out_weight, peer_out], axis=0)

    table = fourier_table(seq_length)
    offsets = jnp.arange(local_width)
    channel = jnp.concatenate(
        [part * local_width + offsets, (part ^ 2) * local_width + offsets]
    ).astype(full)

    bands = (filter_w1.shape[0] - 1) // 2
    features = lax.optimization_barrier(positions(seq_length, bands)).T
    sum_one = jnp.dot(filter_w1.T, features, precision=highest) + filter_b1[:, None]
    angle_one = filter_freq1[:, None] * sum_one
    hidden_one = jnp.sin(angle_one)
    sum_two = jnp.dot(filter_w2.T, hidden_one, precision=highest) + filter_b2[:, None]
    angle_two = filter_freq2[:, None] * sum_two
    hidden_two = jnp.sin(angle_two)
    filter_held = jnp.stack(
        [hidden_one, hidden_two, jnp.cos(angle_one), jnp.cos(angle_two), sum_one, sum_two]
    )
    taps = jnp.einsum("hc,ht->ct", w_three, hidden_two, precision=highest) * decay(
        seq_length, channel, model_width
    )
    scale = 1.0 / seq_length
    taps_factor = split_factor(spectrum(taps, table), scale)

    projected = (
        jnp.einsum("icd,td->ict", in_w, normed_in, preferred_element_type=full) + in_b[:, :, None]
    )
    streams = conv_b[:, :, None] + sum(conv_w[j][:, :, None] * later(projected, j) for j in range(3))
    gate_out, gate_in, values = streams[0], streams[1], streams[2]
    mixed_in = values * gate_in
    signal = spectrum(mixed_in, table)
    conv_out = from_spectrum(times(signal, taps_factor), table) + mixed_in * filter_b[:, None]
    mixed = (conv_out * gate_out).astype(low)
    far_cot_own = cross(behind(cot_own, peer_weights))
    mixed, far_cot_own = lax.optimization_barrier((mixed, far_cot_own))
    branch = pair_sum(jnp.einsum("ct,cd->td", mixed, out_w, preferred_element_type=full))
    residual = inputs + branch + out_bias
    normed_two, inv_two = norm_stats(residual)
    mid_own = (normed_two * norm2_gain + norm2_bias).astype(low)

    far_mid_own = cross(mid_own)
    mid_near = pair(mid_own, swap(mid_own))
    cot_near = pair(cot_own, swap(cot_own))
    mid_far = pair(far_mid_own, swap(far_mid_own))
    cot_far = pair(far_cot_own, swap(far_cot_own))

    def mlp(mid, cot):
        pre_act = jnp.dot(mid, up_weight, preferred_element_type=full) + up_bias
        act, slope = gelu_both(pre_act)
        hidden = act.astype(low)
        hidden_grad = jnp.einsum("td,fd->tf", cot, down_weight, preferred_element_type=full)
        pre_grad = (hidden_grad * slope).astype(low)
        mid_part = jnp.einsum("tf,df->td", pre_grad, up_weight, preferred_element_type=full)
        return (hidden, pre_grad, mid_part)

    hidden_near, pre_grad_near, mid_part_near = mlp(mid_near, cot_near)
    mid_far = behind(mid_far, mid_part_near)
    hidden_far, pre_grad_far, mid_part_far = mlp(mid_far, cot_far)
    mid_sent = pair_sum(mid_part_far).astype(low)
    mid_back = cross(mid_sent)
    mid_near, mid_far, cot_near, cot_far, mid_part_near, hidden_far = lax.optimization_barrier(
        (mid_near, mid_far, cot_near, cot_far, mid_part_near, hidden_far, mid_sent)
    )[:6]

    def both(form, left, right):
        return jnp.einsum(form, left[0], right[0], preferred_element_type=full) + jnp.einsum(
            form, left[1], right[1], preferred_element_type=full
        )

    down_grad = both("td,tf->df", (cot_near, cot_far), (hidden_near, hidden_far))
    up_grad = both("td,tf->df", (mid_near, mid_far), (pre_grad_near, pre_grad_far))
    up_bias_grad = jnp.sum(pre_grad_near.astype(full), axis=0) + jnp.sum(
        pre_grad_far.astype(full), axis=0
    )
    down_part_near = jnp.dot(hidden_near, down_weight, preferred_element_type=full)
    down_part_far = jnp.dot(hidden_far, down_weight, preferred_element_type=full)
    mid_rows = pair_sum(mid_part_near)
    mid_back, up_grad, down_grad, mid_rows, down_part_near, down_part_far = lax.optimization_barrier(
        (mid_back, up_grad, down_grad, mid_rows, down_part_near, down_part_far)
    )
    mid_rows = mid_rows + mid_back.astype(full)

    residual_grad = cot_rows + norm_back(mid_rows, normed_two, inv_two, norm2_gain)
    gain_two_grad = jnp.sum(mid_rows * normed_two, axis=0)
    shift_two_grad = jnp.sum(mid_rows, axis=0)
    residual_low_own = residual_grad.astype(low)
    out_bias_grad = jnp.sum(residual_low_own.astype(full), axis=0)
    down_bias_grad = jnp.sum(cot_rows, axis=0)
    blocks = (2, 2, 2, model_width // BLOCKS, model_width)
    rates = slow_rate + (fast_rate - slow_rate) * channel / (model_width - 1)
    par = jnp.concatenate([chan[:16], rates[None] / (seq_length - 1)], axis=0)
    extra = jnp.stack([out_bias_grad, gain_two_grad, shift_two_grad, down_bias_grad])
    operands = {
        "resid": residual_low_own,
        "w_peer": peer_weights,
        "w_own": own_weights,
        "proj": projected,
        "conv": conv_out,
        "par": jnp.pad(par.T, ((0, 0), (0, 111))),
        "table": jnp.stack(table),
        "factor": jnp.stack(taps_factor),
        "signal": jnp.stack(signal),
        "normed": normed_in,
        "filt": filter_held,
        "w_last": jnp.stack([w_three[:, :local_width], w_three[:, local_width:]]),
        "up": up_grad.astype(low).reshape(blocks),
        "down": down_grad.astype(low).reshape(blocks),
        "w_mid": filter_w2,
        "feat": jnp.pad(features, ((0, 7), (0, 0))),
        "freq": jnp.pad(jnp.stack([filter_freq1, filter_freq2]).T, ((0, 0), (0, 126))),
        "tokens": tokens,
        "gain": jnp.pad(norm1_gain[None], ((0, 7), (0, 0))),
        "residual": residual_grad,
        "extra": jnp.pad(extra, ((0, 4), (0, 0))),
        "upb": jnp.pad(up_bias_grad.reshape(-1, local_width), ((0, 4), (0, 0))),
    }
    input_grad, op_part, up_part, down_part, shared, chan_grads = call_operator_back(
        operands, local_width, seq_length, model_width, dp_count
    )
    rest = dp_count.bit_length() - 4

    def rest_scatter(grad):
        for bit_index in range(rest):
            bit = (group >> bit_index) & 1
            count = 1 << (rest - 1 - bit_index)
            kept = grad.reshape(count, 2, model_width // dp_count, -1)
            mine = lax.dynamic_index_in_dim(kept, bit, 1, keepdims=False)
            sent = lax.dynamic_index_in_dim(kept, 1 - bit, 1, keepdims=False)
            flips = [(i, i ^ (1 << bit_index)) for i in range(dp_count)]
            grad = mine + lax.ppermute(sent.astype(low), "dp", flips).astype(full)
        return grad.reshape(model_width // dp_count, -1)

    def rest_sum(values):
        for bit_index in range(rest):
            flips = [(i, i ^ (1 << bit_index)) for i in range(dp_count)]
            values = values + lax.ppermute(values, "dp", flips)
        return values

    operator_grads = rest_scatter(op_part)
    up_grad, down_grad = rest_scatter(up_part), rest_scatter(down_part)
    shared, chan_grads = rest_sum(shared), rest_sum(chan_grads)
    down_sent = pair_sum(down_part_far).astype(low)
    down_back = cross(down_sent).astype(full)
    block_sum = pair_sum(down_part_near) + down_back
    activations = (mask_rows * (residual + block_sum + down_bias)).astype(low)
    pieces = model_width // 128
    wide = shared[: 6 * pieces].reshape(6, model_width)
    inputs_count = filter_w1.shape[0]
    units = filter_w2.shape[0]
    share = units // dp_count
    block = model_width // dp_count
    grad_in = operator_grads[:, : 3 * local_width].reshape(block, 3, local_width)
    return (
        activations,
        input_grad,
        wide[0],
        wide[1],
        jnp.transpose(grad_in, (1, 2, 0)),
        chan_grads[9:12],
        chan_grads[0:9].reshape(3, 3, local_width),
        chan_grads[12:15],
        shared[40 : 40 + inputs_count, :units],
        shared[144, :units],
        shared[145, :units],
        shared[80 : 80 + units, :units],
        shared[146, :units],
        shared[147, :units],
        lax.dynamic_slice_in_dim(chan_grads[16 : 16 + units], group * share, share, 0),
        chan_grads[15],
        jnp.transpose(operator_grads[:, 3 * local_width :]),
        wide[2],
        wide[3],
        wide[4],
        up_grad,
        chan_grads[80:84].reshape(-1),
        jnp.transpose(down_grad),
        wide[5],
    )


def solution(mesh):
    in_specs = (
        P(("dp", "tensor"), None),
        P("dp"),
        P("dp", None),
        P(),
        P(),
        P(None, "tensor", None),
        P(None, "tensor"),
        P(None, None, "tensor"),
        P(None, "tensor"),
        P(),
        P(),
        P(),
        P(),
        P(),
        P(),
        P(None, "tensor"),
        P("tensor"),
        P("tensor", None),
        P(),
        P(),
        P(),
        P(None, "tensor"),
        P("tensor"),
        P("tensor", None),
        P(),
        P(("dp", "tensor"), None),
    )
    out_specs = (
        P(("dp", "tensor"), None),
        P(("dp", "tensor"), None),
        P(),
        P(),
        P(None, "tensor", "dp"),
        P(None, "tensor"),
        P(None, None, "tensor"),
        P(None, "tensor"),
        P(),
        P(),
        P(),
        P(),
        P(),
        P(),
        P("dp", "tensor"),
        P("tensor"),
        P("tensor", "dp"),
        P(),
        P(),
        P(),
        P("dp", "tensor"),
        P("tensor"),
        P("tensor", "dp"),
        P(),
    )
    return jax.shard_map(local, mesh=mesh, in_specs=in_specs, out_specs=out_specs, check_vma=False)
```

```python
import functools
import math

import jax
import jax.numpy as jnp
from jax import lax
from jax.experimental import pallas as pl
from jax.experimental.pallas import tpu as pltpu
from jax.sharding import PartitionSpec as P

highest = lax.Precision.HIGHEST
norm_epsilon = 1e-05
slow_rate = math.log(100.0) / 1.5
fast_rate = math.log(100.0) / 0.3


def positions(length, bands):
    steps = jnp.arange(length).astype(jnp.float32)
    levels = (jnp.arange(bands) + 1).astype(jnp.float32)
    angle = 2.0 * math.pi / length * steps[:, None] * levels[None, :]
    return jnp.concatenate([steps[:, None] / (length - 1), jnp.cos(angle), -jnp.sin(angle)], axis=1)


def turn_seeds(length):
    low = 1 << (length.bit_length() // 2)
    steps = jnp.arange(length)[None, :]

    def turn(level):
        angle = (level[:, None] * steps % (2 * length)).astype(jnp.float32) * (math.pi / length)
        return (jnp.cos(angle), jnp.sin(angle))

    return jnp.stack(turn(jnp.arange(length // low) * low) + turn(jnp.arange(low)))


def dot_nt(left, right):
    return lax.dot_general(
        left, right, (((1,), (1,)), ((), ())), preferred_element_type=jnp.float32
    )


def dot_nn(left, right):
    return jnp.dot(left, right, preferred_element_type=jnp.float32)


def dot_tn(left, right):
    return lax.dot_general(
        left, right, (((0,), (0,)), ((), ())), preferred_element_type=jnp.float32
    )


def shifted(values, shift, lanes):
    length = values.shape[1]
    if shift == 0:
        return values
    if shift > 0:
        return jnp.where(lanes >= shift, pltpu.roll(values, shift, 1), 0.0)
    return jnp.where(lanes < length + shift, pltpu.roll(values, length + shift, 1), 0.0)


def column(params, index):
    return params[:, index : index + 1]


def pack_columns(columns, rows):
    lanes = lax.broadcasted_iota(jnp.int32, (rows, 128), 1)
    packed = jnp.zeros((rows, 128), jnp.float32)
    for index, values in columns:
        packed = jnp.where(lanes == index, values, packed)
    return packed


BLOCKS = 8
CHUNK = 16


def other_of(index, step):
    return index + step * (1 - 2 * ((index // step) % 2))


FRONT_PLAN = ("norm", "win", "wout", "par", "w3", "cotn", "coty", "cotf", "branch", "midn", "midy0", "midy1",
              "midf0", "midf1", "near", "farx0", "farx1", "back0", "back1", "downn", "downf")
FRONT_LOADS = ("tokens", "norms", "w_own", "par", "w3", "cot", "seeds", "feat", "fw1", "fw2", "fcol", "upb", "up", "down")
FRONT_OUTS = ("proj", "signal", "factor", "conv", "normed", "w_peer", "par", "table", "filt", "w_last",
              "resid", "residual_grad", "residual", "up_g", "down_g", "down_near", "down_far", "extra", "upb_g")


def gelu_parts(values):
    cdf = 0.5 * (1.0 + lax.erf(values * (1.0 / math.sqrt(2.0))))
    density = jnp.exp(-0.5 * values * values) * (1.0 / math.sqrt(2.0 * math.pi))
    return (values * cdf, cdf + values * density)


def normed_parts(values):
    centred = values - jnp.mean(values, axis=-1, keepdims=True)
    inverse = lax.rsqrt(jnp.mean(centred * centred, axis=-1, keepdims=True) + norm_epsilon)
    return (centred * inverse, inverse)


def norm_rows_back(back, normed, inverse, gain):
    scaled = back * gain
    return inverse * (
        scaled
        - jnp.mean(scaled, axis=-1, keepdims=True)
        - normed * jnp.mean(scaled * normed, axis=-1, keepdims=True)
    )


def path_place(row, block_rows, order):
    index, offset = row // block_rows, row % block_rows
    bits = [(index >> b) & 1 for b in range(3)]
    return (bits[order[0]] * 4 + bits[order[1]] * 2 + bits[order[2]]) * block_rows + offset


def store_rows(ref, start, values, block_rows, order):
    stop, begin = start + values.shape[0], start
    while begin < stop:
        size = min(block_rows - begin % block_rows, stop - begin)
        place = path_place(begin, block_rows, order)
        ref[place : place + size, :] = values[begin - start : begin - start + size, :]
        begin += size


HALVES = ("proj", "signal", "factor", "conv")
STORES = tuple(name + half for name in HALVES for half in "01") + FRONT_OUTS[4:]
PATHS = ((0, 1, 2), (1, 0, 2))


def operator_front(*refs):
    full, low = jnp.float32, jnp.bfloat16
    n, m = len(FRONT_LOADS), len(FRONT_OUTS)
    source = dict(zip(FRONT_LOADS, refs[:n]))
    target = dict(zip(FRONT_OUTS, refs[n : n + m]))
    held = dict(zip(FRONT_LOADS, refs[n + m : 2 * n + m]))
    made = dict(zip(FRONT_OUTS, refs[2 * n + m : 2 * n + 2 * m]))
    (mid_near, mid_far, cot_near, cot_far, hid_near, hid_far, pg_near, pg_far, acc, gates, inner, real,
     pair_a, pair_b, pair_c, send_row, recv_branch, recv_near, send_far, recv_far, send_back, recv_back,
     recv_down_near, recv_down_far, load_sem, store_sem, send_sem, recv_sem) = refs[2 * n + 2 * m :]

    part = lax.axis_index("tensor")
    side = part % 2
    across = {"tensor": other_of(part, 1)}
    over = {"tensor": other_of(part, 2)}
    width = gates.shape[0]
    length, model_width = acc.shape
    half = length // 2
    tile = half // 2
    mine = pl.ds(pl.multiple_of(side * half, half), half)
    theirs = pl.ds(pl.multiple_of((1 - side) * half, half), half)

    def mine_at(start, size):
        return pl.ds(pl.multiple_of(side * half + start, CHUNK), size)

    def theirs_at(start, size):
        return pl.ds(pl.multiple_of((1 - side) * half + start, CHUNK), size)

    def remote(name, src, dst, to):
        index = FRONT_PLAN.index(name)
        copy = pltpu.make_async_remote_copy(
            src_ref=src,
            dst_ref=dst,
            send_sem=send_sem.at[index],
            recv_sem=recv_sem.at[index],
            device_id=to,
            device_id_type=pl.DeviceIdType.MESH,
        )
        copy.start()
        return copy

    loads = {}
    for index, name in enumerate(FRONT_LOADS):
        place = held[name]
        if name == "cot":
            place = cot_near.at[mine]
        elif name == "par":
            place = made["par"].at[0:width]
        elif name == "w3":
            place = made["w_last"].at[0]
        loads[name] = pltpu.make_async_copy(source[name], place, load_sem.at[index])
        loads[name].start()
    stores = {}

    def put(name, src, dst):
        stores[name] = pltpu.make_async_copy(src, dst, store_sem.at[STORES.index(name)])
        stores[name].start()

    barrier = pltpu.get_barrier_semaphore()
    for to in (across, over):
        pl.semaphore_signal(barrier, inc=1, device_id=to, device_id_type=pl.DeviceIdType.MESH)
    pl.semaphore_wait(barrier, 2)

    normed, w_own, w_peer, par = made["normed"], held["w_own"], made["w_peer"], made["par"]
    norms = held["norms"]
    loads["w_own"].wait()
    copies = {"win": remote("win", w_own.at[0 : 3 * width], w_peer.at[0 : 3 * width], over)}
    loads["tokens"].wait()
    loads["norms"].wait()

    def norm_one(index, carry):
        rows = pl.ds(pl.multiple_of(index * CHUNK, CHUNK), CHUNK)
        lines = normed_parts(held["tokens"][rows, :].astype(full))[0]
        normed[mine_at(index * CHUNK, CHUNK), :] = (lines * norms[0:1, :] + norms[1:2, :]).astype(low)
        return carry

    lax.fori_loop(0, half // CHUNK, norm_one, 0)
    copies["norm"] = remote("norm", normed.at[mine], normed.at[mine], across)
    for name in ("par", "w3", "cot"):
        loads[name].wait()
    copies["wout"] = remote("wout", w_own.at[3 * width :], w_peer.at[3 * width :], over)
    copies["par"] = remote("par", par.at[0:width], par.at[width:], over)
    copies["w3"] = remote("w3", made["w_last"].at[0], made["w_last"].at[1], over)
    copies["coty"] = remote("coty", cot_near.at[mine], cot_far.at[mine], over)

    loads["seeds"].wait()
    seeds, table = held["seeds"], made["table"]
    lows = seeds.shape[1]
    for high in range(length // lows):
        cos_high, sin_high = seeds[0, high : high + 1, :], seeds[1, high : high + 1, :]
        cos_low, sin_low = seeds[2], seeds[3]
        rows = slice(high * lows, (high + 1) * lows)
        table[0, rows, :] = (cos_high * cos_low - sin_high * sin_low).astype(low)
        sines = sin_high * cos_low + cos_high * sin_low
        if high == 0:
            place = lax.broadcasted_iota(jnp.int32, sines.shape, 1)
            first = lax.broadcasted_iota(jnp.int32, sines.shape, 0) == 0
            sines = jnp.where(first, (1 - 2 * (place % 2)).astype(full), sines)
        table[1, rows, :] = sines.astype(low)
    put("table", table, target["table"])
    cos, sin = table.at[0], table.at[1]

    for name in ("feat", "fw1", "fw2", "fcol"):
        loads[name].wait()

    def exact_tn(left, right):
        return lax.dot_general(
            left, right, (((0,), (0,)), ((), ())), precision=highest, preferred_element_type=full
        )

    filt, fcol = made["filt"], held["fcol"][...]
    sum_one = exact_tn(held["fw1"][...], held["feat"][...]) + column(fcol, 2)
    angle = column(fcol, 0) * sum_one
    filt[0] = jnp.sin(angle)
    filt[2] = jnp.cos(angle)
    filt[4] = sum_one
    sum_two = exact_tn(held["fw2"][...], filt[0]) + column(fcol, 3)
    angle = column(fcol, 1) * sum_two
    filt[1] = jnp.sin(angle)
    filt[3] = jnp.cos(angle)
    filt[5] = sum_two
    put("filt", filt, target["filt"])

    lanes = lax.broadcasted_iota(jnp.int32, (CHUNK, length), 1)
    first_lane = lanes == 0
    scale = jnp.where(first_lane, 0.5 / length, 1.0 / length)
    proj, signal, factor, conv = made["proj"], made["signal"], made["factor"], made["conv"]

    def forward(side_index, weight):
        base = side_index * width
        if side_index == 1:
            for name in HALVES:
                stores.pop(name + "0").wait()
        real[...] = exact_tn(made["w_last"][side_index], filt[1])

        def windowed(index, carry):
            rows = pl.ds(pl.multiple_of(index * CHUNK, CHUNK), CHUNK)
            params = par[pl.ds(pl.multiple_of(base + index * CHUNK, CHUNK), CHUNK), :]
            pair_a[rows, :] = (
                real[rows, :] * jnp.exp(-lanes.astype(full) * column(params, 16))
            ).astype(low)
            return carry

        lax.fori_loop(0, width // CHUNK, windowed, 0)
        factor[0] = dot_nt(pair_a[...], cos[...])
        factor[1] = dot_nt(pair_a[...], sin[...])
        for i in range(3):
            proj[i] = dot_nt(weight[i * width : (i + 1) * width, :], normed[...]) + column(
                par[base : base + width, :], 9 + i
            )

        def mixing(index, carry):
            rows = pl.ds(pl.multiple_of(index * CHUNK, CHUNK), CHUNK)
            params = par[pl.ds(pl.multiple_of(base + index * CHUNK, CHUNK), CHUNK), :]

            def stream(i):
                line = proj[i, rows, :]
                return column(params, 12 + i) + sum(
                    column(params, 3 * j + i) * shifted(line, j, lanes) for j in range(3)
                )

            gates[rows, :] = stream(0)
            mixed_in = stream(1) * stream(2)
            inner[rows, :] = mixed_in
            pair_a[rows, :] = mixed_in.astype(low)
            return carry

        lax.fori_loop(0, width // CHUNK, mixing, 0)
        signal[0] = dot_nt(pair_a[...], cos[...])
        signal[1] = dot_nt(pair_a[...], sin[...])

        def product(index, carry):
            rows = pl.ds(pl.multiple_of(index * CHUNK, CHUNK), CHUNK)
            s_cos, s_sin = signal[0, rows, :] * scale, signal[1, rows, :] * scale
            f_cos, f_sin = factor[0, rows, :], factor[1, rows, :]
            f_last = jnp.where(first_lane, f_sin, f_cos)
            f_sin = jnp.where(first_lane, 0.0, f_sin)
            pair_a[rows, :] = (s_cos * f_cos - s_sin * f_sin).astype(low)
            pair_b[rows, :] = (s_cos * f_sin + s_sin * f_last).astype(low)
            return carry

        lax.fori_loop(0, width // CHUNK, product, 0)
        real[...] = dot_nn(pair_a[...], cos[...])
        real[...] += dot_nn(pair_b[...], sin[...])

        def gating(index, carry):
            rows = pl.ds(pl.multiple_of(index * CHUNK, CHUNK), CHUNK)
            params = par[pl.ds(pl.multiple_of(base + index * CHUNK, CHUNK), CHUNK), :]
            lines = real[rows, :] + inner[rows, :] * column(params, 15)
            conv[rows, :] = lines
            pair_c[rows, :] = (lines * gates[rows, :]).astype(low)
            return carry

        lax.fori_loop(0, width // CHUNK, gating, 0)
        for start in range(0, length, 256):
            piece = dot_tn(pair_c[:, start : start + 256], weight[3 * width :, :])
            if side_index == 0:
                acc[start : start + 256, :] = piece
            else:
                acc[start : start + 256, :] += piece
        span = slice(base, base + width)
        for name in HALVES:
            place = target[name].at[span] if name == "conv" else target[name].at[:, span]
            put(name + str(side_index), made[name], place)

    copies["norm"].wait()
    copies["cotn"] = remote("cotn", cot_near.at[mine], cot_near.at[mine], across)
    put("normed", normed, target["normed"])
    forward(0, w_own)
    for name in ("win", "wout", "par", "w3"):
        copies[name].wait()
    put("w_peer", w_peer, target["w_peer"])
    put("par", par, target["par"])
    put("w_last", made["w_last"], target["w_last"])
    forward(1, w_peer)

    send_row[...] = acc[theirs, :].astype(low)
    copies["branch"] = remote("branch", send_row, recv_branch, across)
    copies["branch"].wait()
    residual, residual_grad, resid = made["residual"], made["residual_grad"], made["resid"]

    def norm_two(chunk):
        def body(index, carry):
            start = chunk * tile + index * CHUNK
            rows = pl.ds(pl.multiple_of(start, CHUNK), CHUNK)
            place = mine_at(start, CHUNK)
            lines = (
                held["tokens"][rows, :].astype(full)
                + acc[place, :]
                + recv_branch[rows, :].astype(full)
                + norms[2:3, :]
            )
            residual[rows, :] = lines
            mid_near[place, :] = (normed_parts(lines)[0] * norms[3:4, :] + norms[4:5, :]).astype(low)
            return carry

        lax.fori_loop(0, tile // CHUNK, body, 0)
        place = mine_at(chunk * tile, tile)
        copies["midy" + str(chunk)] = remote("midy" + str(chunk), mid_near.at[place], mid_far.at[place], over)

    norm_two(0)
    norm_two(1)
    copies["midn"] = remote("midn", mid_near.at[mine], mid_near.at[mine], across)
    put("residual", residual, target["residual"])
    copies["cotn"].wait()
    for name in ("upb", "up", "down"):
        loads[name].wait()
    up, down, upb = held["up"], held["down"], held["upb"]
    bias_sum = [jnp.zeros((1, model_width), full)]

    def units(rows, mid, cot, hid, pg):
        act, slope = gelu_parts(dot_nn(mid[rows, :], up[...]) + upb[0:1, :])
        hid[rows, :] = act.astype(low)
        back = (dot_nt(cot[rows, :], down[...]) * slope).astype(low)
        pg[rows, :] = back
        return (dot_nt(back, up[...]), jnp.sum(back.astype(full), axis=0, keepdims=True))

    copies["midn"].wait()

    def near(index, total):
        rows = pl.ds(pl.multiple_of(index * tile, tile), tile)
        product, found = units(rows, mid_near, cot_near, hid_near, pg_near)
        acc[rows, :] = product
        return total + found

    total = lax.fori_loop(0, length // tile, near, jnp.zeros((1, model_width), full))
    send_row[...] = acc[theirs, :].astype(low)
    copies["near"] = remote("near", send_row, recv_near, across)

    copies["coty"].wait()
    copies["cotf"] = remote("cotf", cot_far.at[mine], cot_far.at[mine], across)
    copies["midy0"].wait()
    place = mine_at(0, tile)
    copies["midf0"] = remote("midf0", mid_far.at[place], mid_far.at[place], across)
    copies["cotf"].wait()
    for chunk in range(2):
        copies["midf" + str(chunk)].wait()
        product, found = units(theirs_at(chunk * tile, tile), mid_far, cot_far, hid_far, pg_far)
        total = total + found
        span = slice(chunk * tile, (chunk + 1) * tile)
        send_far[span, :] = product.astype(low)
        copies["farx" + str(chunk)] = remote("farx" + str(chunk), send_far.at[span], recv_far.at[span], across)
        product, found = units(mine_at(chunk * tile, tile), mid_far, cot_far, hid_far, pg_far)
        total = total + found
        if chunk == 0:
            copies["midy1"].wait()
            place = mine_at(tile, tile)
            copies["midf1"] = remote("midf1", mid_far.at[place], mid_far.at[place], across)
        copies["farx" + str(chunk)].wait()
        send_back[span, :] = (product + recv_far[span, :].astype(full)).astype(low)
        copies["back" + str(chunk)] = remote("back" + str(chunk), send_back.at[span], recv_back.at[span], over)

    for piece in range(model_width // 256):
        span = slice(piece * 256, (piece + 1) * 256)
        product = dot_tn(mid_near[:, span], pg_near[...]) + dot_tn(mid_far[:, span], pg_far[...])
        store_rows(made["up_g"], piece * 256, product.astype(low), model_width // BLOCKS, PATHS[0])
        product = dot_tn(cot_near[:, span], hid_near[...]) + dot_tn(cot_far[:, span], hid_far[...])
        store_rows(made["down_g"], piece * 256, product.astype(low), model_width // BLOCKS, PATHS[1])
    put("up_g", made["up_g"], target["up_g"])
    put("down_g", made["down_g"], target["down_g"])
    copies["near"].wait()
    down_near, down_far = made["down_near"], made["down_far"]
    send_row[...] = dot_nn(hid_far[theirs, :], down[...]).astype(low)
    copies["downf"] = remote("downf", send_row, recv_down_far, across)
    made["upb_g"][0:1, :] = total
    down_near[...] = dot_nn(hid_near[mine, :], down[...])
    copies["downf"].wait()
    down_far[...] = (dot_nn(hid_far[mine, :], down[...]) + recv_down_far[...].astype(full)).astype(low)
    put("down_far", down_far, target["down_far"])
    send_row[...] = dot_nn(hid_near[theirs, :], down[...]).astype(low)
    copies["downn"] = remote("downn", send_row, recv_down_near, across)
    copies["downn"].wait()
    down_near[...] += recv_down_near[...].astype(full)
    put("down_near", down_near, target["down_near"])

    sums = [jnp.zeros((1, model_width), full)] * 4
    sums = tuple(sums)
    for chunk in range(2):
        copies["back" + str(chunk)].wait()

        def body(index, carry):
            start = chunk * tile + index * CHUNK
            rows = pl.ds(pl.multiple_of(start, CHUNK), CHUNK)
            place = mine_at(start, CHUNK)
            normed_rows, inverse = normed_parts(residual[rows, :])
            back = acc[place, :] + recv_near[rows, :].astype(full) + recv_back[rows, :].astype(full)
            cots = cot_near[place, :].astype(full)
            grad = cots + norm_rows_back(back, normed_rows, inverse, norms[3:4, :])
            residual_grad[rows, :] = grad
            rounded = grad.astype(low)
            resid[rows, :] = rounded
            found = (rounded.astype(full), back * normed_rows, back, cots)
            return tuple(a + jnp.sum(b, axis=0, keepdims=True) for a, b in zip(carry, found))

        sums = lax.fori_loop(0, tile // CHUNK, body, sums)
    extra = made["extra"]
    for index in range(4):
        extra[index : index + 1, :] = sums[index]
    put("resid", resid, target["resid"])
    put("residual_grad", residual_grad, target["residual_grad"])
    put("extra", extra, target["extra"])
    put("upb_g", made["upb_g"], target["upb_g"])
    for copy in stores.values():
        copy.wait()


def call_operator_front(operands, width, length, model_width):
    full, low = jnp.float32, jnp.bfloat16
    half = length // 2
    channels = 2 * width
    units = operands["fw2"].shape[0]
    shapes = {
        "proj": ((3, channels, length), full),
        "signal": ((2, channels, length), full),
        "factor": ((2, channels, length), full),
        "conv": ((channels, length), full),
        "normed": ((length, model_width), low),
        "w_peer": ((4 * width, model_width), low),
        "par": ((channels, 128), full),
        "table": ((2, length, length), low),
        "filt": ((6, units, length), full),
        "w_last": ((2, units, width), full),
        "resid": ((half, model_width), low),
        "residual_grad": ((half, model_width), full),
        "residual": ((half, model_width), full),
        "up_g": ((model_width, model_width), low),
        "down_g": ((model_width, model_width), low),
        "down_near": ((half, model_width), full),
        "down_far": ((half, model_width), low),
        "extra": ((8, model_width), full),
        "upb_g": ((8, model_width), full),
    }
    split = {
        "proj": (3, width, length),
        "signal": (2, width, length),
        "factor": (2, width, length),
        "conv": (width, length),
    }
    placed = {"cot": (8, 128), "par": (8, 128), "w3": (8, 128)}
    rows = pltpu.VMEM((length, model_width), low)
    half_rows = pltpu.VMEM((half, model_width), low)
    wide, thin = pltpu.VMEM((width, length), full), pltpu.VMEM((width, length), low)
    scratch = [
        pltpu.VMEM(placed.get(name, operands[name].shape), operands[name].dtype) for name in FRONT_LOADS
    ]
    scratch += [pltpu.VMEM(split.get(name, shapes[name][0]), shapes[name][1]) for name in FRONT_OUTS]
    scratch += [rows] * 8 + [pltpu.VMEM((length, model_width), full)] + [wide] * 3 + [thin] * 3
    scratch += [half_rows] * 9
    scratch += [
        pltpu.SemaphoreType.DMA((len(FRONT_LOADS),)),
        pltpu.SemaphoreType.DMA((len(STORES),)),
        pltpu.SemaphoreType.DMA((len(FRONT_PLAN),)),
        pltpu.SemaphoreType.DMA((len(FRONT_PLAN),)),
    ]
    results = pl.pallas_call(
        operator_front,
        out_shape=tuple(jax.ShapeDtypeStruct(*shapes[name]) for name in FRONT_OUTS),
        in_specs=[pl.BlockSpec(memory_space=pl.ANY)] * len(FRONT_LOADS),
        out_specs=tuple(pl.BlockSpec(memory_space=pl.ANY) for name in FRONT_OUTS),
        scratch_shapes=scratch,
        compiler_params=pltpu.CompilerParams(
            vmem_limit_bytes=63 * 1024 * 1024, collective_id=1, has_side_effects=True
        ),
        name="operator_front",
    )(*(operands[name] for name in FRONT_LOADS))
    return dict(zip(FRONT_OUTS, results))


PLAN = ("resid", "downy", "up1", "down1", "up2", "down2", "up3", "down3", "gradsa", "gradsb", "chan", "first") + tuple(
    f"{name}{hop}" for name in ("a", "b", "c") for hop in (1, 2, 3)
) + tuple(f"s{hop}" for hop in range(5))
LOADS = ("resid", "w_peer", "w_own", "proj", "conv", "par", "table", "factor", "signal", "normed",
         "filt", "w_last", "up", "down", "down_far", "w_mid", "feat", "freq", "tokens", "gain", "rgrad", "extra", "upb",
         "residual", "down_near", "mask", "down_bias")


def operator_back(dp_step, outs, *refs):
    sizes = len(LOADS)
    source = dict(zip(LOADS, refs[:sizes]))
    out = dict(zip(outs, refs[sizes : sizes + len(outs)]))
    refs = refs[sizes + len(outs) :]
    held = dict(zip(LOADS, refs[: len(LOADS)]))
    refs = refs[len(LOADS) :]
    (grad, real, imag, pair_a, pair_b, pair_c, pair_d, stack, proj_low, h_grad, first, first_send, first_recv,
     peer_a, peer_b, recv_a, recv_b, sum_a, sum_b, recv_down, sums, chan_peer, chan_recv, chan, chan_hops,
     shared, shared_hops) = refs[:27]
    hops = dict(zip(("up", "down", "a", "b"), (refs[27 + 5 * i : 32 + 5 * i] for i in range(4))))
    load_sem, send_sem, recv_sem = refs[47:]
    full, low = jnp.float32, jnp.bfloat16

    part = lax.axis_index("tensor")
    group = lax.axis_index("dp")
    side = part % 2
    bits = [(group // (dp_step << b)) % 2 for b in range(3)]
    across = {"tensor": other_of(part, 1)}
    over = {"tensor": other_of(part, 2)}
    flips = [{"dp": other_of(group, dp_step << b)} for b in range(3)]

    def remote(name, src, dst, target):
        index = PLAN.index(name)
        return pltpu.make_async_remote_copy(
            src_ref=src,
            dst_ref=dst,
            send_sem=send_sem.at[index],
            recv_sem=recv_sem.at[index],
            device_id=target,
            device_id_type=pl.DeviceIdType.MESH,
        )

    width, length = grad.shape
    model_width = first.shape[1]
    half_rows = length // 2
    block_rows = model_width // BLOCKS
    mine = pl.ds(pl.multiple_of(side * half_rows, half_rows), half_rows)
    theirs = pl.ds(pl.multiple_of((1 - side) * half_rows, half_rows), half_rows)

    loads = {
        name: pltpu.make_async_copy(
            source[name],
            held[name].at[mine] if name == "resid" else held[name],
            load_sem.at[index],
        )
        for index, name in enumerate(LOADS)
    }
    for name in LOADS:
        loads[name].start()

    barrier = pltpu.get_barrier_semaphore()
    for target in [across, over] + flips:
        pl.semaphore_signal(barrier, inc=1, device_id=target, device_id_type=pl.DeviceIdType.MESH)
    pl.semaphore_wait(barrier, 5)

    resid = held["resid"]
    resid_copy = remote("resid", source["resid"], resid.at[mine], across)
    resid_copy.start()
    loads["resid"].wait()
    loads["w_peer"].wait()
    loads["w_own"].wait()
    resid_copy.wait()

    def spot(index, size):
        return pl.ds(pl.multiple_of(index * size, size), size)

    def order_of(name):
        return PATHS[0] if name in ("up", "a") else PATHS[1]

    def hop_one(name, grads):
        bit = order_of(name)[0]
        src = grads.at[spot(1 - bits[bit], 4 * block_rows)]
        copy = remote(name + "1", src, hops[name][0], flips[bit])
        copy.start()
        return copy

    def hop_two(name, grads, copy):
        recv_one, send_two, keep_two, recv_two, _ = hops[name]
        top, bit, _ = order_of(name)
        copy.wait()
        for keep in (0, 1):
            pick = bits[bit] if keep else 1 - bits[bit]
            total = (
                grads[spot(2 * bits[top] + pick, 2 * block_rows), :].astype(full)
                + recv_one[spot(pick, 2 * block_rows), :].astype(full)
            )
            if keep:
                keep_two[...] = total
            else:
                send_two[...] = total.astype(low)
                copy = remote(name + "2", send_two, recv_two, flips[bit])
                copy.start()
        return copy

    def hop_three(name, copy):
        recv_one, send_two, keep_two, recv_two, recv_three = hops[name]
        bit = order_of(name)[2]
        copy.wait()
        place = spot(1 - bits[bit], block_rows)
        send_two[0:block_rows, :] = (keep_two[place, :] + recv_two[place, :].astype(full)).astype(low)
        copy = remote(name + "3", send_two.at[0:block_rows], recv_three, flips[bit])
        copy.start()
        return copy

    def hop_last(name, copy):
        recv_one, send_two, keep_two, recv_two, recv_three = hops[name]
        copy.wait()
        place = spot(bits[order_of(name)[2]], block_rows)
        return keep_two[place, :] + recv_two[place, :].astype(full) + recv_three[...].astype(full)

    loads["up"].wait()
    loads["down"].wait()
    loads["down_far"].wait()
    copies = {"up": hop_one("up", held["up"]), "down": hop_one("down", held["down"])}
    copies["downy"] = remote("downy", held["down_far"], recv_down, over)
    copies["downy"].start()

    lanes = lax.broadcasted_iota(jnp.int32, (CHUNK, length), 1)
    par, proj, conv = held["par"], held["proj"], held["conv"]
    cos, sin = held["table"].at[0], held["table"].at[1]
    factor, signal, normed = held["factor"], held["signal"], held["normed"]
    filt = held["filt"]
    weights = (held["w_own"], held["w_peer"])

    def half_pass(half, loaded, middle):
        base = half * width
        weight = weights[half]
        own_w = 3 * width

        def at(index):
            return pl.ds(pl.multiple_of(index * CHUNK, CHUNK), CHUNK)

        def far(index):
            return pl.ds(pl.multiple_of(base + index * CHUNK, CHUNK), CHUNK)

        def stream(i, rows, params):
            line = proj[i, rows, :]
            lines = [line, shifted(line, 1, lanes), shifted(line, 2, lanes)]
            total = column(params, 12 + i) + sum(column(params, 3 * j + i) * lines[j] for j in range(3))
            return (lines, total)

        def stream_back(i, index, params, back, lines):
            out = sum(column(params, 3 * j + i) * shifted(back, -j, lanes) for j in range(3)).astype(low)
            start = pl.multiple_of(i * width + index * CHUNK, CHUNK)
            proj_low[pl.ds(start, CHUNK), :] = out
            found = [(3 * j + i, jnp.sum(back * lines[j], axis=1, keepdims=True)) for j in range(3)]
            found.append((9 + i, jnp.sum(out.astype(full), axis=1, keepdims=True)))
            found.append((12 + i, jnp.sum(back, axis=1, keepdims=True)))
            return found

        grad[...] = dot_nt(weight[own_w:, :], resid[...])
        if not loaded:
            for name in ("proj", "conv", "par"):
                loads[name].wait()

        def before(index, carry):
            rows = far(index)
            params = par[rows, :]
            lines, gate_out = stream(0, rows, params)
            gate_in = stream(1, rows, params)[1]
            values = stream(2, rows, params)[1]
            mixed_grad = grad[at(index), :]
            conv_part = conv[rows, :]
            conv_grad = mixed_grad * gate_out
            grad[at(index), :] = conv_grad
            pair_a[at(index), :] = conv_grad.astype(low)
            pair_b[at(index), :] = (conv_part * gate_out).astype(low)
            found = stream_back(0, index, params, mixed_grad * conv_part, lines)
            found.append((15, jnp.sum(conv_grad * values * gate_in, axis=1, keepdims=True)))
            sums[at(index), :] = pack_columns(found, CHUNK)
            return carry

        lax.fori_loop(0, width // CHUNK, before, 0)
        stack[3 * width :, :] = dot_nn(pair_b[...], resid[...])
        if not loaded:
            loads["table"].wait()
        real[...] = dot_nt(pair_a[...], cos[...])
        imag[...] = dot_nt(pair_a[...], sin[...])
        if not loaded:
            loads["factor"].wait()
            loads["signal"].wait()
        first_lane = lanes == 0
        scale = jnp.where(first_lane, 0.5 / length, 1.0 / length)

        def between(index, carry):
            rows, place = far(index), at(index)
            cos_part, sin_part = real[place, :] * scale, imag[place, :] * scale
            f_cos, f_sin = factor[0, rows, :], factor[1, rows, :]
            f_last = jnp.where(first_lane, f_sin, f_cos)
            f_sin = jnp.where(first_lane, 0.0, f_sin)
            pair_a[place, :] = (cos_part * f_cos + sin_part * f_sin).astype(low)
            pair_b[place, :] = (sin_part * f_last - cos_part * f_sin).astype(low)
            s_cos, s_sin = signal[0, rows, :], signal[1, rows, :]
            s_last = jnp.where(first_lane, s_sin, s_cos)
            s_sin = jnp.where(first_lane, 0.0, s_sin)
            pair_c[place, :] = (cos_part * s_cos + sin_part * s_sin).astype(low)
            pair_d[place, :] = (sin_part * s_last - cos_part * s_sin).astype(low)
            return carry

        lax.fori_loop(0, width // CHUNK, between, 0)
        middle()
        real[...] = dot_nn(pair_a[...], cos[...]) + dot_nn(pair_b[...], sin[...])
        imag[...] = dot_nn(pair_c[...], cos[...]) + dot_nn(pair_d[...], sin[...])

        def after(index, carry):
            rows = far(index)
            params = par[rows, :]
            lines_in, gate_in = stream(1, rows, params)
            lines_value, values = stream(2, rows, params)
            back = real[at(index), :] + grad[at(index), :] * column(params, 15)
            found = stream_back(1, index, params, back * values, lines_in)
            found += stream_back(2, index, params, back * gate_in, lines_value)
            sums[at(index), :] = sums[at(index), :] + pack_columns(found, CHUNK)
            window = jnp.exp(-lanes.astype(full) * column(params, 16))
            pair_a[at(index), :] = (imag[at(index), :] * window).astype(low)
            return carry

        lax.fori_loop(0, width // CHUNK, after, 0)
        if not loaded:
            for name in ("normed", "filt", "w_last"):
                loads[name].wait()
        stack[: 3 * width, :] = dot_nn(proj_low[...], normed[...])
        target = chan_peer if half == 1 else chan
        target[0:16, :] = jnp.transpose(sums[...])[0:16, :]
        target[16:80, :] = dot_nt(filt[1].astype(low), pair_a[...])
        h_part = dot_nn(held["w_last"][half].astype(low), pair_a[...])
        if half == 1:
            h_grad[...] = h_part
        else:
            h_grad[...] += h_part

    def turned(store):
        middle = model_width // 2
        for start in range(0, model_width, 128):
            block = jnp.transpose(stack[:, start : start + 128])
            begin = start
            while begin < start + 128:
                size = min(block_rows - begin % block_rows, start + 128 - begin)
                piece = block[begin - start : begin - start + size, :]
                for path, columns in enumerate((piece[:, :middle], piece[:, middle:])):
                    place = path_place(begin, block_rows, PATHS[path])
                    store(path, slice(place, place + size), columns)
                begin += size

    def store_peer(path, rows, values):
        (peer_a, peer_b)[path][rows, :] = values.astype(low)

    def store_sum(path, rows, values):
        total = values + (recv_a, recv_b)[path][rows, :].astype(full)
        (sum_a, sum_b)[path][rows, :] = total.astype(low)

    def first_part(half):
        for start in range(0, length, 256):
            product = dot_tn(proj_low[:, start : start + 256], weights[half][: 3 * width, :])
            if half == 1:
                first[start : start + 256, :] = product
            else:
                first[start : start + 256, :] += product

    half_pass(1, False, lambda: None)
    turned(store_peer)
    chan_peer[80:88, :] = jnp.zeros((8, width), full)
    copies["gradsa"] = remote("gradsa", peer_a, recv_a, over)
    copies["gradsb"] = remote("gradsb", peer_b, recv_b, over)
    copies["chan"] = remote("chan", chan_peer, chan_recv, over)
    for name in ("gradsa", "gradsb", "chan"):
        copies[name].start()
    first_part(1)
    for name in ("up", "down"):
        copies[name] = hop_two(name, held[name], copies[name])

    def last_hops():
        for name in ("up", "down"):
            copies[name] = hop_three(name, copies[name])

    half_pass(0, True, last_hops)
    first_part(0)
    first_send[...] = first[theirs, :].astype(low)
    first_copy = remote("first", first_send, first_recv, across)
    first_copy.start()
    copies["gradsa"].wait()
    copies["gradsb"].wait()
    turned(store_sum)
    copies["a"] = hop_one("a", sum_a)
    copies["b"] = hop_one("b", sum_b)

    copies["chan"].wait()
    loads["upb"].wait()
    chan[0:80, :] = chan[0:80, :] + chan_recv[0:80, :]
    chan[80:88, :] = jnp.zeros((8, width), full)
    for index in range(held["upb"].shape[1] // width):
        chan[80 + index : 81 + index, :] = held["upb"][0:1, index * width : (index + 1) * width]
    chan_copy = remote("c1", chan, chan_hops.at[0], flips[0])
    chan_copy.start()

    for name in ("w_mid", "feat", "freq"):
        loads[name].wait()
    freq, w_mid = held["freq"], held["w_mid"]
    shared[...] = jnp.zeros_like(shared)
    units = w_mid.shape[0]
    feats = held["feat"].shape[0]
    slope = h_grad[...] * filt[3]
    q_two = jnp.sum(slope * filt[5], axis=1, keepdims=True)
    slope = slope * column(freq[...], 1)
    b_two = jnp.sum(slope, axis=1, keepdims=True)
    slope_low = slope.astype(low)
    shared[80 : 80 + units, 0:units] = dot_nt(filt[0].astype(low), slope_low)
    slope = dot_nn(w_mid[...].astype(low), slope_low) * filt[2]
    q_one = jnp.sum(slope * filt[4], axis=1, keepdims=True)
    slope = slope * column(freq[...], 0)
    b_one = jnp.sum(slope, axis=1, keepdims=True)
    shared[40 : 40 + feats, 0:units] = dot_nt(held["feat"][...].astype(low), slope.astype(low))
    vectors = pack_columns([(0, b_one), (1, q_one), (2, b_two), (3, q_two)], units)
    shared[144:152, 0:units] = jnp.transpose(vectors)[0:8, :]

    for name in ("tokens", "gain", "rgrad", "extra"):
        loads[name].wait()
    first_copy.wait()
    gain = held["gain"][0:1, :]

    def norm_rows(index, carry):
        rows = pl.ds(pl.multiple_of(index * CHUNK, CHUNK), CHUNK)
        own = pl.ds(pl.multiple_of(side * half_rows + index * CHUNK, CHUNK), CHUNK)
        normed_rows, inverse = normed_parts(held["tokens"][rows, :].astype(full))
        back = first[own, :] + first_recv[rows, :].astype(full)
        grad_rows = norm_rows_back(back, normed_rows, inverse, gain)
        out["input_grad"][rows, :] = held["rgrad"][rows, :] + grad_rows
        return (
            carry[0] + jnp.sum(back * normed_rows, axis=0, keepdims=True),
            carry[1] + jnp.sum(back, axis=0, keepdims=True),
        )

    zero = jnp.zeros((1, model_width), full)
    found = lax.fori_loop(0, half_rows // CHUNK, norm_rows, (zero, zero))
    extra = held["extra"]
    vectors = list(found) + [extra[i : i + 1, :] for i in range(4)]
    for index, vector in enumerate(vectors):
        for piece in range(model_width // 128):
            row = index * (model_width // 128) + piece
            shared[row : row + 1, :] = vector[:, piece * 128 : (piece + 1) * 128]

    shared_targets = [across, over] + flips

    def share(hop):
        copy = remote("s" + str(hop), shared, shared_hops.at[hop], shared_targets[hop])
        copy.start()
        return copy

    def shared_next(hop, copy):
        copy.wait()
        shared[...] = shared[...] + shared_hops[hop]
        return share(hop + 1) if hop < 4 else None

    def chan_next(hop, copy):
        copy.wait()
        chan[...] = chan[...] + chan_hops[hop]
        if hop == 2:
            return None
        copy = remote("c" + str(hop + 2), chan, chan_hops.at[hop + 1], flips[hop + 1])
        copy.start()
        return copy

    shared_copy = share(0)
    for name, grads in (("a", sum_a), ("b", sum_b)):
        copies[name] = hop_two(name, grads, copies[name])
    shared_copy = shared_next(0, shared_copy)
    chan_copy = chan_next(0, chan_copy)

    for name in ("residual", "down_near", "mask", "down_bias"):
        loads[name].wait()
    copies["downy"].wait()

    def result_rows(index, carry):
        rows = pl.ds(pl.multiple_of(index * CHUNK, CHUNK), CHUNK)
        total = held["residual"][rows, :] + held["down_near"][rows, :] + recv_down[rows, :].astype(full)
        total = (total + held["down_bias"][0:1, :]) * held["mask"][rows, 0:1]
        out["activations"][rows, :] = total.astype(low)
        return carry

    lax.fori_loop(0, half_rows // CHUNK, result_rows, 0)
    shared_copy = shared_next(1, shared_copy)
    for name in ("a", "b"):
        copies[name] = hop_three(name, copies[name])
    chan_copy = chan_next(1, chan_copy)
    shared_copy = shared_next(2, shared_copy)
    up_part = hop_last("up", copies["up"])
    out["up"][...] = up_part
    down_part = hop_last("down", copies["down"])
    out["down"][...] = jnp.transpose(down_part) if "wide0" in out else down_part
    chan_next(2, chan_copy)
    shared_copy = shared_next(3, shared_copy)
    for name in ("a", "b"):
        part_sum = hop_last(name, copies[name])
        if "wide0" in out:
            part_sum = jnp.transpose(part_sum)
            if name == "a":
                out["in"][0] = part_sum[0:width, :]
                out["in"][1] = part_sum[width:, :]
            else:
                out["in"][2] = part_sum[0:width, :]
                out["out"][...] = part_sum[width:, :]
        else:
            out[name][...] = part_sum
    shared_next(4, shared_copy)
    if "wide0" not in out:
        out["shared"][...] = shared[...]
        out["chan"][...] = chan[...]
        return
    pieces = model_width // 128
    for index in range(6):
        for piece in range(pieces):
            row = index * pieces + piece
            out["wide" + str(index)][0:1, piece * 128 : (piece + 1) * 128] = shared[row : row + 1, :]
    out["w1"][...] = shared[40 : 40 + out["w1"].shape[0], 0:units]
    out["w2"][...] = shared[80 : 80 + units, 0:units]
    for index in range(4):
        out["vec" + str(index)][...] = shared[144 + index : 145 + index, 0:units]
    for name, start in (("conv_w", 0), ("in_b", 9), ("conv_b", 12), ("f_bias", 15), ("up_b", 80)):
        out[name][...] = chan[start : start + out[name].shape[0], :]
    share_rows = out["w3"].shape[0]
    out["w3"][...] = chan[pl.ds(pl.multiple_of(16 + group * share_rows, 8), share_rows), :]


def call_operator_back(operands, width, length, model_width, dp_count):
    full, low = jnp.float32, jnp.bfloat16
    units = operands["w_mid"].shape[0]
    half_rows = length // 2
    block = model_width // BLOCKS
    thin_grads = pltpu.VMEM((model_width, model_width // 2), low)
    low_rows = pltpu.VMEM((half_rows, model_width), low)
    held = []
    for name in LOADS:
        shape = operands[name].shape
        if name == "resid":
            shape = (length, model_width)
        held.append(pltpu.VMEM(shape, operands[name].dtype))
    wide, thin = pltpu.VMEM((width, length), full), pltpu.VMEM((width, length), low)
    chan = pltpu.VMEM((88, width), full)
    shared = pltpu.VMEM((152, 128), full)
    scratch = held + [wide] * 3 + [thin] * 4
    scratch += [
        pltpu.VMEM((4 * width, model_width), full),
        pltpu.VMEM((3 * width, length), low),
        pltpu.VMEM((units, length), full),
        pltpu.VMEM((length, model_width), full),
        low_rows,
        low_rows,
        thin_grads,
        thin_grads,
        thin_grads,
        thin_grads,
        thin_grads,
        thin_grads,
        low_rows,
        pltpu.VMEM((width, 128), full),
        chan,
        chan,
        chan,
        pltpu.VMEM((3, 88, width), full),
        shared,
        pltpu.VMEM((5, 152, 128), full),
    ]
    for columns in (model_width, model_width, model_width // 2, model_width // 2):
        scratch += [
            pltpu.VMEM((4 * block, columns), low),
            pltpu.VMEM((2 * block, columns), low),
            pltpu.VMEM((2 * block, columns), full),
            pltpu.VMEM((2 * block, columns), low),
            pltpu.VMEM((block, columns), low),
        ]
    scratch += [
        pltpu.SemaphoreType.DMA((len(LOADS),)),
        pltpu.SemaphoreType.DMA((len(PLAN),)),
        pltpu.SemaphoreType.DMA((len(PLAN),)),
    ]
    shapes = {"activations": (half_rows, model_width), "input_grad": (half_rows, model_width)}
    if dp_count == BLOCKS:
        shapes.update({"wide" + str(i): (1, model_width) for i in range(6)})
        shapes.update({"vec" + str(i): (1, units) for i in range(4)})
        shapes.update(
            {
                "in": (3, width, block),
                "out": (width, block),
                "up": (block, model_width),
                "down": (model_width, block),
                "w1": (operands["w_one"].shape[0], units),
                "w2": (units, units),
                "w3": (units // BLOCKS, width),
                "conv_w": (9, width),
                "in_b": (3, width),
                "conv_b": (3, width),
                "f_bias": (1, width),
                "up_b": (model_width // width, width),
            }
        )
    else:
        shapes.update({"up": (block, model_width), "down": (block, model_width)})
        shapes.update({"a": (block, model_width // 2), "b": (block, model_width // 2)})
        shapes.update({"shared": (152, 128), "chan": (88, width)})
    outs = tuple(shapes)
    results = pl.pallas_call(
        functools.partial(operator_back, dp_count // BLOCKS, outs),
        out_shape=tuple(
            jax.ShapeDtypeStruct(shapes[name], low if name == "activations" else full) for name in outs
        ),
        in_specs=[pl.BlockSpec(memory_space=pl.ANY)] * len(LOADS),
        out_specs=tuple(pl.BlockSpec(memory_space=pltpu.VMEM) for out in outs),
        scratch_shapes=scratch,
        compiler_params=pltpu.CompilerParams(
            vmem_limit_bytes=63 * 1024 * 1024, collective_id=0, has_side_effects=True
        ),
        cost_estimate=pl.CostEstimate(
            flops=4 * width * length * (10 * length + 8 * model_width),
            bytes_accessed=40 * 1024 * 1024,
            transcendentals=0,
        ),
        name="operator_back",
    )(*(operands[name] for name in LOADS))
    return dict(zip(outs, results))


def local(
    tokens,
    seq_counts,
    seq_lengths,
    norm1_gain,
    norm1_bias,
    in_weight,
    in_bias,
    conv_weight,
    conv_bias,
    filter_w1,
    filter_b1,
    filter_freq1,
    filter_w2,
    filter_b2,
    filter_freq2,
    filter_w3,
    filter_bias,
    out_weight,
    out_bias,
    norm2_gain,
    norm2_bias,
    up_weight,
    up_bias,
    down_weight,
    down_bias,
    cotangent,
):
    low = jnp.bfloat16
    full = jnp.float32
    tensor_count = lax.axis_size("tensor")
    dp_count = lax.axis_size("dp")
    row_share, model_width = tokens.shape
    width = in_weight.shape[1]
    slot_count = seq_lengths.shape[1]
    length = row_share * tensor_count // slot_count
    part = lax.axis_index("tensor")
    group = lax.axis_index("dp")

    first_row = part * row_share
    slot = first_row // length
    position = first_row % length + lax.broadcasted_iota(jnp.int32, (row_share, 128), 0)
    live = (slot < seq_counts[0]) & (position < lax.dynamic_index_in_dim(seq_lengths[0], slot, 0))
    mask = live.astype(full)
    cot_own = (cotangent.astype(full) * mask[:, 0:1]).astype(low)

    channel = (part * width + jnp.arange(width)).astype(full)
    rates = slow_rate + (fast_rate - slow_rate) * channel / (model_width - 1)
    par = jnp.concatenate(
        [conv_weight.reshape(9, width), in_bias, conv_bias, filter_bias[None], rates[None] / (length - 1)]
    )

    def pad_rows(rows, count):
        return jnp.pad(rows, ((0, count - rows.shape[0]), (0, 0)))

    def pad_columns(rows):
        return jnp.pad(jnp.stack(rows).T, ((0, 0), (0, 128 - len(rows))))

    bands = (filter_w1.shape[0] - 1) // 2
    inputs_count = filter_w1.shape[0]
    units = filter_w2.shape[0]
    padded = -(-inputs_count // 8) * 8
    features = pad_rows(positions(length, bands).T, padded)
    own_weights = jnp.concatenate([in_weight.reshape(3 * width, model_width), out_weight], axis=0)
    freq = pad_columns([filter_freq1, filter_freq2, filter_b1, filter_b2])
    front = call_operator_front(
        {
            "tokens": tokens,
            "norms": pad_rows(
                jnp.stack([norm1_gain, norm1_bias, out_bias, norm2_gain, norm2_bias, down_bias]), 8
            ),
            "w_own": own_weights,
            "par": pad_columns(list(par)),
            "w3": filter_w3,
            "cot": cot_own,
            "seeds": turn_seeds(length),
            "feat": features,
            "fw1": pad_rows(filter_w1, padded),
            "fw2": filter_w2,
            "fcol": freq,
            "upb": pad_rows(up_bias[None], 8),
            "up": up_weight,
            "down": down_weight,
        },
        width,
        length,
        model_width,
    )
    back = call_operator_back(
        {
            "resid": front["resid"],
            "w_peer": front["w_peer"],
            "w_own": own_weights,
            "proj": front["proj"],
            "conv": front["conv"],
            "par": front["par"],
            "table": front["table"],
            "factor": front["factor"],
            "signal": front["signal"],
            "normed": front["normed"],
            "filt": front["filt"],
            "w_last": front["w_last"],
            "up": front["up_g"],
            "down": front["down_g"],
            "down_far": front["down_far"],
            "w_mid": filter_w2,
            "feat": features,
            "freq": freq,
            "tokens": tokens,
            "gain": pad_rows(norm1_gain[None], 8),
            "rgrad": front["residual_grad"],
            "extra": front["extra"],
            "upb": front["upb_g"],
            "residual": front["residual"],
            "down_near": front["down_near"],
            "mask": mask,
            "down_bias": pad_rows(down_bias[None], 8),
            "w_one": filter_w1,
        },
        width,
        length,
        model_width,
        dp_count,
    )
    if dp_count == BLOCKS:
        return (
            back["activations"],
            back["input_grad"],
            back["wide0"].reshape(-1),
            back["wide1"].reshape(-1),
            back["in"],
            back["in_b"],
            back["conv_w"].reshape(3, 3, width),
            back["conv_b"],
            back["w1"],
            back["vec0"].reshape(-1),
            back["vec1"].reshape(-1),
            back["w2"],
            back["vec2"].reshape(-1),
            back["vec3"].reshape(-1),
            back["w3"],
            back["f_bias"].reshape(-1),
            back["out"],
            back["wide2"].reshape(-1),
            back["wide3"].reshape(-1),
            back["wide4"].reshape(-1),
            back["up"],
            back["up_b"].reshape(-1),
            back["down"],
            back["wide5"].reshape(-1),
        )

    rest = dp_count.bit_length() - BLOCKS.bit_length()

    def flips(bit_index):
        return [(i, i ^ (1 << bit_index)) for i in range(dp_count)]

    def rest_scatter(grad):
        for bit_index in range(rest):
            bit = (group >> bit_index) & 1
            kept = grad.reshape(1 << (rest - 1 - bit_index), 2, model_width // dp_count, -1)
            mine = lax.dynamic_index_in_dim(kept, bit, 1, keepdims=False)
            sent = lax.dynamic_index_in_dim(kept, 1 - bit, 1, keepdims=False)
            grad = mine + lax.ppermute(sent.astype(low), "dp", flips(bit_index)).astype(full)
        return grad.reshape(model_width // dp_count, -1)

    def rest_sum(values):
        for bit_index in range(rest):
            values = values + lax.ppermute(values, "dp", flips(bit_index))
        return values

    operator_grads = rest_scatter(jnp.concatenate([back["a"], back["b"]], axis=1))
    shared, chan = rest_sum(back["shared"]), rest_sum(back["chan"])
    wide = shared[: 6 * (model_width // 128)].reshape(6, model_width)
    share = units // dp_count
    grad_in = operator_grads[:, : 3 * width].reshape(-1, 3, width)
    return (
        back["activations"],
        back["input_grad"],
        wide[0],
        wide[1],
        jnp.transpose(grad_in, (1, 2, 0)),
        chan[9:12],
        chan[0:9].reshape(3, 3, width),
        chan[12:15],
        shared[40 : 40 + inputs_count, :units],
        shared[144, :units],
        shared[145, :units],
        shared[80 : 80 + units, :units],
        shared[146, :units],
        shared[147, :units],
        lax.dynamic_slice_in_dim(chan[16 : 16 + units], group * share, share, 0),
        chan[15],
        jnp.transpose(operator_grads[:, 3 * width :]),
        wide[2],
        wide[3],
        wide[4],
        rest_scatter(back["up"]),
        chan[80 : 80 + model_width // width].reshape(-1),
        jnp.transpose(rest_scatter(back["down"])),
        wide[5],
    )


def solution(mesh):
    in_specs = (
        P(("dp", "tensor"), None),
        P("dp"),
        P("dp", None),
        P(),
        P(),
        P(None, "tensor", None),
        P(None, "tensor"),
        P(None, None, "tensor"),
        P(None, "tensor"),
        P(),
        P(),
        P(),
        P(),
        P(),
        P(),
        P(None, "tensor"),
        P("tensor"),
        P("tensor", None),
        P(),
        P(),
        P(),
        P(None, "tensor"),
        P("tensor"),
        P("tensor", None),
        P(),
        P(("dp", "tensor"), None),
    )
    out_specs = (
        P(("dp", "tensor"), None),
        P(("dp", "tensor"), None),
        P(),
        P(),
        P(None, "tensor", "dp"),
        P(None, "tensor"),
        P(None, None, "tensor"),
        P(None, "tensor"),
        P(),
        P(),
        P(),
        P(),
        P(),
        P(),
        P("dp", "tensor"),
        P("tensor"),
        P("tensor", "dp"),
        P(),
        P(),
        P(),
        P("dp", "tensor"),
        P("tensor"),
        P("tensor", "dp"),
        P(),
    )
    return jax.shard_map(local, mesh=mesh, in_specs=in_specs, out_specs=out_specs, check_vma=False)
```

```python
import functools
import math

import jax
import jax.numpy as jnp
import numpy as np
from jax import lax
from jax.experimental import pallas as pl
from jax.experimental.pallas import tpu as pltpu
from jax.sharding import PartitionSpec as P

highest = lax.Precision.HIGHEST
norm_epsilon = 1e-05
slow_rate = math.log(100.0) / 1.5
fast_rate = math.log(100.0) / 0.3


def positions(length, bands):
    steps = np.arange(length)
    levels = np.arange(bands)[:, None] + 1
    angle = (levels * steps % length) * (2.0 * math.pi / length)
    return np.concatenate([steps[None] / (length - 1), np.cos(angle), -np.sin(angle)]).astype(np.float32)


def turn_seeds(length):
    low = 1 << (length.bit_length() // 2)
    steps = np.arange(length)[None]

    def turn(level):
        angle = (level[:, None] * steps % (2 * length)) * (math.pi / length)
        return [np.cos(angle), np.sin(angle)]

    return np.stack(turn(np.arange(length // low) * low) + turn(np.arange(low))).astype(np.float32)


def dot_nt(left, right):
    return lax.dot_general(
        left, right, (((1,), (1,)), ((), ())), preferred_element_type=jnp.float32
    )


def dot_nn(left, right):
    return jnp.dot(left, right, preferred_element_type=jnp.float32)


def dot_tn(left, right):
    return lax.dot_general(
        left, right, (((0,), (0,)), ((), ())), preferred_element_type=jnp.float32
    )


def shifted(values, shift, lanes):
    length = values.shape[1]
    if shift == 0:
        return values
    if shift > 0:
        return jnp.where(lanes >= shift, pltpu.roll(values, shift, 1), 0.0)
    return jnp.where(lanes < length + shift, pltpu.roll(values, length + shift, 1), 0.0)


def column(params, index):
    return params[:, index : index + 1]


def pack_columns(columns, rows):
    lanes = lax.broadcasted_iota(jnp.int32, (rows, 128), 1)
    packed = jnp.zeros((rows, 128), jnp.float32)
    for index, values in columns:
        packed = jnp.where(lanes == index, values, packed)
    return packed


BLOCKS = 8
CHUNK = 64
ROWS = 128


def other_of(index, step):
    return index + step * (1 - 2 * ((index // step) % 2))


TENSOR = "tensor"
DP = "dp"


class N:
    (
        a, activations, b, b1, b2, back, branch, cb, chan, conv, conv_b, conv_w, cot, cotf, cotn,
        coty, cw, down, down_b, down_bias, down_far, down_g, down_near, downf, downn, downy, extra,
        f_bias, factor, farx, fb, fb1, fb2, feat, ff1, ff2, filt, first, freq, fw1, fw2, g1, g2,
        gain, gain1, gain2, ib, in_b, in_w, input_grad, midf, midn, midy, near, norm, normed, ob,
        out, out_b, par, peer_a, peer_b, proj, resid, residual, residual_grad, rgrad, seeds, shared,
        shift1, shift2, signal, streams, table, tokens, up, up_b, up_g, upb, upb_g, w1, w2, w3,
        w_in, w_last, w_mid, w_out, w_peer, wx, wy, y_a, y_b,
    ) = range(92)


FRONT_PLAN = ((N.wy, 0), (N.wy, 1), (N.wy, 2), (N.wx, 0), (N.wx, 1), (N.wx, 2), N.norm, N.par, N.w3, N.cotn, N.coty, N.cotf, N.branch, N.midn, (N.midy, 0), (N.midy, 1),
              (N.midf, 0), (N.midf, 1), N.near, (N.farx, 0), (N.farx, 1), (N.back, 0), (N.back, 1), N.downn, N.downf)
FRONT_LOADS = (N.w_in, N.w_out, N.tokens, N.g1, N.b1, N.cw, N.ib, N.cb, N.fb, N.w3, N.cot, N.seeds, N.feat, N.fw1,
               N.fw2, N.fb1, N.ff1, N.fb2, N.ff2, N.ob, N.g2, N.b2, N.upb, N.up, N.down)
FRONT_OUTS = (N.proj, N.streams, N.signal, N.factor, N.conv, N.normed, N.w_peer, N.par, N.table, N.filt, N.w_last,
              N.resid, N.residual_grad, N.residual, N.up_g, N.down_g, N.down_near, N.down_far, N.extra, N.upb_g, N.freq)


def gelu_parts(values):
    cdf = 0.5 * (1.0 + lax.erf(values * (1.0 / math.sqrt(2.0))))
    density = jnp.exp(-0.5 * values * values) * (1.0 / math.sqrt(2.0 * math.pi))
    return (values * cdf, cdf + values * density)


def normed_parts(values):
    centred = values - jnp.mean(values, axis=-1, keepdims=True)
    inverse = lax.rsqrt(jnp.mean(centred * centred, axis=-1, keepdims=True) + norm_epsilon)
    return (centred * inverse, inverse)


def norm_rows_back(back, normed, inverse, gain):
    scaled = back * gain
    return inverse * (
        scaled
        - jnp.mean(scaled, axis=-1, keepdims=True)
        - normed * jnp.mean(scaled * normed, axis=-1, keepdims=True)
    )


def path_place(row, block_rows, order):
    index, offset = row // block_rows, row % block_rows
    bits = [(index >> b) & 1 for b in range(3)]
    return (bits[order[0]] * 4 + bits[order[1]] * 2 + bits[order[2]]) * block_rows + offset


def store_rows(ref, start, values, block_rows, order):
    stop, begin = start + values.shape[0], start
    while begin < stop:
        size = min(block_rows - begin % block_rows, stop - begin)
        place = path_place(begin, block_rows, order)
        ref[place : place + size, :] = values[begin - start : begin - start + size, :]
        begin += size


HALVES = (N.proj, N.streams, N.signal, N.factor, N.conv)
STORES = tuple((name, half) for name in HALVES for half in (0, 1)) + FRONT_OUTS[5:]
WIDES = (N.gain1, N.shift1, N.out_b, N.gain2, N.shift2, N.down_b)
VECTORS = (N.fb1, N.ff1, N.fb2, N.ff2)
RAW = (N.activations, N.input_grad, N.up, N.down, N.a, N.b, N.shared, N.chan)
RESULTS = (N.activations, N.input_grad, N.gain1, N.shift1, N.in_w, N.in_b, N.conv_w, N.conv_b, N.w1, N.fb1, N.ff1, N.w2,
           N.fb2, N.ff2, N.w3, N.f_bias, N.out, N.out_b, N.gain2, N.shift2, N.up, N.up_b, N.down, N.down_b)
PATHS = ((0, 1, 2), (1, 0, 2))


def operator_front(*refs):
    full, low = jnp.float32, jnp.bfloat16
    n, m = len(FRONT_LOADS), len(FRONT_OUTS)
    source = dict(zip(FRONT_LOADS, refs[:n]))
    counts, lengths = refs[n], refs[n + 1]
    refs = refs[:n] + refs[n + 2 :]
    target = dict(zip(FRONT_OUTS, refs[n : n + m]))
    held = dict(zip(FRONT_LOADS, refs[n + m : 2 * n + m]))
    made = dict(zip(FRONT_OUTS, refs[2 * n + m : 2 * n + 2 * m]))
    (mid_near, mid_far, cot_near, cot_far, hid_near, hid_far, pg_near, pg_far, acc, inner, real,
     pair_a, pair_b, pair_c, send_row, recv_branch, recv_near, send_far, recv_far, send_back, recv_back,
     recv_down_near, recv_down_far, w_own, norms, lines, fcol, load_sem, store_sem, send_sem, recv_sem,
     ) = refs[2 * n + 2 * m :]

    part = lax.axis_index(TENSOR)
    group = lax.axis_index(DP)
    side = part % 2
    across = {TENSOR: other_of(part, 1)}
    over = {TENSOR: other_of(part, 2)}
    beside = {DP: other_of(group, 1)}
    width = inner.shape[0]
    length, model_width = acc.shape
    half = length // 2
    tile = half // 2
    mine = pl.ds(pl.multiple_of(side * half, half), half)
    theirs = pl.ds(pl.multiple_of((1 - side) * half, half), half)

    def mine_at(start, size):
        return pl.ds(pl.multiple_of(side * half + start, 16), size)

    def theirs_at(start, size):
        return pl.ds(pl.multiple_of((1 - side) * half + start, 16), size)

    def remote(name, src, dst, to):
        index = FRONT_PLAN.index(name)
        copy = pltpu.make_async_remote_copy(
            src_ref=src,
            dst_ref=dst,
            send_sem=send_sem.at[index],
            recv_sem=recv_sem.at[index],
            device_id=to,
            device_id_type=pl.DeviceIdType.MESH,
        )
        copy.start()
        return copy

    loads = {}
    for index, name in enumerate(FRONT_LOADS):
        place = held[name]
        if name == N.w_in:
            place = w_own.at[0 : 3 * width]
        elif name == N.w_out:
            place = w_own.at[3 * width :]
        elif name == N.w3:
            place = made[N.w_last].at[0]
        loads[name] = pltpu.make_async_copy(source[name], place, load_sem.at[index])
        loads[name].start()
    stores = {}

    def put(name, src, dst):
        stores[name] = pltpu.make_async_copy(src, dst, store_sem.at[STORES.index(name)])
        stores[name].start()

    barrier = pltpu.get_barrier_semaphore()
    for to in (across, over, beside):
        pl.semaphore_signal(barrier, inc=1, device_id=to, device_id_type=pl.DeviceIdType.MESH)
    pl.semaphore_wait(barrier, 3)

    normed, w_peer, par = made[N.normed], made[N.w_peer], made[N.par]
    loads[N.w_in].wait()
    loads[N.w_out].wait()
    pieces = 3
    share = 4 * width // (2 * pieces)
    copies = {}

    def weight_rows(piece):
        return pl.ds(pl.multiple_of((2 * piece + group % 2) * share, 16), share)

    for piece in range(pieces):
        rows = weight_rows(piece)
        copies[N.wy, piece] = remote((N.wy, piece), w_own.at[rows], w_peer.at[rows], over)

    def pass_on(piece):
        copies[N.wy, piece].wait()
        rows = weight_rows(piece)
        copies[N.wx, piece] = remote((N.wx, piece), w_peer.at[rows], w_peer.at[rows], beside)

    for name in (N.tokens, N.g1, N.b1, N.ob, N.g2, N.b2, N.upb):
        loads[name].wait()
    for index, name in enumerate((N.g1, N.b1, N.ob, N.g2, N.b2, N.upb)):
        norms[index : index + 1, :] = held[name][...][None, :]

    def norm_one(index, carry):
        rows = pl.ds(pl.multiple_of(index * ROWS, ROWS), ROWS)
        values = normed_parts(held[N.tokens][rows, :].astype(full))[0]
        normed[mine_at(index * ROWS, ROWS), :] = (values * norms[0:1, :] + norms[1:2, :]).astype(low)
        return carry

    lax.fori_loop(0, half // ROWS, norm_one, 0)
    copies[N.norm] = remote(N.norm, normed.at[mine], normed.at[mine], across)

    for name in (N.cw, N.ib, N.cb, N.fb, N.w3):
        loads[name].wait()
    lines[...] = jnp.zeros_like(lines)
    lines[0:9, :] = held[N.cw][...].reshape(9, width)
    lines[9:12, :] = held[N.ib][...]
    lines[12:15, :] = held[N.cb][...]
    lines[15:16, :] = held[N.fb][...][None, :]
    channel = (part * width + lax.broadcasted_iota(jnp.int32, (1, width), 1)).astype(full)
    channels = 4 * width
    lines[16:17, :] = (slow_rate + (fast_rate - slow_rate) / (channels - 1) * channel) * (1.0 / (length - 1))
    par[0:width, 0:24] = jnp.transpose(lines[...])
    copies[N.par] = remote(N.par, par.at[0:width], par.at[width:], over)
    copies[N.w3] = remote(N.w3, made[N.w_last].at[0], made[N.w_last].at[1], over)

    loads[N.cot].wait()
    slot = part * half // length
    mask_rows = jnp.where(slot < counts[0], lengths[0, slot], 0) - part * half % length

    def mask_cot(index, carry):
        rows = pl.ds(pl.multiple_of(index * ROWS, ROWS), ROWS)
        place = lax.broadcasted_iota(jnp.int32, (ROWS, model_width), 0) + index * ROWS
        values = held[N.cot][rows, :]
        cot_near[mine_at(index * ROWS, ROWS), :] = jnp.where(
            place < mask_rows, values.astype(full), 0.0
        ).astype(low)
        return carry

    lax.fori_loop(0, half // ROWS, mask_cot, 0)
    copies[N.coty] = remote(N.coty, cot_near.at[mine], cot_far.at[mine], over)

    loads[N.seeds].wait()
    seeds, table = held[N.seeds], made[N.table]
    lows = seeds.shape[1]
    for high in range(length // lows):
        cos_high, sin_high = seeds[0, high : high + 1, :], seeds[1, high : high + 1, :]
        cos_low, sin_low = seeds[2], seeds[3]
        rows = slice(high * lows, (high + 1) * lows)
        table[0, rows, :] = (cos_high * cos_low - sin_high * sin_low).astype(low)
        sines = sin_high * cos_low + cos_high * sin_low
        if high == 0:
            place = lax.broadcasted_iota(jnp.int32, sines.shape, 1)
            first = lax.broadcasted_iota(jnp.int32, sines.shape, 0) == 0
            sines = jnp.where(first, (1 - 2 * (place % 2)).astype(full), sines)
        table[1, rows, :] = sines.astype(low)
    put(N.table, table, target[N.table])
    pass_on(0)
    cos, sin = table.at[0], table.at[1]

    for name in (N.feat, N.fw1, N.fw2, N.fb1, N.ff1, N.fb2, N.ff2):
        loads[name].wait()

    def exact_tn(left, right):
        return lax.dot_general(
            left, right, (((0,), (0,)), ((), ())), precision=highest, preferred_element_type=full
        )

    filt = made[N.filt]
    units = held[N.fw2].shape[0]
    fcol[...] = jnp.zeros_like(fcol)
    for index, name in enumerate((N.ff1, N.ff2, N.fb1, N.fb2)):
        fcol[index : index + 1, 0:units] = held[name][...][None, :]
    freq = made[N.freq]
    freq[...] = jnp.zeros_like(freq)
    freq[:, 0:8] = jnp.transpose(fcol[...])[0:units, :]
    fcol = freq[...]
    put(N.freq, freq, target[N.freq])
    sum_one = exact_tn(held[N.fw1][...], held[N.feat][...]) + column(fcol, 2)
    angle = column(fcol, 0) * sum_one
    filt[0] = jnp.sin(angle)
    filt[2] = jnp.cos(angle)
    filt[4] = sum_one
    sum_two = exact_tn(held[N.fw2][...], filt[0]) + column(fcol, 3)
    angle = column(fcol, 1) * sum_two
    filt[1] = jnp.sin(angle)
    filt[3] = jnp.cos(angle)
    filt[5] = sum_two
    put(N.filt, filt, target[N.filt])
    pass_on(1)

    lanes = lax.broadcasted_iota(jnp.int32, (CHUNK, length), 1)
    first_lane = lanes == 0
    scale = jnp.where(first_lane, 0.5 / length, 1.0 / length)
    proj, signal, factor, conv = made[N.proj], made[N.signal], made[N.factor], made[N.conv]
    streams = made[N.streams]

    def forward(side_index, weight):
        base = side_index * width
        if side_index == 1:
            for name in HALVES:
                stores.pop((name, 0)).wait()
        real[...] = exact_tn(made[N.w_last][side_index], filt[1])

        def windowed(index, carry):
            rows = pl.ds(pl.multiple_of(index * CHUNK, CHUNK), CHUNK)
            params = par[pl.ds(pl.multiple_of(base + index * CHUNK, CHUNK), CHUNK), :]
            pair_a[rows, :] = (
                real[rows, :] * jnp.exp(-lanes.astype(full) * column(params, 16))
            ).astype(low)
            return carry

        lax.fori_loop(0, width // CHUNK, windowed, 0)
        factor[0] = dot_nn(pair_a[...], cos[...])
        factor[1] = dot_nt(pair_a[...], sin[...])
        if side_index == 0:
            pass_on(2)
        for i in range(3):
            streams[i] = dot_nt(weight[i * width : (i + 1) * width, :], normed[...]) + column(
                par[base : base + width, :], 9 + i
            )

        def mixing(index, carry):
            rows = pl.ds(pl.multiple_of(index * CHUNK, CHUNK), CHUNK)
            params = par[pl.ds(pl.multiple_of(base + index * CHUNK, CHUNK), CHUNK), :]

            def stream(i):
                line = streams[i, rows, :]
                proj[i, rows, :] = line.astype(low)
                total = column(params, 12 + i) + sum(
                    column(params, 3 * j + i) * shifted(line, j, lanes) for j in range(3)
                )
                streams[i, rows, :] = total
                return total

            stream(0)
            mixed_in = stream(1) * stream(2)
            inner[rows, :] = mixed_in
            pair_a[rows, :] = mixed_in.astype(low)
            return carry

        lax.fori_loop(0, width // CHUNK, mixing, 0)
        signal[0] = dot_nn(pair_a[...], cos[...])
        signal[1] = dot_nt(pair_a[...], sin[...])

        def product(index, carry):
            rows = pl.ds(pl.multiple_of(index * CHUNK, CHUNK), CHUNK)
            s_cos, s_sin = signal[0, rows, :] * scale, signal[1, rows, :] * scale
            f_cos, f_sin = factor[0, rows, :], factor[1, rows, :]
            f_last = jnp.where(first_lane, f_sin, f_cos)
            f_sin = jnp.where(first_lane, 0.0, f_sin)
            pair_a[rows, :] = (s_cos * f_cos - s_sin * f_sin).astype(low)
            pair_b[rows, :] = (s_cos * f_sin + s_sin * f_last).astype(low)
            return carry

        lax.fori_loop(0, width // CHUNK, product, 0)
        real[...] = dot_nn(pair_a[...], cos[...])
        real[...] += dot_nn(pair_b[...], sin[...])

        def gating(index, carry):
            rows = pl.ds(pl.multiple_of(index * CHUNK, CHUNK), CHUNK)
            params = par[pl.ds(pl.multiple_of(base + index * CHUNK, CHUNK), CHUNK), :]
            lines = real[rows, :] + inner[rows, :] * column(params, 15)
            conv[rows, :] = lines
            pair_c[rows, :] = (lines * streams[0, rows, :]).astype(low)
            return carry

        lax.fori_loop(0, width // CHUNK, gating, 0)
        for start in range(0, length, 256):
            piece = dot_tn(pair_c[:, start : start + 256], weight[3 * width :, :])
            if side_index == 0:
                acc[start : start + 256, :] = piece
            else:
                acc[start : start + 256, :] += piece
        span = slice(base, base + width)
        for name in HALVES:
            place = target[name].at[span] if name == N.conv else target[name].at[:, span]
            put((name, side_index), made[name], place)

    copies[N.norm].wait()
    copies[N.cotn] = remote(N.cotn, cot_near.at[mine], cot_near.at[mine], across)
    put(N.normed, normed, target[N.normed])
    forward(0, w_own)
    for name in (N.par, N.w3) + tuple((N.wx, piece) for piece in range(pieces)):
        copies[name].wait()
    put(N.w_peer, w_peer, target[N.w_peer])
    put(N.par, par, target[N.par])
    put(N.w_last, made[N.w_last], target[N.w_last])
    forward(1, w_peer)

    send_row[...] = acc[theirs, :].astype(low)
    copies[N.branch] = remote(N.branch, send_row, recv_branch, across)
    copies[N.branch].wait()
    residual, residual_grad, resid = made[N.residual], made[N.residual_grad], made[N.resid]

    def norm_two(chunk):
        def body(index, carry):
            start = chunk * tile + index * ROWS
            rows = pl.ds(pl.multiple_of(start, ROWS), ROWS)
            place = mine_at(start, ROWS)
            lines = (
                held[N.tokens][rows, :].astype(full)
                + acc[place, :]
                + recv_branch[rows, :].astype(full)
                + norms[2:3, :]
            )
            residual[rows, :] = lines
            mid_near[place, :] = (normed_parts(lines)[0] * norms[3:4, :] + norms[4:5, :]).astype(low)
            return carry

        lax.fori_loop(0, tile // ROWS, body, 0)
        place = mine_at(chunk * tile, tile)
        copies[N.midy, chunk] = remote((N.midy, chunk), mid_near.at[place], mid_far.at[place], over)

    norm_two(0)
    norm_two(1)
    copies[N.midn] = remote(N.midn, mid_near.at[mine], mid_near.at[mine], across)
    put(N.residual, residual, target[N.residual])
    copies[N.cotn].wait()
    for name in (N.up, N.down):
        loads[name].wait()
    up, down = held[N.up], held[N.down]

    def units(rows, mid, cot, hid, pg):
        act, slope = gelu_parts(dot_nn(mid[rows, :], up[...]) + norms[5:6, :])
        hid[rows, :] = act.astype(low)
        back = (dot_nt(cot[rows, :], down[...]) * slope).astype(low)
        pg[rows, :] = back
        return (dot_nt(back, up[...]), jnp.sum(back.astype(full), axis=0, keepdims=True))

    copies[N.midn].wait()

    def near(index, total):
        rows = pl.ds(pl.multiple_of(index * tile, tile), tile)
        product, found = units(rows, mid_near, cot_near, hid_near, pg_near)
        acc[rows, :] = product
        return total + found

    total = lax.fori_loop(0, length // tile, near, jnp.zeros((1, model_width), full))
    send_row[...] = acc[theirs, :].astype(low)
    copies[N.near] = remote(N.near, send_row, recv_near, across)

    copies[N.coty].wait()
    copies[N.cotf] = remote(N.cotf, cot_far.at[mine], cot_far.at[mine], across)
    copies[N.midy, 0].wait()
    place = mine_at(0, tile)
    copies[N.midf, 0] = remote((N.midf, 0), mid_far.at[place], mid_far.at[place], across)
    copies[N.cotf].wait()
    for chunk in range(2):
        copies[N.midf, chunk].wait()
        product, found = units(theirs_at(chunk * tile, tile), mid_far, cot_far, hid_far, pg_far)
        total = total + found
        span = slice(chunk * tile, (chunk + 1) * tile)
        send_far[span, :] = product.astype(low)
        copies[N.farx, chunk] = remote((N.farx, chunk), send_far.at[span], recv_far.at[span], across)
        product, found = units(mine_at(chunk * tile, tile), mid_far, cot_far, hid_far, pg_far)
        total = total + found
        if chunk == 0:
            copies[N.midy, 1].wait()
            place = mine_at(tile, tile)
            copies[N.midf, 1] = remote((N.midf, 1), mid_far.at[place], mid_far.at[place], across)
        copies[N.farx, chunk].wait()
        send_back[span, :] = (product + recv_far[span, :].astype(full)).astype(low)
        copies[N.back, chunk] = remote((N.back, chunk), send_back.at[span], recv_back.at[span], over)

    for piece in range(model_width // 256):
        span = slice(piece * 256, (piece + 1) * 256)
        product = dot_tn(mid_near[:, span], pg_near[...]) + dot_tn(mid_far[:, span], pg_far[...])
        store_rows(made[N.up_g], piece * 256, product.astype(low), model_width // BLOCKS, PATHS[0])
        product = dot_tn(cot_near[:, span], hid_near[...]) + dot_tn(cot_far[:, span], hid_far[...])
        store_rows(made[N.down_g], piece * 256, product.astype(low), model_width // BLOCKS, PATHS[1])
    put(N.up_g, made[N.up_g], target[N.up_g])
    put(N.down_g, made[N.down_g], target[N.down_g])
    copies[N.near].wait()
    down_near, down_far = made[N.down_near], made[N.down_far]
    send_row[...] = dot_nn(hid_far[theirs, :], down[...]).astype(low)
    copies[N.downf] = remote(N.downf, send_row, recv_down_far, across)
    made[N.upb_g][0:1, :] = total
    down_near[...] = dot_nn(hid_near[mine, :], down[...])
    copies[N.downf].wait()
    down_far[...] = (dot_nn(hid_far[mine, :], down[...]) + recv_down_far[...].astype(full)).astype(low)
    put(N.down_far, down_far, target[N.down_far])
    send_row[...] = dot_nn(hid_near[theirs, :], down[...]).astype(low)
    copies[N.downn] = remote(N.downn, send_row, recv_down_near, across)
    copies[N.downn].wait()
    down_near[...] += recv_down_near[...].astype(full)
    put(N.down_near, down_near, target[N.down_near])

    sums = [jnp.zeros((1, model_width), full)] * 4
    sums = tuple(sums)
    for chunk in range(2):
        copies[N.back, chunk].wait()

        def body(index, carry):
            start = chunk * tile + index * ROWS
            rows = pl.ds(pl.multiple_of(start, ROWS), ROWS)
            place = mine_at(start, ROWS)
            normed_rows, inverse = normed_parts(residual[rows, :])
            back = acc[place, :] + recv_near[rows, :].astype(full) + recv_back[rows, :].astype(full)
            cots = cot_near[place, :].astype(full)
            grad = cots + norm_rows_back(back, normed_rows, inverse, norms[3:4, :])
            residual_grad[rows, :] = grad
            rounded = grad.astype(low)
            resid[rows, :] = rounded
            found = (rounded.astype(full), back * normed_rows, back, cots)
            return tuple(a + jnp.sum(b, axis=0, keepdims=True) for a, b in zip(carry, found))

        sums = lax.fori_loop(0, tile // ROWS, body, sums)
    extra = made[N.extra]
    for index in range(4):
        extra[index : index + 1, :] = sums[index]
    put(N.resid, resid, target[N.resid])
    put(N.residual_grad, residual_grad, target[N.residual_grad])
    put(N.extra, extra, target[N.extra])
    put(N.upb_g, made[N.upb_g], target[N.upb_g])
    for copy in stores.values():
        copy.wait()


def call_operator_front(operands, counts, lengths, width, length, model_width):
    full, low = jnp.float32, jnp.bfloat16
    half = length // 2
    channels = 2 * width
    units = operands[N.fw2].shape[0]
    shapes = {
        N.proj: ((3, channels, length), low),
        N.streams: ((3, channels, length), full),
        N.signal: ((2, channels, length), full),
        N.factor: ((2, channels, length), full),
        N.conv: ((channels, length), full),
        N.normed: ((length, model_width), low),
        N.w_peer: ((4 * width, model_width), low),
        N.par: ((channels, 128), full),
        N.table: ((2, length, length), low),
        N.filt: ((6, units, length), full),
        N.w_last: ((2, units, width), full),
        N.resid: ((half, model_width), low),
        N.residual_grad: ((half, model_width), full),
        N.residual: ((half, model_width), full),
        N.up_g: ((model_width, model_width), low),
        N.down_g: ((model_width, model_width), low),
        N.down_near: ((half, model_width), full),
        N.down_far: ((half, model_width), low),
        N.extra: ((8, model_width), full),
        N.upb_g: ((8, model_width), full),
        N.freq: ((units, 128), full),
    }
    split = {
        N.proj: (3, width, length),
        N.streams: (3, width, length),
        N.signal: (2, width, length),
        N.factor: (2, width, length),
        N.conv: (width, length),
    }
    placed = {N.w_in: (16, 128), N.w_out: (16, 128), N.w3: (8, 128)}
    rows = pltpu.VMEM((length, model_width), low)
    half_rows = pltpu.VMEM((half, model_width), low)
    wide, thin = pltpu.VMEM((width, length), full), pltpu.VMEM((width, length), low)
    scratch = [
        pltpu.VMEM(placed.get(name, operands[name].shape), operands[name].dtype) for name in FRONT_LOADS
    ]
    scratch += [pltpu.VMEM(split.get(name, shapes[name][0]), shapes[name][1]) for name in FRONT_OUTS]
    scratch += [rows] * 8 + [pltpu.VMEM((length, model_width), full)] + [wide] * 2 + [thin] * 3
    scratch += [half_rows] * 9
    scratch += [
        pltpu.VMEM((4 * width, model_width), low),
        pltpu.VMEM((8, model_width), full),
        pltpu.VMEM((24, width), full),
        pltpu.VMEM((8, 128), full),
        pltpu.SemaphoreType.DMA((len(FRONT_LOADS),)),
        pltpu.SemaphoreType.DMA((len(STORES),)),
        pltpu.SemaphoreType.DMA((len(FRONT_PLAN),)),
        pltpu.SemaphoreType.DMA((len(FRONT_PLAN),)),
    ]
    results = pl.pallas_call(
        operator_front,
        out_shape=tuple(jax.ShapeDtypeStruct(*shapes[name]) for name in FRONT_OUTS),
        in_specs=[pl.BlockSpec(memory_space=pl.ANY)] * len(FRONT_LOADS)
        + [pl.BlockSpec(memory_space=pltpu.SMEM)] * 2,
        out_specs=tuple(pl.BlockSpec(memory_space=pl.ANY) for name in FRONT_OUTS),
        scratch_shapes=scratch,
        compiler_params=pltpu.CompilerParams(
            vmem_limit_bytes=63 * 1024 * 1024, collective_id=1, has_side_effects=True
        ),
        name="operator_front",
    )(*(operands[name] for name in FRONT_LOADS), counts, lengths)
    return dict(zip(FRONT_OUTS, results))


PLAN = (N.resid, N.downy, N.peer_a, N.peer_b, N.y_a, N.y_b, N.chan, N.first) + tuple(
    (name, hop) for name in (N.up, N.down, N.a, N.b, N.chan) for hop in (1, 2, 3)
) + tuple((N.shared, hop) for hop in range(5))
LOADS = (N.resid, N.w_peer, N.w_in, N.w_out, N.streams, N.proj, N.conv, N.par, N.table, N.factor, N.signal, N.normed,
         N.filt, N.w_last, N.up, N.down, N.down_far, N.w_mid, N.feat, N.freq, N.tokens, N.gain, N.rgrad, N.extra, N.upb,
         N.residual, N.down_near, N.down_bias)


def operator_back(dp_step, outs, *refs):
    sizes = len(LOADS)
    source = dict(zip(LOADS, refs[:sizes]))
    counts, lengths = refs[sizes], refs[sizes + 1]
    refs = refs[:sizes] + refs[sizes + 2 :]
    out = dict(zip(outs, refs[sizes : sizes + len(outs)]))
    refs = refs[sizes + len(outs) :]
    held = dict(zip(LOADS, refs[: len(LOADS)]))
    refs = refs[len(LOADS) :]
    (grad, real, imag, pair_a, pair_b, pair_c, pair_d, stack, proj_low, h_grad, first, first_send, first_recv,
     peer_a, peer_b, beside_a, beside_b, send_a, send_b, recv_a, recv_b, sum_a, sum_b, recv_down, sums, chan_peer, chan_recv, chan, chan_hops,
     shared, shared_hops, w_own) = refs[:32]
    hops = dict(zip((N.up, N.down, N.a, N.b), (refs[32 + 5 * i : 37 + 5 * i] for i in range(4))))
    load_sem, send_sem, recv_sem = refs[52:]
    full, low = jnp.float32, jnp.bfloat16

    part = lax.axis_index(TENSOR)
    group = lax.axis_index(DP)
    side = part % 2
    bits = [(group // (dp_step << b)) % 2 for b in range(3)]
    across = {TENSOR: other_of(part, 1)}
    over = {TENSOR: other_of(part, 2)}
    flips = [{DP: other_of(group, dp_step << b)} for b in range(3)]

    def remote(name, src, dst, target):
        index = PLAN.index(name)
        return pltpu.make_async_remote_copy(
            src_ref=src,
            dst_ref=dst,
            send_sem=send_sem.at[index],
            recv_sem=recv_sem.at[index],
            device_id=target,
            device_id_type=pl.DeviceIdType.MESH,
        )

    width, length = grad.shape
    model_width = first.shape[1]
    half_rows = length // 2
    block_rows = model_width // BLOCKS
    mine = pl.ds(pl.multiple_of(side * half_rows, half_rows), half_rows)
    theirs = pl.ds(pl.multiple_of((1 - side) * half_rows, half_rows), half_rows)

    places = dict(held)
    places[N.resid] = held[N.resid].at[mine]
    places[N.w_in] = w_own.at[0 : 3 * width]
    places[N.w_out] = w_own.at[3 * width :]
    loads = {
        name: pltpu.make_async_copy(source[name], places[name], load_sem.at[index])
        for index, name in enumerate(LOADS)
    }
    for name in LOADS:
        loads[name].start()

    barrier = pltpu.get_barrier_semaphore()
    for target in [across, over] + flips:
        pl.semaphore_signal(barrier, inc=1, device_id=target, device_id_type=pl.DeviceIdType.MESH)
    pl.semaphore_wait(barrier, 5)

    resid = held[N.resid]
    resid_copy = remote(N.resid, source[N.resid], resid.at[mine], across)
    resid_copy.start()
    loads[N.resid].wait()
    loads[N.w_peer].wait()
    loads[N.w_in].wait()
    loads[N.w_out].wait()
    resid_copy.wait()

    def spot(index, size):
        return pl.ds(pl.multiple_of(index * size, size), size)

    def order_of(name):
        return PATHS[0] if name in (N.up, N.a, N.peer_a) else PATHS[1]

    def hop_one(name, grads):
        bit = order_of(name)[0]
        src = grads.at[spot(1 - bits[bit], 4 * block_rows)]
        copy = remote((name, 1), src, hops[name][0], flips[bit])
        copy.start()
        return copy

    def hop_two(name, grads, copy):
        recv_one, send_two, keep_two, recv_two, _ = hops[name]
        top, bit, _ = order_of(name)
        copy.wait()
        crossed = {N.a: recv_a, N.b: recv_b}.get(name)
        for keep in (0, 1):
            pick = bits[bit] if keep else 1 - bits[bit]
            total = (
                grads[spot(2 * bits[top] + pick, 2 * block_rows), :].astype(full)
                + recv_one[spot(pick, 2 * block_rows), :].astype(full)
            )
            if crossed is not None:
                total = total + crossed[spot(pick, 2 * block_rows), :].astype(full)
            if keep:
                keep_two[...] = total
            else:
                send_two[...] = total.astype(low)
                copy = remote((name, 2), send_two, recv_two, flips[bit])
                copy.start()
        return copy

    def hop_three(name, copy):
        recv_one, send_two, keep_two, recv_two, recv_three = hops[name]
        bit = order_of(name)[2]
        copy.wait()
        place = spot(1 - bits[bit], block_rows)
        send_two[0:block_rows, :] = (keep_two[place, :] + recv_two[place, :].astype(full)).astype(low)
        copy = remote((name, 3), send_two.at[0:block_rows], recv_three, flips[bit])
        copy.start()
        return copy

    def hop_last(name, copy):
        recv_one, send_two, keep_two, recv_two, recv_three = hops[name]
        copy.wait()
        place = spot(bits[order_of(name)[2]], block_rows)
        return keep_two[place, :] + recv_two[place, :].astype(full) + recv_three[...].astype(full)

    loads[N.up].wait()
    loads[N.down].wait()
    loads[N.down_far].wait()
    copies = {N.up: hop_one(N.up, held[N.up]), N.down: hop_one(N.down, held[N.down])}
    copies[N.downy] = remote(N.downy, held[N.down_far], recv_down, over)
    copies[N.downy].start()

    lanes = lax.broadcasted_iota(jnp.int32, (CHUNK, length), 1)
    par, streams, proj, conv = held[N.par], held[N.streams], held[N.proj], held[N.conv]
    cos, sin = held[N.table].at[0], held[N.table].at[1]
    factor, signal, normed = held[N.factor], held[N.signal], held[N.normed]
    filt = held[N.filt]
    weights = (w_own, held[N.w_peer])

    def half_pass(half, loaded, middle):
        base = half * width
        weight = weights[half]
        own_w = 3 * width

        def at(index):
            return pl.ds(pl.multiple_of(index * CHUNK, CHUNK), CHUNK)

        def far(index):
            return pl.ds(pl.multiple_of(base + index * CHUNK, CHUNK), CHUNK)

        def stream_back(i, index, params, back):
            moved = [shifted(back, -j, lanes) for j in range(3)]
            out = sum(column(params, 3 * j + i) * moved[j] for j in range(3)).astype(low)
            line = proj[i, far(index), :].astype(full)
            start = pl.multiple_of(i * width + index * CHUNK, CHUNK)
            proj_low[pl.ds(start, CHUNK), :] = out
            found = [(3 * j + i, jnp.sum(moved[j] * line, axis=1, keepdims=True)) for j in range(3)]
            found.append((9 + i, jnp.sum(out.astype(full), axis=1, keepdims=True)))
            found.append((12 + i, jnp.sum(back, axis=1, keepdims=True)))
            return found

        grad[...] = dot_nt(weight[own_w:, :], resid[...])
        if not loaded:
            for name in (N.streams, N.proj, N.conv, N.par):
                loads[name].wait()

        def before(index, carry):
            rows = far(index)
            params = par[rows, :]
            gate_out, gate_in, values = streams[0, rows, :], streams[1, rows, :], streams[2, rows, :]
            mixed_grad = grad[at(index), :]
            conv_part = conv[rows, :]
            conv_grad = mixed_grad * gate_out
            grad[at(index), :] = conv_grad
            pair_a[at(index), :] = conv_grad.astype(low)
            pair_b[at(index), :] = (conv_part * gate_out).astype(low)
            found = stream_back(0, index, params, mixed_grad * conv_part)
            found.append((15, jnp.sum(conv_grad * values * gate_in, axis=1, keepdims=True)))
            sums[at(index), :] = pack_columns(found, CHUNK)
            return carry

        lax.fori_loop(0, width // CHUNK, before, 0)
        stack[3 * width :, :] = dot_nn(pair_b[...], resid[...])
        if not loaded:
            loads[N.table].wait()
        real[...] = dot_nn(pair_a[...], cos[...])
        imag[...] = dot_nt(pair_a[...], sin[...])
        if not loaded:
            loads[N.factor].wait()
            loads[N.signal].wait()
        first_lane = lanes == 0
        scale = jnp.where(first_lane, 0.5 / length, 1.0 / length)

        def between(index, carry):
            rows, place = far(index), at(index)
            cos_part, sin_part = real[place, :] * scale, imag[place, :] * scale
            f_cos, f_sin = factor[0, rows, :], factor[1, rows, :]
            f_last = jnp.where(first_lane, f_sin, f_cos)
            f_sin = jnp.where(first_lane, 0.0, f_sin)
            pair_a[place, :] = (cos_part * f_cos + sin_part * f_sin).astype(low)
            pair_b[place, :] = (sin_part * f_last - cos_part * f_sin).astype(low)
            s_cos, s_sin = signal[0, rows, :], signal[1, rows, :]
            s_last = jnp.where(first_lane, s_sin, s_cos)
            s_sin = jnp.where(first_lane, 0.0, s_sin)
            pair_c[place, :] = (cos_part * s_cos + sin_part * s_sin).astype(low)
            pair_d[place, :] = (sin_part * s_last - cos_part * s_sin).astype(low)
            return carry

        lax.fori_loop(0, width // CHUNK, between, 0)
        middle()
        real[...] = dot_nn(pair_a[...], cos[...]) + dot_nn(pair_b[...], sin[...])
        imag[...] = dot_nn(pair_c[...], cos[...]) + dot_nn(pair_d[...], sin[...])

        def after(index, carry):
            rows = far(index)
            params = par[rows, :]
            gate_in, values = streams[1, rows, :], streams[2, rows, :]
            back = real[at(index), :] + grad[at(index), :] * column(params, 15)
            found = stream_back(1, index, params, back * values)
            found += stream_back(2, index, params, back * gate_in)
            sums[at(index), :] = sums[at(index), :] + pack_columns(found, CHUNK)
            window = jnp.exp(-lanes.astype(full) * column(params, 16))
            pair_a[at(index), :] = (imag[at(index), :] * window).astype(low)
            return carry

        lax.fori_loop(0, width // CHUNK, after, 0)
        if not loaded:
            for name in (N.normed, N.filt, N.w_last):
                loads[name].wait()
        stack[: 3 * width, :] = dot_nn(proj_low[...], normed[...])
        target = chan_peer if half == 1 else chan
        target[0:16, :] = jnp.transpose(sums[...])[0:16, :]
        target[16:80, :] = dot_nt(filt[1].astype(low), pair_a[...])
        h_part = dot_nn(held[N.w_last][half].astype(low), pair_a[...])
        if half == 1:
            h_grad[...] = h_part
        else:
            h_grad[...] += h_part

    def turned(store):
        middle = model_width // 2
        for start in range(0, model_width, 128):
            block = jnp.transpose(stack[:, start : start + 128])
            begin = start
            while begin < start + 128:
                size = min(block_rows - begin % block_rows, start + 128 - begin)
                piece = block[begin - start : begin - start + size, :]
                for path, columns in enumerate((piece[:, :middle], piece[:, middle:])):
                    place = path_place(begin, block_rows, PATHS[path])
                    store(path, slice(place, place + size), columns)
                begin += size

    def store_peer(path, rows, values):
        (peer_a, peer_b)[path][rows, :] = values.astype(low)

    def store_own(path, rows, values):
        (sum_a, sum_b)[path][rows, :] = values.astype(low)

    peers = ((N.peer_a, peer_a, beside_a, send_a), (N.peer_b, peer_b, beside_b, send_b))

    def peer_first():
        for name, grads, beside, _ in peers:
            bit = order_of(name)[0]
            src = grads.at[spot(1 - bits[bit], 4 * block_rows)]
            copies[name] = remote(name, src, beside, flips[bit])
            copies[name].start()

    def peer_cross():
        for (name, grads, beside, sent), across_name, crossed in zip(peers, (N.y_a, N.y_b), (recv_a, recv_b)):
            bit = order_of(name)[0]
            copies[name].wait()
            kept = grads[spot(bits[bit], 4 * block_rows), :].astype(full)
            sent[...] = (kept + beside[...].astype(full)).astype(low)
            copies[across_name] = remote(across_name, sent, crossed, over)
            copies[across_name].start()

    def first_part(half):
        for start in range(0, length, 256):
            product = dot_tn(proj_low[:, start : start + 256], weights[half][: 3 * width, :])
            if half == 1:
                first[start : start + 256, :] = product
            else:
                first[start : start + 256, :] += product

    half_pass(1, False, lambda: None)
    turned(store_peer)
    chan_peer[80:88, :] = jnp.zeros((8, width), full)
    peer_first()
    copies[N.chan] = remote(N.chan, chan_peer, chan_recv, over)
    copies[N.chan].start()
    first_part(1)
    for name in (N.up, N.down):
        copies[name] = hop_two(name, held[name], copies[name])

    def last_hops():
        peer_cross()
        for name in (N.up, N.down):
            copies[name] = hop_three(name, copies[name])

    half_pass(0, True, last_hops)
    first_part(0)
    first_send[...] = first[theirs, :].astype(low)
    first_copy = remote(N.first, first_send, first_recv, across)
    first_copy.start()
    turned(store_own)
    copies[N.a] = hop_one(N.a, sum_a)
    copies[N.b] = hop_one(N.b, sum_b)

    copies[N.chan].wait()
    loads[N.upb].wait()
    chan[0:80, :] = chan[0:80, :] + chan_recv[0:80, :]
    chan[80:88, :] = jnp.zeros((8, width), full)
    for index in range(held[N.upb].shape[1] // width):
        chan[80 + index : 81 + index, :] = held[N.upb][0:1, index * width : (index + 1) * width]
    chan_copy = remote((N.chan, 1), chan, chan_hops.at[0], flips[0])
    chan_copy.start()

    for name in (N.w_mid, N.feat, N.freq):
        loads[name].wait()
    freq, w_mid = held[N.freq], held[N.w_mid]
    shared[...] = jnp.zeros_like(shared)
    units = w_mid.shape[0]
    feats = held[N.feat].shape[0]
    slope = h_grad[...] * filt[3]
    q_two = jnp.sum(slope * filt[5], axis=1, keepdims=True)
    slope = slope * column(freq[...], 1)
    b_two = jnp.sum(slope, axis=1, keepdims=True)
    slope_low = slope.astype(low)
    shared[80 : 80 + units, 0:units] = dot_nt(filt[0].astype(low), slope_low)
    slope = dot_nn(w_mid[...].astype(low), slope_low) * filt[2]
    q_one = jnp.sum(slope * filt[4], axis=1, keepdims=True)
    slope = slope * column(freq[...], 0)
    b_one = jnp.sum(slope, axis=1, keepdims=True)
    shared[40 : 40 + feats, 0:units] = dot_nt(held[N.feat][...].astype(low), slope.astype(low))
    vectors = pack_columns([(0, b_one), (1, q_one), (2, b_two), (3, q_two)], units)
    shared[144:152, 0:units] = jnp.transpose(vectors)[0:8, :]

    for name in (N.tokens, N.gain, N.rgrad, N.extra):
        loads[name].wait()
    first_copy.wait()
    gain = held[N.gain][...][None, :]

    def norm_rows(index, carry):
        rows = pl.ds(pl.multiple_of(index * ROWS, ROWS), ROWS)
        own = pl.ds(pl.multiple_of(side * half_rows + index * ROWS, ROWS), ROWS)
        normed_rows, inverse = normed_parts(held[N.tokens][rows, :].astype(full))
        back = first[own, :] + first_recv[rows, :].astype(full)
        grad_rows = norm_rows_back(back, normed_rows, inverse, gain)
        out[N.input_grad][rows, :] = held[N.rgrad][rows, :] + grad_rows
        return (
            carry[0] + jnp.sum(back * normed_rows, axis=0, keepdims=True),
            carry[1] + jnp.sum(back, axis=0, keepdims=True),
        )

    zero = jnp.zeros((1, model_width), full)
    found = lax.fori_loop(0, half_rows // ROWS, norm_rows, (zero, zero))
    extra = held[N.extra]
    vectors = list(found) + [extra[i : i + 1, :] for i in range(4)]
    for index, vector in enumerate(vectors):
        for piece in range(model_width // 128):
            row = index * (model_width // 128) + piece
            shared[row : row + 1, :] = vector[:, piece * 128 : (piece + 1) * 128]

    shared_targets = [across, over] + flips

    def share(hop):
        copy = remote((N.shared, hop), shared, shared_hops.at[hop], shared_targets[hop])
        copy.start()
        return copy

    def shared_next(hop, copy):
        copy.wait()
        shared[...] = shared[...] + shared_hops[hop]
        return share(hop + 1) if hop < 4 else None

    def chan_next(hop, copy):
        copy.wait()
        chan[...] = chan[...] + chan_hops[hop]
        if hop == 2:
            return None
        copy = remote((N.chan, hop + 2), chan, chan_hops.at[hop + 1], flips[hop + 1])
        copy.start()
        return copy

    shared_copy = share(0)
    copies[N.y_a].wait()
    copies[N.y_b].wait()
    for name, grads in ((N.a, sum_a), (N.b, sum_b)):
        copies[name] = hop_two(name, grads, copies[name])
    shared_copy = shared_next(0, shared_copy)
    chan_copy = chan_next(0, chan_copy)

    for name in (N.residual, N.down_near, N.down_bias):
        loads[name].wait()
    copies[N.downy].wait()
    slot = part * half_rows // length
    mask_rows = jnp.where(slot < counts[0], lengths[0, slot], 0) - part * half_rows % length
    down_bias = held[N.down_bias][...][None, :]

    def result_rows(index, carry):
        rows = pl.ds(pl.multiple_of(index * ROWS, ROWS), ROWS)
        total = held[N.residual][rows, :] + held[N.down_near][rows, :] + recv_down[rows, :].astype(full)
        place = lax.broadcasted_iota(jnp.int32, (ROWS, model_width), 0) + index * ROWS
        out[N.activations][rows, :] = jnp.where(place < mask_rows, total + down_bias, 0.0).astype(low)
        return carry

    lax.fori_loop(0, half_rows // ROWS, result_rows, 0)
    shared_copy = shared_next(1, shared_copy)
    for name in (N.a, N.b):
        copies[name] = hop_three(name, copies[name])
    chan_copy = chan_next(1, chan_copy)
    shared_copy = shared_next(2, shared_copy)
    up_part = hop_last(N.up, copies[N.up])
    out[N.up][...] = up_part
    down_part = hop_last(N.down, copies[N.down])
    out[N.down][...] = down_part
    chan_next(2, chan_copy)
    shared_copy = shared_next(3, shared_copy)
    for name in (N.a, N.b):
        out[name][...] = hop_last(name, copies[name])
    shared_next(4, shared_copy)
    out[N.shared][...] = shared[...]
    out[N.chan][...] = chan[...]


PASSED = (N.activations, N.input_grad, N.up)


def lay_out(group_units, *refs):
    sources = dict(zip(RAW, refs[: len(RAW)]))
    outs = dict(zip(RESULTS, refs[len(RAW) : len(RAW) + len(RESULTS)]))
    held = dict(zip(RAW, refs[len(RAW) + len(RESULTS) : -1]))
    sem = refs[-1]
    group = lax.axis_index(DP)
    loads, passes = {}, []
    for index, name in enumerate(RAW):
        if name in PASSED:
            passes.append(pltpu.make_async_copy(sources[name], outs[name], sem.at[index]))
            passes[-1].start()
        else:
            loads[name] = pltpu.make_async_copy(sources[name], held[name], sem.at[index])
            loads[name].start()
    for copy in loads.values():
        copy.wait()
    part_a, part_b = jnp.transpose(held[N.a][...]), jnp.transpose(held[N.b][...])
    width = outs[N.out].shape[0]
    outs[N.in_w][0] = part_a[0:width, :]
    outs[N.in_w][1] = part_a[width:, :]
    outs[N.in_w][2] = part_b[0:width, :]
    outs[N.out][...] = part_b[width:, :]
    outs[N.down][...] = jnp.transpose(held[N.down][...])
    shared, chan = held[N.shared], held[N.chan]
    model_width = outs[N.up].shape[1]
    units = outs[N.w2].shape[0]
    pieces = model_width // 128
    for index, name in enumerate(WIDES):
        row = index * pieces
        lines = [shared[row + piece : row + piece + 1, :] for piece in range(pieces)]
        outs[name][...] = jnp.concatenate(lines, axis=1).reshape(model_width)
    outs[N.w1][...] = shared[40 : 40 + outs[N.w1].shape[0], 0:units]
    outs[N.w2][...] = shared[80 : 80 + units, 0:units]
    for index, name in enumerate(VECTORS):
        outs[name][...] = shared[144 + index : 145 + index, 0:units].reshape(units)
    outs[N.conv_w][...] = chan[0:9, :].reshape(3, 3, width)
    outs[N.in_b][...] = chan[9:12, :]
    outs[N.conv_b][...] = chan[12:15, :]
    outs[N.f_bias][...] = chan[15:16, :].reshape(width)
    lines = [chan[80 + index : 81 + index, :] for index in range(model_width // width)]
    outs[N.up_b][...] = jnp.concatenate(lines, axis=1).reshape(model_width)
    outs[N.w3][...] = chan[pl.ds(pl.multiple_of(16 + group * group_units, 8), group_units), :]
    for copy in passes:
        copy.wait()


def call_lay_out(raw, inputs_count, units, width):
    full, low = jnp.float32, jnp.bfloat16
    rows, model_width = raw[N.input_grad].shape
    block = raw[N.up].shape[0]
    shapes = {name: raw[name].shape for name in PASSED}
    shapes.update({name: (model_width,) for name in WIDES + (N.up_b,)})
    shapes.update({name: (units,) for name in VECTORS})
    shapes.update(
        {
            N.in_w: (3, width, block),
            N.out: (width, block),
            N.down: (model_width, block),
            N.w1: (inputs_count, units),
            N.w2: (units, units),
            N.w3: (units // BLOCKS, width),
            N.conv_w: (3, 3, width),
            N.in_b: (3, width),
            N.conv_b: (3, width),
            N.f_bias: (width,),
        }
    )
    results = pl.pallas_call(
        functools.partial(lay_out, units // BLOCKS),
        out_shape=tuple(
            jax.ShapeDtypeStruct(shapes[name], low if name == N.activations else full) for name in RESULTS
        ),
        in_specs=[pl.BlockSpec(memory_space=pl.ANY)] * len(RAW),
        out_specs=tuple(pl.BlockSpec(memory_space=pltpu.VMEM) for name in RESULTS),
        scratch_shapes=[
            pltpu.VMEM((8, 128) if name in PASSED else raw[name].shape, full) for name in RAW
        ]
        + [pltpu.SemaphoreType.DMA((len(RAW),))],
        name="lay_out",
    )(*(raw[name] for name in RAW))
    return results


def call_operator_back(operands, counts, lengths, width, length, model_width, dp_count):
    full, low = jnp.float32, jnp.bfloat16
    units = operands[N.w_mid].shape[0]
    half_rows = length // 2
    block = model_width // BLOCKS
    thin_grads = pltpu.VMEM((model_width, model_width // 2), low)
    part_grads = pltpu.VMEM((model_width // 2, model_width // 2), low)
    low_rows = pltpu.VMEM((half_rows, model_width), low)
    held = []
    for name in LOADS:
        shape = operands[name].shape
        if name == N.resid:
            shape = (length, model_width)
        elif name in (N.w_in, N.w_out):
            shape = (16, 128)
        held.append(pltpu.VMEM(shape, operands[name].dtype))
    wide, thin = pltpu.VMEM((width, length), full), pltpu.VMEM((width, length), low)
    chan = pltpu.VMEM((88, width), full)
    shared = pltpu.VMEM((152, 128), full)
    scratch = held + [wide] * 3 + [thin] * 4
    scratch += [
        pltpu.VMEM((4 * width, model_width), full),
        pltpu.VMEM((3 * width, length), low),
        pltpu.VMEM((units, length), full),
        pltpu.VMEM((length, model_width), full),
        low_rows,
        low_rows,
        thin_grads,
        thin_grads,
        part_grads,
        part_grads,
        part_grads,
        part_grads,
        part_grads,
        part_grads,
        thin_grads,
        thin_grads,
        low_rows,
        pltpu.VMEM((width, 128), full),
        chan,
        chan,
        chan,
        pltpu.VMEM((3, 88, width), full),
        shared,
        pltpu.VMEM((5, 152, 128), full),
        pltpu.VMEM((4 * width, model_width), low),
    ]
    for columns in (model_width, model_width, model_width // 2, model_width // 2):
        scratch += [
            pltpu.VMEM((4 * block, columns), low),
            pltpu.VMEM((2 * block, columns), low),
            pltpu.VMEM((2 * block, columns), full),
            pltpu.VMEM((2 * block, columns), low),
            pltpu.VMEM((block, columns), low),
        ]
    scratch += [
        pltpu.SemaphoreType.DMA((len(LOADS),)),
        pltpu.SemaphoreType.DMA((len(PLAN),)),
        pltpu.SemaphoreType.DMA((len(PLAN),)),
    ]
    shapes = {N.activations: (half_rows, model_width), N.input_grad: (half_rows, model_width)}
    shapes.update({N.up: (block, model_width), N.down: (block, model_width)})
    shapes.update({N.a: (block, model_width // 2), N.b: (block, model_width // 2)})
    shapes.update({N.shared: (152, 128), N.chan: (88, width)})
    outs = tuple(shapes)
    results = pl.pallas_call(
        functools.partial(operator_back, dp_count // BLOCKS, outs),
        out_shape=tuple(
            jax.ShapeDtypeStruct(shapes[name], low if name == N.activations else full) for name in outs
        ),
        in_specs=[pl.BlockSpec(memory_space=pl.ANY)] * len(LOADS)
        + [pl.BlockSpec(memory_space=pltpu.SMEM)] * 2,
        out_specs=tuple(pl.BlockSpec(memory_space=pltpu.VMEM) for out in outs),
        scratch_shapes=scratch,
        compiler_params=pltpu.CompilerParams(
            vmem_limit_bytes=63 * 1024 * 1024, collective_id=0, has_side_effects=True
        ),
        cost_estimate=pl.CostEstimate(
            flops=4 * width * length * (10 * length + 8 * model_width),
            bytes_accessed=40 * 1024 * 1024,
            transcendentals=0,
        ),
        name="operator_back",
    )(*(operands[name] for name in LOADS), counts, lengths)
    return dict(zip(outs, results))


def local(
    tokens,
    seq_counts,
    seq_lengths,
    norm1_gain,
    norm1_bias,
    in_weight,
    in_bias,
    conv_weight,
    conv_bias,
    filter_w1,
    filter_b1,
    filter_freq1,
    filter_w2,
    filter_b2,
    filter_freq2,
    filter_w3,
    filter_bias,
    out_weight,
    out_bias,
    norm2_gain,
    norm2_bias,
    up_weight,
    up_bias,
    down_weight,
    down_bias,
    cotangent,
):
    low = jnp.bfloat16
    full = jnp.float32
    tensor_count = lax.axis_size(TENSOR)
    dp_count = lax.axis_size(DP)
    row_share, model_width = tokens.shape
    width = in_weight.shape[1]
    slot_count = seq_lengths.shape[1]
    length = row_share * tensor_count // slot_count
    part = lax.axis_index(TENSOR)
    group = lax.axis_index(DP)

    inputs_count = filter_w1.shape[0]
    units = filter_w2.shape[0]
    features = jnp.asarray(positions(length, (inputs_count - 1) // 2))
    flat_in = in_weight.reshape(3 * width, model_width)
    front = call_operator_front(
        {
            N.w_in: flat_in,
            N.w_out: out_weight,
            N.tokens: tokens,
            N.g1: norm1_gain,
            N.b1: norm1_bias,
            N.cw: conv_weight,
            N.ib: in_bias,
            N.cb: conv_bias,
            N.fb: filter_bias,
            N.w3: filter_w3,
            N.cot: cotangent,
            N.seeds: jnp.asarray(turn_seeds(length)),
            N.feat: features,
            N.fw1: filter_w1,
            N.fw2: filter_w2,
            N.fb1: filter_b1,
            N.ff1: filter_freq1,
            N.fb2: filter_b2,
            N.ff2: filter_freq2,
            N.ob: out_bias,
            N.g2: norm2_gain,
            N.b2: norm2_bias,
            N.upb: up_bias,
            N.up: up_weight,
            N.down: down_weight,
        },
        seq_counts,
        seq_lengths,
        width,
        length,
        model_width,
    )
    back = call_operator_back(
        {
            N.resid: front[N.resid],
            N.w_peer: front[N.w_peer],
            N.w_in: flat_in,
            N.w_out: out_weight,
            N.streams: front[N.streams],
            N.proj: front[N.proj],
            N.conv: front[N.conv],
            N.par: front[N.par],
            N.table: front[N.table],
            N.factor: front[N.factor],
            N.signal: front[N.signal],
            N.normed: front[N.normed],
            N.filt: front[N.filt],
            N.w_last: front[N.w_last],
            N.up: front[N.up_g],
            N.down: front[N.down_g],
            N.down_far: front[N.down_far],
            N.w_mid: filter_w2,
            N.feat: features,
            N.freq: front[N.freq],
            N.tokens: tokens,
            N.gain: norm1_gain,
            N.rgrad: front[N.residual_grad],
            N.extra: front[N.extra],
            N.upb: front[N.upb_g],
            N.residual: front[N.residual],
            N.down_near: front[N.down_near],
            N.down_bias: down_bias,
        },
        seq_counts,
        seq_lengths,
        width,
        length,
        model_width,
        dp_count,
    )
    if dp_count == BLOCKS:
        return tuple(call_lay_out(back, inputs_count, units, width))

    rest = dp_count.bit_length() - BLOCKS.bit_length()

    def flips(bit_index):
        return [(i, i ^ (1 << bit_index)) for i in range(dp_count)]

    def rest_scatter(grad):
        for bit_index in range(rest):
            bit = (group >> bit_index) & 1
            kept = grad.reshape(1 << (rest - 1 - bit_index), 2, model_width // dp_count, -1)
            mine = lax.dynamic_index_in_dim(kept, bit, 1, keepdims=False)
            sent = lax.dynamic_index_in_dim(kept, 1 - bit, 1, keepdims=False)
            grad = mine + lax.ppermute(sent.astype(low), DP, flips(bit_index)).astype(full)
        return grad.reshape(model_width // dp_count, -1)

    def rest_sum(values):
        for bit_index in range(rest):
            values = values + lax.ppermute(values, DP, flips(bit_index))
        return values

    operator_grads = rest_scatter(jnp.concatenate([back[N.a], back[N.b]], axis=1))
    shared, chan = rest_sum(back[N.shared]), rest_sum(back[N.chan])
    wide = shared[: 6 * (model_width // 128)].reshape(6, model_width)
    share = units // dp_count
    grad_in = operator_grads[:, : 3 * width].reshape(-1, 3, width)
    return (
        back[N.activations],
        back[N.input_grad],
        wide[0],
        wide[1],
        jnp.transpose(grad_in, (1, 2, 0)),
        chan[9:12],
        chan[0:9].reshape(3, 3, width),
        chan[12:15],
        shared[40 : 40 + inputs_count, :units],
        shared[144, :units],
        shared[145, :units],
        shared[80 : 80 + units, :units],
        shared[146, :units],
        shared[147, :units],
        lax.dynamic_slice_in_dim(chan[16 : 16 + units], group * share, share, 0),
        chan[15],
        jnp.transpose(operator_grads[:, 3 * width :]),
        wide[2],
        wide[3],
        wide[4],
        rest_scatter(back[N.up]),
        chan[80 : 80 + model_width // width].reshape(-1),
        jnp.transpose(rest_scatter(back[N.down])),
        wide[5],
    )


def solution(mesh):
    in_specs = (
        P((DP, TENSOR), None),
        P(DP),
        P(DP, None),
        P(),
        P(),
        P(None, TENSOR, None),
        P(None, TENSOR),
        P(None, None, TENSOR),
        P(None, TENSOR),
        P(),
        P(),
        P(),
        P(),
        P(),
        P(),
        P(None, TENSOR),
        P(TENSOR),
        P(TENSOR, None),
        P(),
        P(),
        P(),
        P(None, TENSOR),
        P(TENSOR),
        P(TENSOR, None),
        P(),
        P((DP, TENSOR), None),
    )
    out_specs = (
        P((DP, TENSOR), None),
        P((DP, TENSOR), None),
        P(),
        P(),
        P(None, TENSOR, DP),
        P(None, TENSOR),
        P(None, None, TENSOR),
        P(None, TENSOR),
        P(),
        P(),
        P(),
        P(),
        P(),
        P(),
        P(DP, TENSOR),
        P(TENSOR),
        P(TENSOR, DP),
        P(),
        P(),
        P(),
        P(DP, TENSOR),
        P(TENSOR),
        P(TENSOR, DP),
        P(),
    )
    return jax.shard_map(local, mesh=mesh, in_specs=in_specs, out_specs=out_specs, check_vma=False)
```

```python
import functools
import math

import jax
import jax.numpy as jnp
import numpy as np
from jax import lax
from jax.experimental import pallas as pl
from jax.experimental.pallas import tpu as pltpu
from jax.sharding import PartitionSpec as P

highest = lax.Precision.HIGHEST
norm_epsilon = 1e-05
slow_rate = math.log(100.0) / 1.5
fast_rate = math.log(100.0) / 0.3


def turn_seeds(length):
    levels = np.array(list(range(8)) + [1 << i for i in range(3, length.bit_length() - 1)])
    angle = (levels[:, None] * np.arange(length) % (2 * length)) * (math.pi / length)
    return np.stack([np.cos(angle), np.sin(angle)]).astype(np.float32)


def dot_nt(left, right):
    return lax.dot_general(
        left, right, (((1,), (1,)), ((), ())), preferred_element_type=jnp.float32
    )


def dot_nn(left, right):
    return jnp.dot(left, right, preferred_element_type=jnp.float32)


def dot_tn(left, right):
    return lax.dot_general(
        left, right, (((0,), (0,)), ((), ())), preferred_element_type=jnp.float32
    )


def shifted(values, shift, lanes):
    length = values.shape[1]
    if shift == 0:
        return values
    if shift > 0:
        return jnp.where(lanes >= shift, pltpu.roll(values, shift, 1), 0.0)
    return jnp.where(lanes < length + shift, pltpu.roll(values, length + shift, 1), 0.0)


def column(params, index):
    return params[:, index : index + 1]


def pack_columns(columns, rows):
    lanes = lax.broadcasted_iota(jnp.int32, (rows, 128), 1)
    packed = jnp.zeros((rows, 128), jnp.float32)
    for index, values in columns:
        packed = jnp.where(lanes == index, values, packed)
    return packed


BLOCKS = 8
CHUNK = 64
ROWS = 128


def other_of(index, step):
    return index + step * (1 - 2 * ((index // step) % 2))


TENSOR = "tensor"
DP = "dp"


class N:
    (
        a, activations, b, b1, b2, back, branch, cb, chan, conv, conv_b, conv_w, cot, cotf, cotn,
        coty, cw, down, down_b, down_bias, down_far, down_g, down_near, down_r, downf, downn, downy,
        extra, f_bias, factor, farx, fb, fb1, fb2, feat, ff1, ff2, filt, first, freq, fw1, fw2, g1,
        g2, gain, gain1, gain2, ib, in_b, in_w, input_grad, midf, midn, midy, near, norm, normed,
        ob, out, out_b, par, peer_a, peer_b, proj, resid, residual, residual_grad, rgrad, seeds,
        shared, shift1, shift2, signal, streams, table, tokens, up, up_b, up_g, up_r, upb, upb_g,
        w1, w2, w3, w_in, w_last, w_mid, w_out, w_peer, wx, wy, y_a, y_b,
    ) = range(94)


FRONT_PLAN = (N.up, N.down, (N.wy, 0), (N.wy, 1), (N.wy, 2), (N.wx, 0), (N.wx, 1), (N.wx, 2), N.norm, N.par, N.w3, N.cotn, N.coty, N.cotf, N.branch, N.midn, (N.midy, 0), (N.midy, 1),
              (N.midf, 0), (N.midf, 1), N.near, (N.farx, 0), (N.farx, 1), (N.back, 0), (N.back, 1), N.downn, N.downf)
FRONT_LOADS = (N.w_in, N.w_out, N.tokens, N.g1, N.b1, N.cw, N.ib, N.cb, N.fb, N.w3, N.cot, N.seeds, N.fw1,
               N.fw2, N.fb1, N.ff1, N.fb2, N.ff2, N.ob, N.g2, N.b2, N.upb, N.up, N.down)
FRONT_OUTS = (N.proj, N.streams, N.signal, N.factor, N.conv, N.normed, N.w_peer, N.par, N.table, N.filt, N.w_last,
              N.resid, N.residual_grad, N.residual, N.up_g, N.down_g, N.up_r, N.down_r, N.down_near, N.down_far, N.extra, N.upb_g, N.freq, N.feat)


def gelu_parts(values):
    cdf = 0.5 * (1.0 + lax.erf(values * (1.0 / math.sqrt(2.0))))
    density = jnp.exp(-0.5 * values * values) * (1.0 / math.sqrt(2.0 * math.pi))
    return (values * cdf, cdf + values * density)


def normed_parts(values):
    centred = values - jnp.mean(values, axis=-1, keepdims=True)
    inverse = lax.rsqrt(jnp.mean(centred * centred, axis=-1, keepdims=True) + norm_epsilon)
    return (centred * inverse, inverse)


def norm_rows_back(back, normed, inverse, gain):
    scaled = back * gain
    return inverse * (
        scaled
        - jnp.mean(scaled, axis=-1, keepdims=True)
        - normed * jnp.mean(scaled * normed, axis=-1, keepdims=True)
    )


def path_place(row, block_rows, order):
    index, offset = row // block_rows, row % block_rows
    bits = [(index >> b) & 1 for b in range(3)]
    return (bits[order[0]] * 4 + bits[order[1]] * 2 + bits[order[2]]) * block_rows + offset


def store_rows(ref, start, values, block_rows, order):
    stop, begin = start + values.shape[0], start
    while begin < stop:
        size = min(block_rows - begin % block_rows, stop - begin)
        place = path_place(begin, block_rows, order)
        ref[place : place + size, :] = values[begin - start : begin - start + size, :]
        begin += size


HALVES = (N.proj, N.streams, N.signal, N.factor, N.conv)
STORES = tuple((name, half) for name in HALVES for half in (0, 1)) + FRONT_OUTS[5:]
WIDES = (N.gain1, N.shift1, N.out_b, N.gain2, N.shift2, N.down_b)
VECTORS = (N.fb1, N.ff1, N.fb2, N.ff2)
RAW = (N.activations, N.input_grad, N.up, N.down, N.a, N.b, N.shared, N.chan)
RESULTS = (N.activations, N.input_grad, N.gain1, N.shift1, N.in_w, N.in_b, N.conv_w, N.conv_b, N.w1, N.fb1, N.ff1, N.w2,
           N.fb2, N.ff2, N.w3, N.f_bias, N.out, N.out_b, N.gain2, N.shift2, N.up, N.up_b, N.down, N.down_b)
PATHS = ((0, 1, 2), (1, 0, 2))


def operator_front(dp_step, *refs):
    full, low = jnp.float32, jnp.bfloat16
    n, m = len(FRONT_LOADS), len(FRONT_OUTS)
    source = dict(zip(FRONT_LOADS, refs[:n]))
    counts, lengths = refs[n], refs[n + 1]
    refs = refs[:n] + refs[n + 2 :]
    target = dict(zip(FRONT_OUTS, refs[n : n + m]))
    held = dict(zip(FRONT_LOADS, refs[n + m : 2 * n + m]))
    made = dict(zip(FRONT_OUTS, refs[2 * n + m : 2 * n + 2 * m]))
    (mid_near, mid_far, cot_near, cot_far, hid_near, hid_far, pg_near, pg_far, acc, inner, real,
     pair_a, pair_b, pair_c, send_row, recv_branch, recv_near, send_far, recv_far, send_back, recv_back,
     recv_down_near, recv_down_far, w_own, norms, lines, fcol, low_turns, high_turns, load_sem, store_sem, send_sem, recv_sem,
     ) = refs[2 * n + 2 * m :]

    part = lax.axis_index(TENSOR)
    group = lax.axis_index(DP)
    side = part % 2
    across = {TENSOR: other_of(part, 1)}
    over = {TENSOR: other_of(part, 2)}
    beside = {DP: other_of(group, 1)}
    bits = [(group // (dp_step << b)) % 2 for b in range(3)]
    flips = [{DP: other_of(group, dp_step << b)} for b in range(2)]
    greeted = [across, over] + flips + ([beside] if dp_step > 1 else [])
    width = inner.shape[0]
    length, model_width = acc.shape
    half = length // 2
    tile = half // 2
    mine = pl.ds(pl.multiple_of(side * half, half), half)
    theirs = pl.ds(pl.multiple_of((1 - side) * half, half), half)

    def mine_at(start, size):
        return pl.ds(pl.multiple_of(side * half + start, 16), size)

    def theirs_at(start, size):
        return pl.ds(pl.multiple_of((1 - side) * half + start, 16), size)

    def remote(name, src, dst, to):
        index = FRONT_PLAN.index(name)
        copy = pltpu.make_async_remote_copy(
            src_ref=src,
            dst_ref=dst,
            send_sem=send_sem.at[index],
            recv_sem=recv_sem.at[index],
            device_id=to,
            device_id_type=pl.DeviceIdType.MESH,
        )
        copy.start()
        return copy

    loads = {}
    for index, name in enumerate(FRONT_LOADS):
        place = held[name]
        if name == N.w_in:
            place = w_own.at[0 : 3 * width]
        elif name == N.w_out:
            place = w_own.at[3 * width :]
        elif name == N.w3:
            place = made[N.w_last].at[0]
        loads[name] = pltpu.make_async_copy(source[name], place, load_sem.at[index])
        loads[name].start()
    stores = {}

    def put(name, src, dst):
        stores[name] = pltpu.make_async_copy(src, dst, store_sem.at[STORES.index(name)])
        stores[name].start()

    barrier = pltpu.get_barrier_semaphore()
    for to in greeted:
        pl.semaphore_signal(barrier, inc=1, device_id=to, device_id_type=pl.DeviceIdType.MESH)
    pl.semaphore_wait(barrier, len(greeted))

    normed, w_peer, par = made[N.normed], made[N.w_peer], made[N.par]
    loads[N.w_in].wait()
    loads[N.w_out].wait()
    pieces = 3
    share = 4 * width // (2 * pieces)
    copies = {}

    def weight_rows(piece):
        return pl.ds(pl.multiple_of((2 * piece + group % 2) * share, 16), share)

    for piece in range(pieces):
        rows = weight_rows(piece)
        copies[N.wy, piece] = remote((N.wy, piece), w_own.at[rows], w_peer.at[rows], over)

    def pass_on(piece):
        copies[N.wy, piece].wait()
        rows = weight_rows(piece)
        copies[N.wx, piece] = remote((N.wx, piece), w_peer.at[rows], w_peer.at[rows], beside)

    for name in (N.tokens, N.g1, N.b1, N.ob, N.g2, N.b2, N.upb):
        loads[name].wait()
    for index, name in enumerate((N.g1, N.b1, N.ob, N.g2, N.b2, N.upb)):
        norms[index : index + 1, :] = held[name][...][None, :]

    def norm_one(index, carry):
        rows = pl.ds(pl.multiple_of(index * ROWS, ROWS), ROWS)
        values = normed_parts(held[N.tokens][rows, :].astype(full))[0]
        normed[mine_at(index * ROWS, ROWS), :] = (values * norms[0:1, :] + norms[1:2, :]).astype(low)
        return carry

    lax.fori_loop(0, half // ROWS, norm_one, 0)
    copies[N.norm] = remote(N.norm, normed.at[mine], normed.at[mine], across)

    for name in (N.cw, N.ib, N.cb, N.fb, N.w3):
        loads[name].wait()
    lines[...] = jnp.zeros_like(lines)
    lines[0:9, :] = held[N.cw][...].reshape(9, width)
    lines[9:12, :] = held[N.ib][...]
    lines[12:15, :] = held[N.cb][...]
    lines[15:16, :] = held[N.fb][...][None, :]
    channel = (part * width + lax.broadcasted_iota(jnp.int32, (1, width), 1)).astype(full)
    channels = 4 * width
    lines[16:17, :] = (slow_rate + (fast_rate - slow_rate) / (channels - 1) * channel) * (1.0 / (length - 1))
    par[0:width, 0:24] = jnp.transpose(lines[...])
    copies[N.par] = remote(N.par, par.at[0:width], par.at[width:], over)
    copies[N.w3] = remote(N.w3, made[N.w_last].at[0], made[N.w_last].at[1], over)

    loads[N.cot].wait()
    slot = part * half // length
    mask_rows = jnp.where(slot < counts[0], lengths[0, slot], 0) - part * half % length

    def mask_cot(index, carry):
        rows = pl.ds(pl.multiple_of(index * ROWS, ROWS), ROWS)
        place = lax.broadcasted_iota(jnp.int32, (ROWS, model_width), 0) + index * ROWS
        values = held[N.cot][rows, :]
        cot_near[mine_at(index * ROWS, ROWS), :] = jnp.where(
            place < mask_rows, values.astype(full), 0.0
        ).astype(low)
        return carry

    lax.fori_loop(0, half // ROWS, mask_cot, 0)
    copies[N.coty] = remote(N.coty, cot_near.at[mine], cot_far.at[mine], over)

    loads[N.seeds].wait()
    seeds, table = held[N.seeds], made[N.table]
    lows = low_turns.shape[1]

    def turn_by(turns, start, row):
        cos_row, sin_row = seeds[0, row : row + 1, :], seeds[1, row : row + 1, :]
        cos_part, sin_part = turns[0, 0:start, :], turns[1, 0:start, :]
        turns[0, start : 2 * start, :] = cos_part * cos_row - sin_part * sin_row
        turns[1, start : 2 * start, :] = sin_part * cos_row + cos_part * sin_row

    low_turns[:, 0:8, :] = seeds[:, 0:8, :]
    high_turns[:, 0:1, :] = seeds[:, 0:1, :]
    start, row = 8, 8
    while start < lows:
        turn_by(low_turns, start, row)
        start, row = 2 * start, row + 1
    start = 1
    while start < length // lows:
        turn_by(high_turns, start, row)
        start, row = 2 * start, row + 1
    feat = made[N.feat]
    bands = (feat.shape[0] - 1) // 2
    feat[0:1, :] = lax.broadcasted_iota(jnp.int32, (1, length), 1).astype(full) * (1.0 / (length - 1))
    for band in range(1, bands + 1):
        turns, index = (low_turns, 2 * band) if 2 * band < lows else (high_turns, 2 * band // lows)
        feat[band : band + 1, :] = turns[0, index : index + 1, :]
        feat[bands + band : bands + band + 1, :] = -turns[1, index : index + 1, :]
    put(N.feat, feat, target[N.feat])
    for high in range(length // lows):
        cos_high, sin_high = high_turns[0, high : high + 1, :], high_turns[1, high : high + 1, :]
        cos_low, sin_low = low_turns[0], low_turns[1]
        rows = slice(high * lows, (high + 1) * lows)
        table[0, rows, :] = (cos_high * cos_low - sin_high * sin_low).astype(low)
        sines = sin_high * cos_low + cos_high * sin_low
        if high == 0:
            place = lax.broadcasted_iota(jnp.int32, sines.shape, 1)
            first = lax.broadcasted_iota(jnp.int32, sines.shape, 0) == 0
            sines = jnp.where(first, (1 - 2 * (place % 2)).astype(full), sines)
        table[1, rows, :] = sines.astype(low)
    put(N.table, table, target[N.table])
    pass_on(0)
    cos, sin = table.at[0], table.at[1]

    for name in (N.fw1, N.fw2, N.fb1, N.ff1, N.fb2, N.ff2):
        loads[name].wait()

    def exact_tn(left, right):
        return lax.dot_general(
            left, right, (((0,), (0,)), ((), ())), precision=highest, preferred_element_type=full
        )

    filt = made[N.filt]
    units = held[N.fw2].shape[0]
    fcol[...] = jnp.zeros_like(fcol)
    for index, name in enumerate((N.ff1, N.ff2, N.fb1, N.fb2)):
        fcol[index : index + 1, 0:units] = held[name][...][None, :]
    freq = made[N.freq]
    freq[...] = jnp.zeros_like(freq)
    freq[:, 0:8] = jnp.transpose(fcol[...])[0:units, :]
    fcol = freq[...]
    put(N.freq, freq, target[N.freq])
    sum_one = exact_tn(held[N.fw1][...], feat[...]) + column(fcol, 2)
    angle = column(fcol, 0) * sum_one
    filt[0] = jnp.sin(angle)
    filt[2] = jnp.cos(angle)
    filt[4] = sum_one
    sum_two = exact_tn(held[N.fw2][...], filt[0]) + column(fcol, 3)
    angle = column(fcol, 1) * sum_two
    filt[1] = jnp.sin(angle)
    filt[3] = jnp.cos(angle)
    filt[5] = sum_two
    put(N.filt, filt, target[N.filt])
    pass_on(1)

    lanes = lax.broadcasted_iota(jnp.int32, (CHUNK, length), 1)
    first_lane = lanes == 0
    scale = jnp.where(first_lane, 0.5 / length, 1.0 / length)
    proj, signal, factor, conv = made[N.proj], made[N.signal], made[N.factor], made[N.conv]
    streams = made[N.streams]

    def forward(side_index, weight):
        base = side_index * width
        span = slice(base, base + width)

        def keep(name):
            place = target[name].at[span] if name == N.conv else target[name].at[:, span]
            put((name, side_index), made[name], place)

        def free(*names):
            if side_index == 1:
                for name in names:
                    stores.pop((name, 0)).wait()

        real[...] = exact_tn(made[N.w_last][side_index], filt[1])

        def windowed(index, carry):
            rows = pl.ds(pl.multiple_of(index * CHUNK, CHUNK), CHUNK)
            params = par[pl.ds(pl.multiple_of(base + index * CHUNK, CHUNK), CHUNK), :]
            pair_a[rows, :] = (
                real[rows, :] * jnp.exp(-lanes.astype(full) * column(params, 16))
            ).astype(low)
            return carry

        lax.fori_loop(0, width // CHUNK, windowed, 0)
        free(N.factor)
        factor[0] = dot_nn(pair_a[...], cos[...])
        factor[1] = dot_nt(pair_a[...], sin[...])
        keep(N.factor)
        if side_index == 0:
            pass_on(2)
        free(N.streams, N.proj)
        for i in range(3):
            streams[i] = dot_nt(weight[i * width : (i + 1) * width, :], normed[...]) + column(
                par[base : base + width, :], 9 + i
            )

        def mixing(index, carry):
            rows = pl.ds(pl.multiple_of(index * CHUNK, CHUNK), CHUNK)
            params = par[pl.ds(pl.multiple_of(base + index * CHUNK, CHUNK), CHUNK), :]

            def stream(i):
                line = streams[i, rows, :]
                proj[i, rows, :] = line.astype(low)
                total = column(params, 12 + i) + sum(
                    column(params, 3 * j + i) * shifted(line, j, lanes) for j in range(3)
                )
                streams[i, rows, :] = total
                return total

            stream(0)
            mixed_in = stream(1) * stream(2)
            inner[rows, :] = mixed_in
            pair_a[rows, :] = mixed_in.astype(low)
            return carry

        lax.fori_loop(0, width // CHUNK, mixing, 0)
        keep(N.streams)
        keep(N.proj)
        free(N.signal)
        signal[0] = dot_nn(pair_a[...], cos[...])
        signal[1] = dot_nt(pair_a[...], sin[...])
        keep(N.signal)

        def product(index, carry):
            rows = pl.ds(pl.multiple_of(index * CHUNK, CHUNK), CHUNK)
            s_cos, s_sin = signal[0, rows, :] * scale, signal[1, rows, :] * scale
            f_cos, f_sin = factor[0, rows, :], factor[1, rows, :]
            f_last = jnp.where(first_lane, f_sin, f_cos)
            f_sin = jnp.where(first_lane, 0.0, f_sin)
            pair_a[rows, :] = (s_cos * f_cos - s_sin * f_sin).astype(low)
            pair_b[rows, :] = (s_cos * f_sin + s_sin * f_last).astype(low)
            return carry

        lax.fori_loop(0, width // CHUNK, product, 0)
        real[...] = dot_nn(pair_a[...], cos[...])
        real[...] += dot_nn(pair_b[...], sin[...])

        free(N.conv)

        def gating(index, carry):
            rows = pl.ds(pl.multiple_of(index * CHUNK, CHUNK), CHUNK)
            params = par[pl.ds(pl.multiple_of(base + index * CHUNK, CHUNK), CHUNK), :]
            lines = real[rows, :] + inner[rows, :] * column(params, 15)
            conv[rows, :] = lines
            pair_c[rows, :] = (lines * streams[0, rows, :]).astype(low)
            return carry

        lax.fori_loop(0, width // CHUNK, gating, 0)
        keep(N.conv)
        for start in range(0, length, 256):
            piece = dot_tn(pair_c[:, start : start + 256], weight[3 * width :, :])
            if side_index == 0:
                acc[start : start + 256, :] = piece
            else:
                acc[start : start + 256, :] += piece

    copies[N.norm].wait()
    copies[N.cotn] = remote(N.cotn, cot_near.at[mine], cot_near.at[mine], across)
    put(N.normed, normed, target[N.normed])
    forward(0, w_own)
    for name in (N.par, N.w3) + tuple((N.wx, piece) for piece in range(pieces)):
        copies[name].wait()
    put(N.w_peer, w_peer, target[N.w_peer])
    put(N.par, par, target[N.par])
    put(N.w_last, made[N.w_last], target[N.w_last])
    forward(1, w_peer)

    send_row[...] = acc[theirs, :].astype(low)
    copies[N.branch] = remote(N.branch, send_row, recv_branch, across)
    copies[N.branch].wait()
    residual, residual_grad, resid = made[N.residual], made[N.residual_grad], made[N.resid]

    def norm_two(chunk):
        def body(index, carry):
            start = chunk * tile + index * ROWS
            rows = pl.ds(pl.multiple_of(start, ROWS), ROWS)
            place = mine_at(start, ROWS)
            lines = (
                held[N.tokens][rows, :].astype(full)
                + acc[place, :]
                + recv_branch[rows, :].astype(full)
                + norms[2:3, :]
            )
            residual[rows, :] = lines
            mid_near[place, :] = (normed_parts(lines)[0] * norms[3:4, :] + norms[4:5, :]).astype(low)
            return carry

        lax.fori_loop(0, tile // ROWS, body, 0)
        place = mine_at(chunk * tile, tile)
        copies[N.midy, chunk] = remote((N.midy, chunk), mid_near.at[place], mid_far.at[place], over)

    norm_two(0)
    norm_two(1)
    copies[N.midn] = remote(N.midn, mid_near.at[mine], mid_near.at[mine], across)
    put(N.residual, residual, target[N.residual])
    copies[N.cotn].wait()
    for name in (N.up, N.down):
        loads[name].wait()
    up, down = held[N.up], held[N.down]

    def units(rows, mid, cot, hid, pg):
        act, slope = gelu_parts(dot_nn(mid[rows, :], up[...]) + norms[5:6, :])
        hid[rows, :] = act.astype(low)
        back = (dot_nt(cot[rows, :], down[...]) * slope).astype(low)
        pg[rows, :] = back
        return (dot_nt(back, up[...]), jnp.sum(back.astype(full), axis=0, keepdims=True))

    copies[N.midn].wait()

    def near(index, total):
        rows = pl.ds(pl.multiple_of(index * tile, tile), tile)
        product, found = units(rows, mid_near, cot_near, hid_near, pg_near)
        acc[rows, :] = product
        return total + found

    total = lax.fori_loop(0, length // tile, near, jnp.zeros((1, model_width), full))
    send_row[...] = acc[theirs, :].astype(low)
    copies[N.near] = remote(N.near, send_row, recv_near, across)

    copies[N.coty].wait()
    copies[N.cotf] = remote(N.cotf, cot_far.at[mine], cot_far.at[mine], across)
    copies[N.midy, 0].wait()
    place = mine_at(0, tile)
    copies[N.midf, 0] = remote((N.midf, 0), mid_far.at[place], mid_far.at[place], across)
    copies[N.cotf].wait()
    for chunk in range(2):
        copies[N.midf, chunk].wait()
        product, found = units(theirs_at(chunk * tile, tile), mid_far, cot_far, hid_far, pg_far)
        total = total + found
        span = slice(chunk * tile, (chunk + 1) * tile)
        send_far[span, :] = product.astype(low)
        copies[N.farx, chunk] = remote((N.farx, chunk), send_far.at[span], recv_far.at[span], across)
        product, found = units(mine_at(chunk * tile, tile), mid_far, cot_far, hid_far, pg_far)
        total = total + found
        if chunk == 0:
            copies[N.midy, 1].wait()
            place = mine_at(tile, tile)
            copies[N.midf, 1] = remote((N.midf, 1), mid_far.at[place], mid_far.at[place], across)
        copies[N.farx, chunk].wait()
        send_back[span, :] = (product + recv_far[span, :].astype(full)).astype(low)
        copies[N.back, chunk] = remote((N.back, chunk), send_back.at[span], recv_back.at[span], over)

    part_rows = model_width // 2

    def weight_grads(name, recv, path, left, right):
        grads = made[name]
        for piece in range(model_width // 256):
            span = slice(piece * 256, (piece + 1) * 256)
            product = dot_tn(left[0][:, span], right[0][...]) + dot_tn(left[1][:, span], right[1][...])
            store_rows(grads, piece * 256, product.astype(low), model_width // BLOCKS, PATHS[path])
        bit = PATHS[path][0]
        sent = grads.at[pl.ds(pl.multiple_of((1 - bits[bit]) * part_rows, part_rows), part_rows)]
        kept = grads.at[pl.ds(pl.multiple_of(bits[bit] * part_rows, part_rows), part_rows)]
        short = N.up if path == 0 else N.down
        copies[short] = remote(short, sent, made[recv], flips[bit])
        put(name, kept, target[name])

    weight_grads(N.up_g, N.up_r, 0, (mid_near, mid_far), (pg_near, pg_far))
    weight_grads(N.down_g, N.down_r, 1, (cot_near, cot_far), (hid_near, hid_far))
    copies[N.near].wait()
    down_near, down_far = made[N.down_near], made[N.down_far]
    send_row[...] = dot_nn(hid_far[theirs, :], down[...]).astype(low)
    copies[N.downf] = remote(N.downf, send_row, recv_down_far, across)
    made[N.upb_g][0:1, :] = total
    down_near[...] = dot_nn(hid_near[mine, :], down[...])
    copies[N.downf].wait()
    down_far[...] = (dot_nn(hid_far[mine, :], down[...]) + recv_down_far[...].astype(full)).astype(low)
    put(N.down_far, down_far, target[N.down_far])
    send_row[...] = dot_nn(hid_near[theirs, :], down[...]).astype(low)
    copies[N.downn] = remote(N.downn, send_row, recv_down_near, across)
    copies[N.downn].wait()
    down_near[...] += recv_down_near[...].astype(full)
    put(N.down_near, down_near, target[N.down_near])

    sums = [jnp.zeros((1, model_width), full)] * 4
    sums = tuple(sums)
    for chunk in range(2):
        copies[N.back, chunk].wait()

        def body(index, carry):
            start = chunk * tile + index * ROWS
            rows = pl.ds(pl.multiple_of(start, ROWS), ROWS)
            place = mine_at(start, ROWS)
            normed_rows, inverse = normed_parts(residual[rows, :])
            back = acc[place, :] + recv_near[rows, :].astype(full) + recv_back[rows, :].astype(full)
            cots = cot_near[place, :].astype(full)
            grad = cots + norm_rows_back(back, normed_rows, inverse, norms[3:4, :])
            residual_grad[rows, :] = grad
            rounded = grad.astype(low)
            resid[rows, :] = rounded
            found = (rounded.astype(full), back * normed_rows, back, cots)
            return tuple(a + jnp.sum(b, axis=0, keepdims=True) for a, b in zip(carry, found))

        sums = lax.fori_loop(0, tile // ROWS, body, sums)
    extra = made[N.extra]
    for index in range(4):
        extra[index : index + 1, :] = sums[index]
    put(N.resid, resid, target[N.resid])
    put(N.residual_grad, residual_grad, target[N.residual_grad])
    put(N.extra, extra, target[N.extra])
    put(N.upb_g, made[N.upb_g], target[N.upb_g])
    for short, name in ((N.up, N.up_r), (N.down, N.down_r)):
        copies[short].wait()
        put(name, made[name], target[name])
    for copy in stores.values():
        copy.wait()


def call_operator_front(operands, counts, lengths, width, length, model_width, dp_step):
    full, low = jnp.float32, jnp.bfloat16
    half = length // 2
    channels = 2 * width
    units = operands[N.fw2].shape[0]
    shapes = {
        N.proj: ((3, channels, length), low),
        N.streams: ((3, channels, length), full),
        N.signal: ((2, channels, length), full),
        N.factor: ((2, channels, length), full),
        N.conv: ((channels, length), full),
        N.normed: ((length, model_width), low),
        N.w_peer: ((4 * width, model_width), low),
        N.par: ((channels, 128), full),
        N.table: ((2, length, length), low),
        N.filt: ((6, units, length), full),
        N.w_last: ((2, units, width), full),
        N.resid: ((half, model_width), low),
        N.residual_grad: ((half, model_width), full),
        N.residual: ((half, model_width), full),
        N.up_g: ((model_width // 2, model_width), low),
        N.down_g: ((model_width // 2, model_width), low),
        N.up_r: ((model_width // 2, model_width), low),
        N.down_r: ((model_width // 2, model_width), low),
        N.down_near: ((half, model_width), full),
        N.down_far: ((half, model_width), low),
        N.extra: ((8, model_width), full),
        N.upb_g: ((8, model_width), full),
        N.freq: ((units, 128), full),
        N.feat: ((operands[N.fw1].shape[0], length), full),
    }
    split = {
        N.proj: (3, width, length),
        N.streams: (3, width, length),
        N.signal: (2, width, length),
        N.factor: (2, width, length),
        N.conv: (width, length),
        N.up_g: (model_width, model_width),
        N.down_g: (model_width, model_width),
    }
    placed = {N.w_in: (16, 128), N.w_out: (16, 128), N.w3: (8, 128)}
    rows = pltpu.VMEM((length, model_width), low)
    half_rows = pltpu.VMEM((half, model_width), low)
    wide, thin = pltpu.VMEM((width, length), full), pltpu.VMEM((width, length), low)
    scratch = [
        pltpu.VMEM(placed.get(name, operands[name].shape), operands[name].dtype) for name in FRONT_LOADS
    ]
    scratch += [pltpu.VMEM(split.get(name, shapes[name][0]), shapes[name][1]) for name in FRONT_OUTS]
    scratch += [rows] * 8 + [pltpu.VMEM((length, model_width), full)] + [wide] * 2 + [thin] * 3
    scratch += [half_rows] * 9
    scratch += [
        pltpu.VMEM((4 * width, model_width), low),
        pltpu.VMEM((8, model_width), full),
        pltpu.VMEM((24, width), full),
        pltpu.VMEM((8, 128), full),
        pltpu.VMEM((2, 1 << (length.bit_length() // 2), length), full),
        pltpu.VMEM((2, length >> (length.bit_length() // 2), length), full),
        pltpu.SemaphoreType.DMA((len(FRONT_LOADS),)),
        pltpu.SemaphoreType.DMA((len(STORES),)),
        pltpu.SemaphoreType.DMA((len(FRONT_PLAN),)),
        pltpu.SemaphoreType.DMA((len(FRONT_PLAN),)),
    ]
    results = pl.pallas_call(
        functools.partial(operator_front, dp_step),
        out_shape=tuple(jax.ShapeDtypeStruct(*shapes[name]) for name in FRONT_OUTS),
        in_specs=[pl.BlockSpec(memory_space=pl.ANY)] * len(FRONT_LOADS)
        + [pl.BlockSpec(memory_space=pltpu.SMEM)] * 2,
        out_specs=tuple(pl.BlockSpec(memory_space=pl.ANY) for name in FRONT_OUTS),
        scratch_shapes=scratch,
        compiler_params=pltpu.CompilerParams(
            vmem_limit_bytes=63 * 1024 * 1024, collective_id=1, has_side_effects=True
        ),
        name="operator_front",
    )(*(operands[name] for name in FRONT_LOADS), counts, lengths)
    return dict(zip(FRONT_OUTS, results))


PLAN = (N.resid, N.downy, N.peer_a, N.peer_b, N.y_a, N.y_b, N.chan, N.first) + tuple(
    (name, hop) for name in (N.up, N.down, N.a, N.b, N.chan) for hop in (1, 2, 3) if hop > 1 or name not in (N.up, N.down)
) + tuple((N.shared, hop) for hop in range(5))
LOADS = (N.resid, N.w_peer, N.up, N.up_r, N.down, N.down_r, N.w_in, N.w_out, N.streams, N.proj, N.conv, N.par,
         N.normed, N.table, N.factor, N.signal, N.filt, N.w_last, N.w_mid, N.feat, N.freq, N.tokens, N.gain,
         N.rgrad, N.extra, N.upb, N.residual, N.down_near, N.down_bias)
SPLIT = (N.streams, N.proj, N.conv, N.factor, N.signal)


def operator_back(dp_step, outs, *refs):
    sizes = len(LOADS)
    source = dict(zip(LOADS, refs[:sizes]))
    down_far, counts, lengths = refs[sizes : sizes + 3]
    refs = refs[:sizes] + refs[sizes + 3 :]
    out = dict(zip(outs, refs[sizes : sizes + len(outs)]))
    refs = refs[sizes + len(outs) :]
    held = dict(zip(LOADS, refs[: len(LOADS)]))
    refs = refs[len(LOADS) :]
    (grad, real, imag, pair_a, pair_b, pair_c, pair_d, stack, proj_low, h_grad, first, first_send, first_recv,
     peer_a, peer_b, beside_a, beside_b, send_a, send_b, recv_a, recv_b, sum_a, sum_b, recv_down, sums, chan_peer, chan_recv, chan, chan_hops,
     shared, shared_hops, w_own) = refs[:32]
    hops = dict(zip((N.up, N.down, N.a, N.b), (refs[32 + 5 * i : 37 + 5 * i] for i in range(4))))
    load_sem, send_sem, recv_sem = refs[52:]
    full, low = jnp.float32, jnp.bfloat16

    part = lax.axis_index(TENSOR)
    group = lax.axis_index(DP)
    side = part % 2
    bits = [(group // (dp_step << b)) % 2 for b in range(3)]
    across = {TENSOR: other_of(part, 1)}
    over = {TENSOR: other_of(part, 2)}
    flips = [{DP: other_of(group, dp_step << b)} for b in range(3)]

    def remote(name, src, dst, target):
        index = PLAN.index(name)
        return pltpu.make_async_remote_copy(
            src_ref=src,
            dst_ref=dst,
            send_sem=send_sem.at[index],
            recv_sem=recv_sem.at[index],
            device_id=target,
            device_id_type=pl.DeviceIdType.MESH,
        )

    width, length = grad.shape
    model_width = first.shape[1]
    half_rows = length // 2
    block_rows = model_width // BLOCKS
    mine = pl.ds(pl.multiple_of(side * half_rows, half_rows), half_rows)
    theirs = pl.ds(pl.multiple_of((1 - side) * half_rows, half_rows), half_rows)

    places = dict(held)
    places[N.resid] = held[N.resid].at[mine]
    places[N.w_in] = w_own.at[0 : 3 * width]
    places[N.w_out] = w_own.at[3 * width :]
    loads = {}

    def load(name, half):
        src, dst, index = source[name], places[name], LOADS.index(name)
        key = name
        if half is not None:
            span = slice(half * width, (half + 1) * width)
            if name == N.conv:
                src, dst = src.at[span], dst.at[span]
            else:
                src, dst = src.at[:, span], dst.at[:, span]
            key = (name, half)
            index = index if half == 1 else len(LOADS) + SPLIT.index(name)
        loads[key] = pltpu.make_async_copy(src, dst, load_sem.at[index])
        loads[key].start()

    late = LOADS.index(N.w_mid)
    for name in LOADS[:late]:
        load(name, 1 if name in SPLIT else None)
    for name in SPLIT:
        load(name, 0)
    for name in LOADS[late:]:
        load(name, None)

    barrier = pltpu.get_barrier_semaphore()
    for target in [across, over] + flips:
        pl.semaphore_signal(barrier, inc=1, device_id=target, device_id_type=pl.DeviceIdType.MESH)
    pl.semaphore_wait(barrier, 5)

    resid = held[N.resid]
    resid_copy = remote(N.resid, source[N.resid], resid.at[mine], across)
    resid_copy.start()
    loads[N.resid].wait()
    loads[N.w_peer].wait()
    resid_copy.wait()

    def spot(index, size):
        return pl.ds(pl.multiple_of(index * size, size), size)

    def order_of(name):
        return PATHS[1] if name == N.down else PATHS[0]

    def hop_one(name, grads):
        bit = order_of(name)[0]
        src = grads.at[spot(1 - bits[bit], 4 * block_rows)]
        copy = remote((name, 1), src, hops[name][0], flips[bit])
        copy.start()
        return copy

    def hop_two(name, grads, copy, recv_one):
        _, send_two, keep_two, recv_two, _ = hops[name]
        top, bit, _ = order_of(name)
        whole = copy is not None
        if whole:
            copy.wait()
        crossed = {N.a: recv_a, N.b: recv_b}.get(name)
        for keep in (0, 1):
            pick = bits[bit] if keep else 1 - bits[bit]
            first_place = 2 * bits[top] + pick if whole else pick
            total = (
                grads[spot(first_place, 2 * block_rows), :].astype(full)
                + recv_one[spot(pick, 2 * block_rows), :].astype(full)
            )
            if crossed is not None:
                total = total + crossed[spot(pick, 2 * block_rows), :].astype(full)
            if keep:
                keep_two[...] = total
            else:
                send_two[...] = total.astype(low)
                copy = remote((name, 2), send_two, recv_two, flips[bit])
                copy.start()
        return copy

    def hop_three(name, copy):
        recv_one, send_two, keep_two, recv_two, recv_three = hops[name]
        bit = order_of(name)[2]
        copy.wait()
        place = spot(1 - bits[bit], block_rows)
        send_two[0:block_rows, :] = (keep_two[place, :] + recv_two[place, :].astype(full)).astype(low)
        copy = remote((name, 3), send_two.at[0:block_rows], recv_three, flips[bit])
        copy.start()
        return copy

    def hop_last(name, copy):
        recv_one, send_two, keep_two, recv_two, recv_three = hops[name]
        copy.wait()
        place = spot(bits[order_of(name)[2]], block_rows)
        return keep_two[place, :] + recv_two[place, :].astype(full) + recv_three[...].astype(full)

    copies = {N.downy: remote(N.downy, down_far, recv_down, over)}
    copies[N.downy].start()
    for name in (N.up, N.up_r, N.down, N.down_r):
        loads[name].wait()
    for name, received in ((N.up, N.up_r), (N.down, N.down_r)):
        copies[name] = hop_two(name, held[name], None, held[received])

    lanes = lax.broadcasted_iota(jnp.int32, (CHUNK, length), 1)
    par, streams, proj, conv = held[N.par], held[N.streams], held[N.proj], held[N.conv]
    cos, sin = held[N.table].at[0], held[N.table].at[1]
    factor, signal, normed = held[N.factor], held[N.signal], held[N.normed]
    filt = held[N.filt]
    weights = (w_own, held[N.w_peer])

    def half_pass(half, loaded, early, middle):
        base = half * width
        weight = weights[half]
        own_w = 3 * width

        def at(index):
            return pl.ds(pl.multiple_of(index * CHUNK, CHUNK), CHUNK)

        def far(index):
            return pl.ds(pl.multiple_of(base + index * CHUNK, CHUNK), CHUNK)

        def stream_back(i, index, params, back):
            moved = [shifted(back, -j, lanes) for j in range(3)]
            out = sum(column(params, 3 * j + i) * moved[j] for j in range(3)).astype(low)
            line = proj[i, far(index), :].astype(full)
            start = pl.multiple_of(i * width + index * CHUNK, CHUNK)
            proj_low[pl.ds(start, CHUNK), :] = out
            found = [(3 * j + i, jnp.sum(moved[j] * line, axis=1, keepdims=True)) for j in range(3)]
            found.append((9 + i, jnp.sum(out.astype(full), axis=1, keepdims=True)))
            found.append((12 + i, jnp.sum(back, axis=1, keepdims=True)))
            return found

        grad[...] = dot_nt(weight[own_w:, :], resid[...])
        for name in (N.streams, N.proj, N.conv):
            loads[name, half].wait()
        if not loaded:
            loads[N.par].wait()

        def before(index, carry):
            rows = far(index)
            params = par[rows, :]
            gate_out, gate_in, values = streams[0, rows, :], streams[1, rows, :], streams[2, rows, :]
            mixed_grad = grad[at(index), :]
            conv_part = conv[rows, :]
            conv_grad = mixed_grad * gate_out
            grad[at(index), :] = conv_grad
            pair_a[at(index), :] = conv_grad.astype(low)
            pair_b[at(index), :] = (conv_part * gate_out).astype(low)
            found = stream_back(0, index, params, mixed_grad * conv_part)
            found.append((15, jnp.sum(conv_grad * values * gate_in, axis=1, keepdims=True)))
            sums[at(index), :] = pack_columns(found, CHUNK)
            return carry

        lax.fori_loop(0, width // CHUNK, before, 0)
        if not loaded:
            loads[N.normed].wait()
        stack[0:width, :] = dot_nn(proj_low[0:width, :], normed[...])
        stack[width : 2 * width, :] = dot_nn(pair_b[...], resid[...])
        early()
        if not loaded:
            loads[N.table].wait()
        real[...] = dot_nn(pair_a[...], cos[...])
        imag[...] = dot_nt(pair_a[...], sin[...])
        loads[N.factor, half].wait()
        loads[N.signal, half].wait()
        first_lane = lanes == 0
        scale = jnp.where(first_lane, 0.5 / length, 1.0 / length)

        def between(index, carry):
            rows, place = far(index), at(index)
            cos_part, sin_part = real[place, :] * scale, imag[place, :] * scale
            f_cos, f_sin = factor[0, rows, :], factor[1, rows, :]
            f_last = jnp.where(first_lane, f_sin, f_cos)
            f_sin = jnp.where(first_lane, 0.0, f_sin)
            pair_a[place, :] = (cos_part * f_cos + sin_part * f_sin).astype(low)
            pair_b[place, :] = (sin_part * f_last - cos_part * f_sin).astype(low)
            s_cos, s_sin = signal[0, rows, :], signal[1, rows, :]
            s_last = jnp.where(first_lane, s_sin, s_cos)
            s_sin = jnp.where(first_lane, 0.0, s_sin)
            pair_c[place, :] = (cos_part * s_cos + sin_part * s_sin).astype(low)
            pair_d[place, :] = (sin_part * s_last - cos_part * s_sin).astype(low)
            return carry

        lax.fori_loop(0, width // CHUNK, between, 0)
        middle()
        real[...] = dot_nn(pair_a[...], cos[...]) + dot_nn(pair_b[...], sin[...])
        imag[...] = dot_nn(pair_c[...], cos[...]) + dot_nn(pair_d[...], sin[...])

        def after(index, carry):
            rows = far(index)
            params = par[rows, :]
            gate_in, values = streams[1, rows, :], streams[2, rows, :]
            back = real[at(index), :] + grad[at(index), :] * column(params, 15)
            found = stream_back(1, index, params, back * values)
            found += stream_back(2, index, params, back * gate_in)
            sums[at(index), :] = sums[at(index), :] + pack_columns(found, CHUNK)
            window = jnp.exp(-lanes.astype(full) * column(params, 16))
            pair_a[at(index), :] = (imag[at(index), :] * window).astype(low)
            return carry

        lax.fori_loop(0, width // CHUNK, after, 0)
        if not loaded:
            for name in (N.filt, N.w_last):
                loads[name].wait()
        stack[2 * width :, :] = dot_nn(proj_low[width:, :], normed[...])
        target = chan_peer if half == 1 else chan
        target[0:16, :] = jnp.transpose(sums[...])[0:16, :]
        target[16:80, :] = dot_nt(filt[1].astype(low), pair_a[...])
        h_part = dot_nn(held[N.w_last][half].astype(low), pair_a[...])
        if half == 1:
            h_grad[...] = h_part
        else:
            h_grad[...] += h_part

    def turned(part_index, ref):
        middle = model_width // 2
        rows = slice(part_index * middle, (part_index + 1) * middle)
        for start in range(0, model_width, 128):
            block = jnp.transpose(stack[rows, start : start + 128]).astype(low)
            store_rows(ref, start, block, block_rows, PATHS[0])

    peers = ((N.peer_a, peer_a, beside_a, send_a), (N.peer_b, peer_b, beside_b, send_b))

    def peer_first(part_index):
        name, grads, beside, _ = peers[part_index]
        turned(part_index, grads)
        src = grads.at[spot(1 - bits[0], 4 * block_rows)]
        copies[name] = remote(name, src, beside, flips[0])
        copies[name].start()

    def peer_cross(part_index):
        name, grads, beside, sent = peers[part_index]
        across_name, crossed = ((N.y_a, recv_a), (N.y_b, recv_b))[part_index]
        copies[name].wait()
        kept = grads[spot(bits[0], 4 * block_rows), :].astype(full)
        sent[...] = (kept + beside[...].astype(full)).astype(low)
        copies[across_name] = remote(across_name, sent, crossed, over)
        copies[across_name].start()

    def first_part(half):
        for start in range(0, length, 256):
            product = dot_tn(proj_low[:, start : start + 256], weights[half][: 3 * width, :])
            if half == 1:
                first[start : start + 256, :] = product
            else:
                first[start : start + 256, :] += product

    def last_hops():
        for name in (N.up, N.down):
            copies[name] = hop_three(name, copies[name])

    half_pass(1, False, lambda: peer_first(0), last_hops)
    peer_first(1)
    chan_peer[80:88, :] = jnp.zeros((8, width), full)
    copies[N.chan] = remote(N.chan, chan_peer, chan_recv, over)
    copies[N.chan].start()
    first_part(1)
    loads[N.w_in].wait()
    loads[N.w_out].wait()
    peer_cross(0)

    def own_first():
        turned(0, sum_a)
        copies[N.a] = hop_one(N.a, sum_a)

    half_pass(0, True, own_first, lambda: peer_cross(1))
    first_part(0)
    first_send[...] = first[theirs, :].astype(low)
    first_copy = remote(N.first, first_send, first_recv, across)
    first_copy.start()
    turned(1, sum_b)
    copies[N.b] = hop_one(N.b, sum_b)
    copies[N.y_a].wait()
    copies[N.a] = hop_two(N.a, sum_a, copies[N.a], hops[N.a][0])

    copies[N.chan].wait()
    loads[N.upb].wait()
    chan[0:80, :] = chan[0:80, :] + chan_recv[0:80, :]
    chan[80:88, :] = jnp.zeros((8, width), full)
    for index in range(held[N.upb].shape[1] // width):
        chan[80 + index : 81 + index, :] = held[N.upb][0:1, index * width : (index + 1) * width]
    chan_copy = remote((N.chan, 1), chan, chan_hops.at[0], flips[0])
    chan_copy.start()

    for name in (N.w_mid, N.feat, N.freq):
        loads[name].wait()
    freq, w_mid = held[N.freq], held[N.w_mid]
    shared[...] = jnp.zeros_like(shared)
    units = w_mid.shape[0]
    feats = held[N.feat].shape[0]
    slope = h_grad[...] * filt[3]
    q_two = jnp.sum(slope * filt[5], axis=1, keepdims=True)
    slope = slope * column(freq[...], 1)
    b_two = jnp.sum(slope, axis=1, keepdims=True)
    slope_low = slope.astype(low)
    shared[80 : 80 + units, 0:units] = dot_nt(filt[0].astype(low), slope_low)
    slope = dot_nn(w_mid[...].astype(low), slope_low) * filt[2]
    q_one = jnp.sum(slope * filt[4], axis=1, keepdims=True)
    slope = slope * column(freq[...], 0)
    b_one = jnp.sum(slope, axis=1, keepdims=True)
    shared[40 : 40 + feats, 0:units] = dot_nt(held[N.feat][...].astype(low), slope.astype(low))
    vectors = pack_columns([(0, b_one), (1, q_one), (2, b_two), (3, q_two)], units)
    shared[144:152, 0:units] = jnp.transpose(vectors)[0:8, :]

    for name in (N.tokens, N.gain, N.rgrad, N.extra):
        loads[name].wait()
    first_copy.wait()
    gain = held[N.gain][...][None, :]

    def norm_rows(index, carry):
        rows = pl.ds(pl.multiple_of(index * ROWS, ROWS), ROWS)
        own = pl.ds(pl.multiple_of(side * half_rows + index * ROWS, ROWS), ROWS)
        normed_rows, inverse = normed_parts(held[N.tokens][rows, :].astype(full))
        back = first[own, :] + first_recv[rows, :].astype(full)
        grad_rows = norm_rows_back(back, normed_rows, inverse, gain)
        out[N.input_grad][rows, :] = held[N.rgrad][rows, :] + grad_rows
        return (
            carry[0] + jnp.sum(back * normed_rows, axis=0, keepdims=True),
            carry[1] + jnp.sum(back, axis=0, keepdims=True),
        )

    zero = jnp.zeros((1, model_width), full)
    found = lax.fori_loop(0, half_rows // ROWS, norm_rows, (zero, zero))
    extra = held[N.extra]
    vectors = list(found) + [extra[i : i + 1, :] for i in range(4)]
    for index, vector in enumerate(vectors):
        for piece in range(model_width // 128):
            row = index * (model_width // 128) + piece
            shared[row : row + 1, :] = vector[:, piece * 128 : (piece + 1) * 128]

    shared_targets = [across, over] + flips

    def share(hop):
        copy = remote((N.shared, hop), shared, shared_hops.at[hop], shared_targets[hop])
        copy.start()
        return copy

    def shared_next(hop, copy):
        copy.wait()
        shared[...] = shared[...] + shared_hops[hop]
        return share(hop + 1) if hop < 4 else None

    def chan_next(hop, copy):
        copy.wait()
        chan[...] = chan[...] + chan_hops[hop]
        if hop == 2:
            return None
        copy = remote((N.chan, hop + 2), chan, chan_hops.at[hop + 1], flips[hop + 1])
        copy.start()
        return copy

    shared_copy = share(0)
    chan_copy = chan_next(0, chan_copy)
    copies[N.a] = hop_three(N.a, copies[N.a])
    shared_copy = shared_next(0, shared_copy)
    copies[N.y_b].wait()
    copies[N.b] = hop_two(N.b, sum_b, copies[N.b], hops[N.b][0])

    for name in (N.residual, N.down_near, N.down_bias):
        loads[name].wait()
    copies[N.downy].wait()
    slot = part * half_rows // length
    mask_rows = jnp.where(slot < counts[0], lengths[0, slot], 0) - part * half_rows % length
    down_bias = held[N.down_bias][...][None, :]

    def result_rows(index, carry):
        rows = pl.ds(pl.multiple_of(index * ROWS, ROWS), ROWS)
        total = held[N.residual][rows, :] + held[N.down_near][rows, :] + recv_down[rows, :].astype(full)
        place = lax.broadcasted_iota(jnp.int32, (ROWS, model_width), 0) + index * ROWS
        out[N.activations][rows, :] = jnp.where(place < mask_rows, total + down_bias, 0.0).astype(low)
        return carry

    lax.fori_loop(0, half_rows // ROWS, result_rows, 0)
    shared_copy = shared_next(1, shared_copy)
    chan_copy = chan_next(1, chan_copy)
    copies[N.b] = hop_three(N.b, copies[N.b])
    shared_copy = shared_next(2, shared_copy)
    for name in (N.up, N.down, N.a):
        out[name][...] = hop_last(name, copies[name])
    chan_next(2, chan_copy)
    shared_copy = shared_next(3, shared_copy)
    out[N.b][...] = hop_last(N.b, copies[N.b])
    shared_next(4, shared_copy)
    out[N.shared][...] = shared[...]
    out[N.chan][...] = chan[...]


PASSED = (N.activations, N.input_grad, N.up, N.down)


def lay_out(group_units, *refs):
    sources = dict(zip(RAW, refs[: len(RAW)]))
    outs = dict(zip(RESULTS, refs[len(RAW) : len(RAW) + len(RESULTS)]))
    held = dict(zip(RAW, refs[len(RAW) + len(RESULTS) : -1]))
    sem = refs[-1]
    group = lax.axis_index(DP)
    loads, passes = {}, []
    for index, name in enumerate(RAW):
        if name in PASSED:
            passes.append(pltpu.make_async_copy(sources[name], outs[name], sem.at[index]))
            passes[-1].start()
        else:
            loads[name] = pltpu.make_async_copy(sources[name], held[name], sem.at[index])
            loads[name].start()
    for copy in loads.values():
        copy.wait()
    part_a, part_b = jnp.transpose(held[N.a][...]), jnp.transpose(held[N.b][...])
    width = outs[N.out].shape[0]
    outs[N.in_w][0] = part_a[0:width, :]
    outs[N.in_w][1] = part_b[0:width, :]
    outs[N.in_w][2] = part_b[width:, :]
    outs[N.out][...] = part_a[width:, :]
    shared, chan = held[N.shared], held[N.chan]
    model_width = outs[N.up].shape[1]
    units = outs[N.w2].shape[0]
    pieces = model_width // 128
    for index, name in enumerate(WIDES):
        row = index * pieces
        lines = [shared[row + piece : row + piece + 1, :] for piece in range(pieces)]
        outs[name][...] = jnp.concatenate(lines, axis=1).reshape(model_width)
    outs[N.w1][...] = shared[40 : 40 + outs[N.w1].shape[0], 0:units]
    outs[N.w2][...] = shared[80 : 80 + units, 0:units]
    for index, name in enumerate(VECTORS):
        outs[name][...] = shared[144 + index : 145 + index, 0:units].reshape(units)
    outs[N.conv_w][...] = chan[0:9, :].reshape(3, 3, width)
    outs[N.in_b][...] = chan[9:12, :]
    outs[N.conv_b][...] = chan[12:15, :]
    outs[N.f_bias][...] = chan[15:16, :].reshape(width)
    lines = [chan[80 + index : 81 + index, :] for index in range(model_width // width)]
    outs[N.up_b][...] = jnp.concatenate(lines, axis=1).reshape(model_width)
    outs[N.w3][...] = chan[pl.ds(pl.multiple_of(16 + group * group_units, 8), group_units), :]
    for copy in passes:
        copy.wait()


def call_lay_out(raw, inputs_count, units, width):
    full, low = jnp.float32, jnp.bfloat16
    rows, model_width = raw[N.input_grad].shape
    block = raw[N.up].shape[0]
    shapes = {name: raw[name].shape for name in PASSED}
    shapes.update({name: (model_width,) for name in WIDES + (N.up_b,)})
    shapes.update({name: (units,) for name in VECTORS})
    shapes.update(
        {
            N.in_w: (3, width, block),
            N.out: (width, block),
            N.w1: (inputs_count, units),
            N.w2: (units, units),
            N.w3: (units // BLOCKS, width),
            N.conv_w: (3, 3, width),
            N.in_b: (3, width),
            N.conv_b: (3, width),
            N.f_bias: (width,),
        }
    )
    results = pl.pallas_call(
        functools.partial(lay_out, units // BLOCKS),
        out_shape=tuple(
            jax.ShapeDtypeStruct(shapes[name], low if name == N.activations else full) for name in RESULTS
        ),
        in_specs=[pl.BlockSpec(memory_space=pl.ANY)] * len(RAW),
        out_specs=tuple(pl.BlockSpec(memory_space=pltpu.VMEM) for name in RESULTS),
        scratch_shapes=[
            pltpu.VMEM((8, 128) if name in PASSED else raw[name].shape, full) for name in RAW
        ]
        + [pltpu.SemaphoreType.DMA((len(RAW),))],
        name="lay_out",
    )(*(raw[name] for name in RAW))
    return results


def call_operator_back(operands, counts, lengths, width, length, model_width, dp_count):
    full, low = jnp.float32, jnp.bfloat16
    units = operands[N.w_mid].shape[0]
    half_rows = length // 2
    block = model_width // BLOCKS
    thin_grads = pltpu.VMEM((model_width, model_width // 2), low)
    part_grads = pltpu.VMEM((model_width // 2, model_width // 2), low)
    low_rows = pltpu.VMEM((half_rows, model_width), low)
    held = []
    for name in LOADS:
        shape = operands[name].shape
        if name == N.resid:
            shape = (length, model_width)
        elif name in (N.w_in, N.w_out):
            shape = (16, 128)
        held.append(pltpu.VMEM(shape, operands[name].dtype))
    wide, thin = pltpu.VMEM((width, length), full), pltpu.VMEM((width, length), low)
    chan = pltpu.VMEM((88, width), full)
    shared = pltpu.VMEM((152, 128), full)
    scratch = held + [wide] * 3 + [thin] * 4
    scratch += [
        pltpu.VMEM((4 * width, model_width), full),
        pltpu.VMEM((3 * width, length), low),
        pltpu.VMEM((units, length), full),
        pltpu.VMEM((length, model_width), full),
        low_rows,
        low_rows,
        thin_grads,
        thin_grads,
        part_grads,
        part_grads,
        part_grads,
        part_grads,
        part_grads,
        part_grads,
        thin_grads,
        thin_grads,
        low_rows,
        pltpu.VMEM((width, 128), full),
        chan,
        chan,
        chan,
        pltpu.VMEM((3, 88, width), full),
        shared,
        pltpu.VMEM((5, 152, 128), full),
        pltpu.VMEM((4 * width, model_width), low),
    ]
    for columns in (model_width, model_width, model_width // 2, model_width // 2):
        scratch += [
            pltpu.VMEM((4 * block, columns), low),
            pltpu.VMEM((2 * block, columns), low),
            pltpu.VMEM((2 * block, columns), full),
            pltpu.VMEM((2 * block, columns), low),
            pltpu.VMEM((block, columns), low),
        ]
    scratch += [
        pltpu.SemaphoreType.DMA((len(LOADS) + len(SPLIT),)),
        pltpu.SemaphoreType.DMA((len(PLAN),)),
        pltpu.SemaphoreType.DMA((len(PLAN),)),
    ]
    shapes = {N.activations: (half_rows, model_width), N.input_grad: (half_rows, model_width)}
    shapes.update({N.up: (block, model_width), N.down: (block, model_width)})
    shapes.update({N.a: (block, model_width // 2), N.b: (block, model_width // 2)})
    shapes.update({N.shared: (152, 128), N.chan: (88, width)})
    outs = tuple(shapes)
    results = pl.pallas_call(
        functools.partial(operator_back, dp_count // BLOCKS, outs),
        out_shape=tuple(
            jax.ShapeDtypeStruct(shapes[name], low if name == N.activations else full) for name in outs
        ),
        in_specs=[pl.BlockSpec(memory_space=pl.ANY)] * (len(LOADS) + 1)
        + [pl.BlockSpec(memory_space=pltpu.SMEM)] * 2,
        out_specs=tuple(pl.BlockSpec(memory_space=pltpu.VMEM) for out in outs),
        scratch_shapes=scratch,
        compiler_params=pltpu.CompilerParams(
            vmem_limit_bytes=63 * 1024 * 1024, collective_id=0, has_side_effects=True
        ),
        cost_estimate=pl.CostEstimate(
            flops=4 * width * length * (10 * length + 8 * model_width),
            bytes_accessed=40 * 1024 * 1024,
            transcendentals=0,
        ),
        name="operator_back",
    )(*(operands[name] for name in LOADS), operands[N.down_far], counts, lengths)
    return dict(zip(outs, results))


def local(
    tokens,
    seq_counts,
    seq_lengths,
    norm1_gain,
    norm1_bias,
    in_weight,
    in_bias,
    conv_weight,
    conv_bias,
    filter_w1,
    filter_b1,
    filter_freq1,
    filter_w2,
    filter_b2,
    filter_freq2,
    filter_w3,
    filter_bias,
    out_weight,
    out_bias,
    norm2_gain,
    norm2_bias,
    up_weight,
    up_bias,
    down_weight,
    down_bias,
    cotangent,
):
    low = jnp.bfloat16
    full = jnp.float32
    tensor_count = lax.axis_size(TENSOR)
    dp_count = lax.axis_size(DP)
    row_share, model_width = tokens.shape
    width = in_weight.shape[1]
    slot_count = seq_lengths.shape[1]
    length = row_share * tensor_count // slot_count
    part = lax.axis_index(TENSOR)
    group = lax.axis_index(DP)

    inputs_count = filter_w1.shape[0]
    units = filter_w2.shape[0]
    flat_in = in_weight.reshape(3 * width, model_width)
    front = call_operator_front(
        {
            N.w_in: flat_in,
            N.w_out: out_weight,
            N.tokens: tokens,
            N.g1: norm1_gain,
            N.b1: norm1_bias,
            N.cw: conv_weight,
            N.ib: in_bias,
            N.cb: conv_bias,
            N.fb: filter_bias,
            N.w3: filter_w3,
            N.cot: cotangent,
            N.seeds: jnp.asarray(turn_seeds(length)),
            N.fw1: filter_w1,
            N.fw2: filter_w2,
            N.fb1: filter_b1,
            N.ff1: filter_freq1,
            N.fb2: filter_b2,
            N.ff2: filter_freq2,
            N.ob: out_bias,
            N.g2: norm2_gain,
            N.b2: norm2_bias,
            N.upb: up_bias,
            N.up: up_weight,
            N.down: down_weight,
        },
        seq_counts,
        seq_lengths,
        width,
        length,
        model_width,
        dp_count // BLOCKS,
    )
    back = call_operator_back(
        {
            N.resid: front[N.resid],
            N.w_peer: front[N.w_peer],
            N.w_in: flat_in,
            N.w_out: out_weight,
            N.streams: front[N.streams],
            N.proj: front[N.proj],
            N.conv: front[N.conv],
            N.par: front[N.par],
            N.table: front[N.table],
            N.factor: front[N.factor],
            N.signal: front[N.signal],
            N.normed: front[N.normed],
            N.filt: front[N.filt],
            N.w_last: front[N.w_last],
            N.up: front[N.up_g],
            N.down: front[N.down_g],
            N.up_r: front[N.up_r],
            N.down_r: front[N.down_r],
            N.down_far: front[N.down_far],
            N.w_mid: filter_w2,
            N.feat: front[N.feat],
            N.freq: front[N.freq],
            N.tokens: tokens,
            N.gain: norm1_gain,
            N.rgrad: front[N.residual_grad],
            N.extra: front[N.extra],
            N.upb: front[N.upb_g],
            N.residual: front[N.residual],
            N.down_near: front[N.down_near],
            N.down_bias: down_bias,
        },
        seq_counts,
        seq_lengths,
        width,
        length,
        model_width,
        dp_count,
    )
    if dp_count == BLOCKS:
        results = list(call_lay_out(back, inputs_count, units, width))
        place = RESULTS.index(N.down)
        results[place] = jnp.transpose(results[place])
        return tuple(results)

    rest = dp_count.bit_length() - BLOCKS.bit_length()

    def flips(bit_index):
        return [(i, i ^ (1 << bit_index)) for i in range(dp_count)]

    def rest_scatter(grad):
        for bit_index in range(rest):
            bit = (group >> bit_index) & 1
            kept = grad.reshape(1 << (rest - 1 - bit_index), 2, model_width // dp_count, -1)
            mine = lax.dynamic_index_in_dim(kept, bit, 1, keepdims=False)
            sent = lax.dynamic_index_in_dim(kept, 1 - bit, 1, keepdims=False)
            grad = mine + lax.ppermute(sent.astype(low), DP, flips(bit_index)).astype(full)
        return grad.reshape(model_width // dp_count, -1)

    def rest_sum(values):
        for bit_index in range(rest):
            values = values + lax.ppermute(values, DP, flips(bit_index))
        return values

    part_a, part_b = rest_scatter(back[N.a]), rest_scatter(back[N.b])
    operator_grads = jnp.concatenate([part_a[:, :width], part_b, part_a[:, width:]], axis=1)
    shared, chan = rest_sum(back[N.shared]), rest_sum(back[N.chan])
    wide = shared[: 6 * (model_width // 128)].reshape(6, model_width)
    share = units // dp_count
    grad_in = operator_grads[:, : 3 * width].reshape(-1, 3, width)
    return (
        back[N.activations],
        back[N.input_grad],
        wide[0],
        wide[1],
        jnp.transpose(grad_in, (1, 2, 0)),
        chan[9:12],
        chan[0:9].reshape(3, 3, width),
        chan[12:15],
        shared[40 : 40 + inputs_count, :units],
        shared[144, :units],
        shared[145, :units],
        shared[80 : 80 + units, :units],
        shared[146, :units],
        shared[147, :units],
        lax.dynamic_slice_in_dim(chan[16 : 16 + units], group * share, share, 0),
        chan[15],
        jnp.transpose(operator_grads[:, 3 * width :]),
        wide[2],
        wide[3],
        wide[4],
        rest_scatter(back[N.up]),
        chan[80 : 80 + model_width // width].reshape(-1),
        jnp.transpose(rest_scatter(back[N.down])),
        wide[5],
    )


def solution(mesh):
    in_specs = (
        P((DP, TENSOR), None),
        P(DP),
        P(DP, None),
        P(),
        P(),
        P(None, TENSOR, None),
        P(None, TENSOR),
        P(None, None, TENSOR),
        P(None, TENSOR),
        P(),
        P(),
        P(),
        P(),
        P(),
        P(),
        P(None, TENSOR),
        P(TENSOR),
        P(TENSOR, None),
        P(),
        P(),
        P(),
        P(None, TENSOR),
        P(TENSOR),
        P(TENSOR, None),
        P(),
        P((DP, TENSOR), None),
    )
    out_specs = (
        P((DP, TENSOR), None),
        P((DP, TENSOR), None),
        P(),
        P(),
        P(None, TENSOR, DP),
        P(None, TENSOR),
        P(None, None, TENSOR),
        P(None, TENSOR),
        P(),
        P(),
        P(),
        P(),
        P(),
        P(),
        P(DP, TENSOR),
        P(TENSOR),
        P(TENSOR, DP),
        P(),
        P(),
        P(),
        P(DP, TENSOR),
        P(TENSOR),
        P(TENSOR, DP),
        P(),
    )
    return jax.shard_map(local, mesh=mesh, in_specs=in_specs, out_specs=out_specs, check_vma=False)
```

```python
import functools
import math

import jax
import jax.numpy as jnp
import numpy as np
from jax import lax
from jax.experimental import pallas as pl
from jax.experimental.pallas import tpu as pltpu
from jax.sharding import PartitionSpec as P

highest = lax.Precision.HIGHEST
norm_epsilon = 1e-05
slow_rate = math.log(100.0) / 1.5
fast_rate = math.log(100.0) / 0.3


def turn_seeds(length):
    levels = np.array(list(range(8)) + [1 << i for i in range(3, length.bit_length() - 1)])
    angle = (levels[:, None] * np.arange(length) % (2 * length)) * (math.pi / length)
    return np.stack([np.cos(angle), np.sin(angle)]).astype(np.float32)


def dot_nt(left, right):
    return lax.dot_general(
        left, right, (((1,), (1,)), ((), ())), preferred_element_type=jnp.float32
    )


def dot_nn(left, right):
    return jnp.dot(left, right, preferred_element_type=jnp.float32)


def dot_tn(left, right):
    return lax.dot_general(
        left, right, (((0,), (0,)), ((), ())), preferred_element_type=jnp.float32
    )


def shifted(values, shift, lanes):
    length = values.shape[1]
    if shift == 0:
        return values
    if shift > 0:
        return jnp.where(lanes >= shift, pltpu.roll(values, shift, 1), 0.0)
    return jnp.where(lanes < length + shift, pltpu.roll(values, length + shift, 1), 0.0)


def column(params, index):
    return params[:, index : index + 1]


def pack_columns(columns, rows):
    lanes = lax.broadcasted_iota(jnp.int32, (rows, 128), 1)
    packed = jnp.zeros((rows, 128), jnp.float32)
    for index, values in columns:
        packed = jnp.where(lanes == index, values, packed)
    return packed


BLOCKS = 8
CHUNK = 64
ROWS = 128


def other_of(index, step):
    return index + step * (1 - 2 * ((index // step) % 2))


TENSOR = "tensor"
DP = "dp"


class N:
    (
        a, activations, b, b1, b2, back, branch, cb, chan, conv, conv_b, conv_w, cot, cotf, cotn,
        coty, cw, down, down_b, down_bias, down_far, down_g, down_near, down_r, downf, downn, downy,
        extra, f_bias, factor, farx, fb, fb1, fb2, feat, ff1, ff2, filt, first, freq, fw1, fw2, g1,
        g2, gain, gain1, gain2, ib, in_b, in_w, input_grad, midf, midn, midy, near, norm, normed,
        ob, out, out_b, par, peer_a, peer_b, proj, resid, residual, residual_grad, rgrad, seeds,
        shared, shift1, shift2, signal, streams, table, tokens, up, up_b, up_g, up_r, upb, upb_g,
        w1, w2, w3, w_in, w_last, w_mid, w_out, w_peer, wx, wy, y_a, y_b,
    ) = range(94)


FRONT_PLAN = (N.up, N.down, (N.wy, 0), (N.wy, 1), (N.wy, 2), (N.wx, 0), (N.wx, 1), (N.wx, 2), N.norm, N.par, N.w3, N.cotn, N.coty, N.cotf, N.branch, N.midn, (N.midy, 0), (N.midy, 1),
              (N.midf, 0), (N.midf, 1), N.near, (N.farx, 0), (N.farx, 1), (N.back, 0), (N.back, 1), N.downn, N.downf)
FRONT_LOADS = (N.w_in, N.w_out, N.tokens, N.g1, N.b1, N.cw, N.ib, N.cb, N.fb, N.w3, N.cot, N.seeds, N.fw1,
               N.fw2, N.fb1, N.ff1, N.fb2, N.ff2, N.ob, N.g2, N.b2, N.upb, N.up, N.down)
FRONT_OUTS = (N.proj, N.streams, N.signal, N.factor, N.conv, N.normed, N.w_peer, N.par, N.table, N.filt, N.w_last,
              N.resid, N.residual_grad, N.residual, N.up_g, N.down_g, N.up_r, N.down_r, N.down_near, N.down_far, N.extra, N.upb_g, N.freq, N.feat)


def gelu_parts(values):
    cdf = 0.5 * (1.0 + lax.erf(values * (1.0 / math.sqrt(2.0))))
    density = jnp.exp(-0.5 * values * values) * (1.0 / math.sqrt(2.0 * math.pi))
    return (values * cdf, cdf + values * density)


def normed_parts(values):
    centred = values - jnp.mean(values, axis=-1, keepdims=True)
    inverse = lax.rsqrt(jnp.mean(centred * centred, axis=-1, keepdims=True) + norm_epsilon)
    return (centred * inverse, inverse)


def norm_rows_back(back, normed, inverse, gain):
    scaled = back * gain
    return inverse * (
        scaled
        - jnp.mean(scaled, axis=-1, keepdims=True)
        - normed * jnp.mean(scaled * normed, axis=-1, keepdims=True)
    )


def path_place(row, block_rows, order):
    index, offset = row // block_rows, row % block_rows
    bits = [(index >> b) & 1 for b in range(3)]
    return (bits[order[0]] * 4 + bits[order[1]] * 2 + bits[order[2]]) * block_rows + offset


def store_rows(ref, start, values, block_rows, order):
    stop, begin = start + values.shape[0], start
    while begin < stop:
        size = min(block_rows - begin % block_rows, stop - begin)
        place = path_place(begin, block_rows, order)
        ref[place : place + size, :] = values[begin - start : begin - start + size, :]
        begin += size


HALVES = (N.proj, N.streams, N.signal, N.factor, N.conv)
STORES = tuple((name, half) for name in HALVES for half in (0, 1)) + FRONT_OUTS[5:]
WIDES = (N.gain1, N.shift1, N.out_b, N.gain2, N.shift2, N.down_b)
VECTORS = (N.fb1, N.ff1, N.fb2, N.ff2)
RAW = (N.activations, N.input_grad, N.up, N.down, N.a, N.b, N.shared, N.chan)
RESULTS = (N.activations, N.input_grad, N.gain1, N.shift1, N.in_w, N.in_b, N.conv_w, N.conv_b, N.w1, N.fb1, N.ff1, N.w2,
           N.fb2, N.ff2, N.w3, N.f_bias, N.out, N.out_b, N.gain2, N.shift2, N.up, N.up_b, N.down, N.down_b)
PATHS = ((0, 1, 2), (1, 0, 2))


def operator_front(dp_step, *refs):
    full, low = jnp.float32, jnp.bfloat16
    n, m = len(FRONT_LOADS), len(FRONT_OUTS)
    source = dict(zip(FRONT_LOADS, refs[:n]))
    counts, lengths = refs[n], refs[n + 1]
    refs = refs[:n] + refs[n + 2 :]
    target = dict(zip(FRONT_OUTS, refs[n : n + m]))
    held = dict(zip(FRONT_LOADS, refs[n + m : 2 * n + m]))
    made = dict(zip(FRONT_OUTS, refs[2 * n + m : 2 * n + 2 * m]))
    (mid_near, mid_far, cot_near, cot_far, hid_near, hid_far, pg_near, pg_far, acc, inner, real,
     pair_a, pair_b, pair_c, send_row, recv_branch, recv_near, send_far, recv_far, send_back, recv_back,
     recv_down_near, recv_down_far, w_own, norms, lines, fcol, low_turns, high_turns, in_order, load_sem, store_sem, send_sem, recv_sem,
     ) = refs[2 * n + 2 * m :]

    part = lax.axis_index(TENSOR)
    group = lax.axis_index(DP)
    side = part % 2
    across = {TENSOR: other_of(part, 1)}
    over = {TENSOR: other_of(part, 2)}
    beside = {DP: other_of(group, 1)}
    bits = [(group // (dp_step << b)) % 2 for b in range(3)]
    flips = [{DP: other_of(group, dp_step << b)} for b in range(2)]
    greeted = [across, over] + flips + ([beside] if dp_step > 1 else [])
    width = inner.shape[0]
    length, model_width = acc.shape
    half = length // 2
    tile = half // 2
    mine = pl.ds(pl.multiple_of(side * half, half), half)
    theirs = pl.ds(pl.multiple_of((1 - side) * half, half), half)

    def mine_at(start, size):
        return pl.ds(pl.multiple_of(side * half + start, 16), size)

    def theirs_at(start, size):
        return pl.ds(pl.multiple_of((1 - side) * half + start, 16), size)

    def remote(name, src, dst, to):
        index = FRONT_PLAN.index(name)
        copy = pltpu.make_async_remote_copy(
            src_ref=src,
            dst_ref=dst,
            send_sem=send_sem.at[index],
            recv_sem=recv_sem.at[index],
            device_id=to,
            device_id_type=pl.DeviceIdType.MESH,
        )
        copy.start()
        return copy

    loads = {}
    for index, name in enumerate(FRONT_LOADS):
        place = held[name]
        if name == N.w_in:
            place = w_own.at[0 : 3 * width]
        elif name == N.w_out:
            place = w_own.at[3 * width :]
        elif name == N.w3:
            place = made[N.w_last].at[0]
        loads[name] = pltpu.make_async_copy(source[name], place, load_sem.at[index])
        loads[name].start()
    stores = {}

    def put(name, src, dst):
        stores[name] = pltpu.make_async_copy(src, dst, store_sem.at[STORES.index(name)])
        stores[name].start()

    barrier = pltpu.get_barrier_semaphore()
    for to in greeted:
        pl.semaphore_signal(barrier, inc=1, device_id=to, device_id_type=pl.DeviceIdType.MESH)
    pl.semaphore_wait(barrier, len(greeted))

    normed, w_peer, par = made[N.normed], made[N.w_peer], made[N.par]
    loads[N.w_in].wait()
    loads[N.w_out].wait()
    pieces = 3
    share = 4 * width // (2 * pieces)
    copies = {}

    def weight_rows(piece):
        return pl.ds(pl.multiple_of((2 * piece + group % 2) * share, 16), share)

    for piece in range(pieces):
        rows = weight_rows(piece)
        copies[N.wy, piece] = remote((N.wy, piece), w_own.at[rows], w_peer.at[rows], over)

    def pass_on(piece):
        copies[N.wy, piece].wait()
        rows = weight_rows(piece)
        copies[N.wx, piece] = remote((N.wx, piece), w_peer.at[rows], w_peer.at[rows], beside)

    for name in (N.tokens, N.g1, N.b1, N.ob, N.g2, N.b2, N.upb):
        loads[name].wait()
    for index, name in enumerate((N.g1, N.b1, N.ob, N.g2, N.b2, N.upb)):
        norms[index : index + 1, :] = held[name][...][None, :]

    def norm_one(index, carry):
        rows = pl.ds(pl.multiple_of(index * ROWS, ROWS), ROWS)
        values = normed_parts(held[N.tokens][rows, :].astype(full))[0]
        normed[mine_at(index * ROWS, ROWS), :] = (values * norms[0:1, :] + norms[1:2, :]).astype(low)
        return carry

    lax.fori_loop(0, half // ROWS, norm_one, 0)
    copies[N.norm] = remote(N.norm, normed.at[mine], normed.at[mine], across)

    for name in (N.cw, N.ib, N.cb, N.fb, N.w3):
        loads[name].wait()
    lines[...] = jnp.zeros_like(lines)
    lines[0:9, :] = held[N.cw][...].reshape(9, width)
    lines[9:12, :] = held[N.ib][...]
    lines[12:15, :] = held[N.cb][...]
    lines[15:16, :] = held[N.fb][...][None, :]
    channel = (part * width + lax.broadcasted_iota(jnp.int32, (1, width), 1)).astype(full)
    channels = 4 * width
    lines[16:17, :] = (slow_rate + (fast_rate - slow_rate) / (channels - 1) * channel) * (1.0 / (length - 1))
    par[0:width, 0:24] = jnp.transpose(lines[...])
    copies[N.par] = remote(N.par, par.at[0:width], par.at[width:], over)
    copies[N.w3] = remote(N.w3, made[N.w_last].at[0], made[N.w_last].at[1], over)

    loads[N.cot].wait()
    slot = part * half // length
    mask_rows = jnp.where(slot < counts[0], lengths[0, slot], 0) - part * half % length

    def mask_cot(index, carry):
        rows = pl.ds(pl.multiple_of(index * ROWS, ROWS), ROWS)
        place = lax.broadcasted_iota(jnp.int32, (ROWS, model_width), 0) + index * ROWS
        values = held[N.cot][rows, :]
        cot_near[mine_at(index * ROWS, ROWS), :] = jnp.where(
            place < mask_rows, values.astype(full), 0.0
        ).astype(low)
        return carry

    lax.fori_loop(0, half // ROWS, mask_cot, 0)
    copies[N.coty] = remote(N.coty, cot_near.at[mine], cot_far.at[mine], over)

    loads[N.seeds].wait()
    seeds, table = held[N.seeds], made[N.table]
    lows = low_turns.shape[1]

    def turn_by(turns, start, row):
        cos_row, sin_row = seeds[0, row : row + 1, :], seeds[1, row : row + 1, :]
        cos_part, sin_part = turns[0, 0:start, :], turns[1, 0:start, :]
        turns[0, start : 2 * start, :] = cos_part * cos_row - sin_part * sin_row
        turns[1, start : 2 * start, :] = sin_part * cos_row + cos_part * sin_row

    low_turns[:, 0:8, :] = seeds[:, 0:8, :]
    high_turns[:, 0:1, :] = seeds[:, 0:1, :]
    start, row = 8, 8
    while start < lows:
        turn_by(low_turns, start, row)
        start, row = 2 * start, row + 1
    start = 1
    while start < length // lows:
        turn_by(high_turns, start, row)
        start, row = 2 * start, row + 1
    feat = made[N.feat]
    bands = (feat.shape[0] - 1) // 2
    feat[0:1, :] = lax.broadcasted_iota(jnp.int32, (1, length), 1).astype(full) * (1.0 / (length - 1))
    for band in range(1, bands + 1):
        turns, index = (low_turns, 2 * band) if 2 * band < lows else (high_turns, 2 * band // lows)
        feat[band : band + 1, :] = turns[0, index : index + 1, :]
        feat[bands + band : bands + band + 1, :] = -turns[1, index : index + 1, :]
    put(N.feat, feat, target[N.feat])
    for high in range(length // lows):
        cos_high, sin_high = high_turns[0, high : high + 1, :], high_turns[1, high : high + 1, :]
        cos_low, sin_low = low_turns[0], low_turns[1]
        rows = slice(high * lows, (high + 1) * lows)
        table[0, rows, :] = (cos_high * cos_low - sin_high * sin_low).astype(low)
        sines = sin_high * cos_low + cos_high * sin_low
        if high == 0:
            place = lax.broadcasted_iota(jnp.int32, sines.shape, 1)
            first = lax.broadcasted_iota(jnp.int32, sines.shape, 0) == 0
            sines = jnp.where(first, (1 - 2 * (place % 2)).astype(full), sines)
        table[1, rows, :] = sines.astype(low)
    put(N.table, table, target[N.table])
    pass_on(0)
    cos, sin = table.at[0], table.at[1]

    for name in (N.fw1, N.fw2, N.fb1, N.ff1, N.fb2, N.ff2):
        loads[name].wait()

    def exact_tn(left, right):
        return lax.dot_general(
            left, right, (((0,), (0,)), ((), ())), precision=highest, preferred_element_type=full
        )

    filt = made[N.filt]
    units = held[N.fw2].shape[0]
    fcol[...] = jnp.zeros_like(fcol)
    for index, name in enumerate((N.ff1, N.ff2, N.fb1, N.fb2)):
        fcol[index : index + 1, 0:units] = held[name][...][None, :]
    freq = made[N.freq]
    freq[...] = jnp.zeros_like(freq)
    freq[:, 0:8] = jnp.transpose(fcol[...])[0:units, :]
    fcol = freq[...]
    put(N.freq, freq, target[N.freq])
    sum_one = exact_tn(held[N.fw1][...], feat[...]) + column(fcol, 2)
    angle = column(fcol, 0) * sum_one
    filt[0] = jnp.sin(angle)
    filt[2] = jnp.cos(angle)
    filt[4] = sum_one
    sum_two = exact_tn(held[N.fw2][...], filt[0]) + column(fcol, 3)
    angle = column(fcol, 1) * sum_two
    filt[1] = jnp.sin(angle)
    filt[3] = jnp.cos(angle)
    filt[5] = sum_two
    put(N.filt, filt, target[N.filt])
    pass_on(1)

    lanes = lax.broadcasted_iota(jnp.int32, (CHUNK, length), 1)
    first_lane = lanes == 0
    scale = jnp.where(first_lane, 0.5 / length, 1.0 / length)
    proj, signal, factor, conv = made[N.proj], made[N.signal], made[N.factor], made[N.conv]
    streams = made[N.streams]

    def forward(side_index, weight):
        base = side_index * width
        span = slice(base, base + width)

        def keep(name):
            place = target[name].at[span] if name == N.conv else target[name].at[:, span]
            put((name, side_index), made[name], place)

        def free(*names):
            if side_index == 1:
                for name in names:
                    stores.pop((name, 0)).wait()

        real[...] = exact_tn(made[N.w_last][side_index], filt[1])

        def windowed(index, carry):
            rows = pl.ds(pl.multiple_of(index * CHUNK, CHUNK), CHUNK)
            params = par[pl.ds(pl.multiple_of(base + index * CHUNK, CHUNK), CHUNK), :]
            pair_a[rows, :] = (
                real[rows, :] * jnp.exp(-lanes.astype(full) * column(params, 16))
            ).astype(low)
            return carry

        lax.fori_loop(0, width // CHUNK, windowed, 0)
        free(N.factor)
        factor[0] = dot_nn(pair_a[...], cos[...])
        factor[1] = dot_nt(pair_a[...], sin[...])
        keep(N.factor)
        if side_index == 0:
            pass_on(2)
        free(N.streams, N.proj)
        for i in range(3):
            streams[i] = dot_nt(weight[i * width : (i + 1) * width, :], normed[...]) + column(
                par[base : base + width, :], 9 + i
            )

        def mixing(index, carry):
            rows = pl.ds(pl.multiple_of(index * CHUNK, CHUNK), CHUNK)
            params = par[pl.ds(pl.multiple_of(base + index * CHUNK, CHUNK), CHUNK), :]

            def stream(i):
                line = streams[i, rows, :]
                proj[i, rows, :] = line.astype(low)
                total = column(params, 12 + i) + sum(
                    column(params, 3 * j + i) * shifted(line, j, lanes) for j in range(3)
                )
                streams[i, rows, :] = total
                return total

            stream(0)
            mixed_in = stream(1) * stream(2)
            inner[rows, :] = mixed_in
            pair_a[rows, :] = mixed_in.astype(low)
            return carry

        lax.fori_loop(0, width // CHUNK, mixing, 0)
        keep(N.streams)
        keep(N.proj)
        free(N.signal)
        signal[0] = dot_nn(pair_a[...], cos[...])
        signal[1] = dot_nt(pair_a[...], sin[...])
        keep(N.signal)

        def product(index, carry):
            rows = pl.ds(pl.multiple_of(index * CHUNK, CHUNK), CHUNK)
            s_cos, s_sin = signal[0, rows, :] * scale, signal[1, rows, :] * scale
            f_cos, f_sin = factor[0, rows, :], factor[1, rows, :]
            f_last = jnp.where(first_lane, f_sin, f_cos)
            f_sin = jnp.where(first_lane, 0.0, f_sin)
            pair_a[rows, :] = (s_cos * f_cos - s_sin * f_sin).astype(low)
            pair_b[rows, :] = (s_cos * f_sin + s_sin * f_last).astype(low)
            return carry

        lax.fori_loop(0, width // CHUNK, product, 0)
        real[...] = dot_nn(pair_a[...], cos[...])
        real[...] += dot_nn(pair_b[...], sin[...])

        free(N.conv)

        def gating(index, carry):
            rows = pl.ds(pl.multiple_of(index * CHUNK, CHUNK), CHUNK)
            params = par[pl.ds(pl.multiple_of(base + index * CHUNK, CHUNK), CHUNK), :]
            lines = real[rows, :] + inner[rows, :] * column(params, 15)
            conv[rows, :] = lines
            pair_c[rows, :] = (lines * streams[0, rows, :]).astype(low)
            return carry

        lax.fori_loop(0, width // CHUNK, gating, 0)
        keep(N.conv)
        for start in range(0, length, 256):
            piece = dot_tn(pair_c[:, start : start + 256], weight[3 * width :, :])
            if side_index == 0:
                acc[start : start + 256, :] = piece
            else:
                acc[start : start + 256, :] += piece

    copies[N.norm].wait()
    copies[N.cotn] = remote(N.cotn, cot_near.at[mine], cot_near.at[mine], across)
    put(N.normed, normed, target[N.normed])
    forward(0, w_own)
    for name in (N.par, N.w3) + tuple((N.wx, piece) for piece in range(pieces)):
        copies[name].wait()
    put(N.w_peer, w_peer, target[N.w_peer])
    put(N.par, par, target[N.par])
    put(N.w_last, made[N.w_last], target[N.w_last])
    forward(1, w_peer)

    send_row[...] = acc[theirs, :].astype(low)
    copies[N.branch] = remote(N.branch, send_row, recv_branch, across)
    copies[N.branch].wait()
    residual, residual_grad, resid = made[N.residual], made[N.residual_grad], made[N.resid]

    def norm_two(chunk):
        def body(index, carry):
            start = chunk * tile + index * ROWS
            rows = pl.ds(pl.multiple_of(start, ROWS), ROWS)
            place = mine_at(start, ROWS)
            lines = (
                held[N.tokens][rows, :].astype(full)
                + acc[place, :]
                + recv_branch[rows, :].astype(full)
                + norms[2:3, :]
            )
            residual[rows, :] = lines
            mid_near[place, :] = (normed_parts(lines)[0] * norms[3:4, :] + norms[4:5, :]).astype(low)
            return carry

        lax.fori_loop(0, tile // ROWS, body, 0)
        place = mine_at(chunk * tile, tile)
        copies[N.midy, chunk] = remote((N.midy, chunk), mid_near.at[place], mid_far.at[place], over)

    norm_two(0)
    norm_two(1)
    copies[N.midn] = remote(N.midn, mid_near.at[mine], mid_near.at[mine], across)
    put(N.residual, residual, target[N.residual])
    copies[N.cotn].wait()
    for name in (N.up, N.down):
        loads[name].wait()
    up, down = held[N.up], held[N.down]

    def units(rows, mid, cot, hid, pg):
        act, slope = gelu_parts(dot_nn(mid[rows, :], up[...]) + norms[5:6, :])
        hid[rows, :] = act.astype(low)
        back = (dot_nt(cot[rows, :], down[...]) * slope).astype(low)
        pg[rows, :] = back
        return (dot_nt(back, up[...]), jnp.sum(back.astype(full), axis=0, keepdims=True))

    copies[N.midn].wait()

    def near(index, total):
        rows = pl.ds(pl.multiple_of(index * tile, tile), tile)
        product, found = units(rows, mid_near, cot_near, hid_near, pg_near)
        acc[rows, :] = product
        return total + found

    total = lax.fori_loop(0, length // tile, near, jnp.zeros((1, model_width), full))
    send_row[...] = acc[theirs, :].astype(low)
    copies[N.near] = remote(N.near, send_row, recv_near, across)

    copies[N.coty].wait()
    copies[N.cotf] = remote(N.cotf, cot_far.at[mine], cot_far.at[mine], across)
    copies[N.midy, 0].wait()
    place = mine_at(0, tile)
    copies[N.midf, 0] = remote((N.midf, 0), mid_far.at[place], mid_far.at[place], across)
    copies[N.cotf].wait()
    for chunk in range(2):
        copies[N.midf, chunk].wait()
        product, found = units(theirs_at(chunk * tile, tile), mid_far, cot_far, hid_far, pg_far)
        total = total + found
        span = slice(chunk * tile, (chunk + 1) * tile)
        send_far[span, :] = product.astype(low)
        copies[N.farx, chunk] = remote((N.farx, chunk), send_far.at[span], recv_far.at[span], across)
        product, found = units(mine_at(chunk * tile, tile), mid_far, cot_far, hid_far, pg_far)
        total = total + found
        if chunk == 0:
            copies[N.midy, 1].wait()
            place = mine_at(tile, tile)
            copies[N.midf, 1] = remote((N.midf, 1), mid_far.at[place], mid_far.at[place], across)
        copies[N.farx, chunk].wait()
        send_back[span, :] = (product + recv_far[span, :].astype(full)).astype(low)
        copies[N.back, chunk] = remote((N.back, chunk), send_back.at[span], recv_back.at[span], over)

    part_rows = model_width // 2

    def weight_grads(name, recv, path, left, right):
        grads = made[name]

        def body(piece, carry):
            span = pl.ds(pl.multiple_of(piece * 256, 256), 256)
            product = dot_tn(left[0][:, span], right[0][...]) + dot_tn(left[1][:, span], right[1][...])
            in_order[span, :] = product.astype(low)
            return carry

        lax.fori_loop(0, model_width // 256, body, 0)
        block_rows = model_width // BLOCKS
        for start in range(0, model_width, block_rows):
            store_rows(grads, start, in_order[start : start + block_rows, :], block_rows, PATHS[path])
        bit = PATHS[path][0]
        sent = grads.at[pl.ds(pl.multiple_of((1 - bits[bit]) * part_rows, part_rows), part_rows)]
        kept = grads.at[pl.ds(pl.multiple_of(bits[bit] * part_rows, part_rows), part_rows)]
        short = N.up if path == 0 else N.down
        copies[short] = remote(short, sent, made[recv], flips[bit])
        put(name, kept, target[name])

    weight_grads(N.up_g, N.up_r, 0, (mid_near, mid_far), (pg_near, pg_far))
    weight_grads(N.down_g, N.down_r, 1, (cot_near, cot_far), (hid_near, hid_far))
    copies[N.near].wait()
    down_near, down_far = made[N.down_near], made[N.down_far]

    def down_rows(hid, place, store):
        def body(index, carry):
            rows = pl.ds(pl.multiple_of(index * tile, tile), tile)
            store(rows, dot_nn(hid[place(index * tile, tile), :], down[...]))
            return carry

        lax.fori_loop(0, 2, body, 0)

    def to_send(rows, values):
        send_row[rows, :] = values.astype(low)

    def to_near(rows, values):
        down_near[rows, :] = values

    def to_far(rows, values):
        down_far[rows, :] = (values + recv_down_far[rows, :].astype(full)).astype(low)

    down_rows(hid_far, theirs_at, to_send)
    copies[N.downf] = remote(N.downf, send_row, recv_down_far, across)
    made[N.upb_g][0:1, :] = total
    down_rows(hid_near, mine_at, to_near)
    copies[N.downf].wait()
    down_rows(hid_far, mine_at, to_far)
    put(N.down_far, down_far, target[N.down_far])
    down_rows(hid_near, theirs_at, to_send)
    copies[N.downn] = remote(N.downn, send_row, recv_down_near, across)
    copies[N.downn].wait()
    down_near[...] += recv_down_near[...].astype(full)
    put(N.down_near, down_near, target[N.down_near])

    sums = [jnp.zeros((1, model_width), full)] * 4
    sums = tuple(sums)
    for chunk in range(2):
        copies[N.back, chunk].wait()

        def body(index, carry):
            start = chunk * tile + index * ROWS
            rows = pl.ds(pl.multiple_of(start, ROWS), ROWS)
            place = mine_at(start, ROWS)
            normed_rows, inverse = normed_parts(residual[rows, :])
            back = acc[place, :] + recv_near[rows, :].astype(full) + recv_back[rows, :].astype(full)
            cots = cot_near[place, :].astype(full)
            grad = cots + norm_rows_back(back, normed_rows, inverse, norms[3:4, :])
            residual_grad[rows, :] = grad
            rounded = grad.astype(low)
            resid[rows, :] = rounded
            found = (rounded.astype(full), back * normed_rows, back, cots)
            return tuple(a + jnp.sum(b, axis=0, keepdims=True) for a, b in zip(carry, found))

        sums = lax.fori_loop(0, tile // ROWS, body, sums)
    extra = made[N.extra]
    for index in range(4):
        extra[index : index + 1, :] = sums[index]
    put(N.resid, resid, target[N.resid])
    put(N.residual_grad, residual_grad, target[N.residual_grad])
    put(N.extra, extra, target[N.extra])
    put(N.upb_g, made[N.upb_g], target[N.upb_g])
    for short, name in ((N.up, N.up_r), (N.down, N.down_r)):
        copies[short].wait()
        put(name, made[name], target[name])
    for copy in stores.values():
        copy.wait()


def call_operator_front(operands, counts, lengths, width, length, model_width, dp_step):
    full, low = jnp.float32, jnp.bfloat16
    half = length // 2
    channels = 2 * width
    units = operands[N.fw2].shape[0]
    shapes = {
        N.proj: ((3, channels, length), low),
        N.streams: ((3, channels, length), full),
        N.signal: ((2, channels, length), full),
        N.factor: ((2, channels, length), full),
        N.conv: ((channels, length), full),
        N.normed: ((length, model_width), low),
        N.w_peer: ((4 * width, model_width), low),
        N.par: ((channels, 128), full),
        N.table: ((2, length, length), low),
        N.filt: ((6, units, length), full),
        N.w_last: ((2, units, width), full),
        N.resid: ((half, model_width), low),
        N.residual_grad: ((half, model_width), full),
        N.residual: ((half, model_width), full),
        N.up_g: ((model_width // 2, model_width), low),
        N.down_g: ((model_width // 2, model_width), low),
        N.up_r: ((model_width // 2, model_width), low),
        N.down_r: ((model_width // 2, model_width), low),
        N.down_near: ((half, model_width), full),
        N.down_far: ((half, model_width), low),
        N.extra: ((8, model_width), full),
        N.upb_g: ((8, model_width), full),
        N.freq: ((units, 128), full),
        N.feat: ((operands[N.fw1].shape[0], length), full),
    }
    split = {
        N.proj: (3, width, length),
        N.streams: (3, width, length),
        N.signal: (2, width, length),
        N.factor: (2, width, length),
        N.conv: (width, length),
        N.up_g: (model_width, model_width),
        N.down_g: (model_width, model_width),
    }
    placed = {N.w_in: (16, 128), N.w_out: (16, 128), N.w3: (8, 128)}
    rows = pltpu.VMEM((length, model_width), low)
    half_rows = pltpu.VMEM((half, model_width), low)
    wide, thin = pltpu.VMEM((width, length), full), pltpu.VMEM((width, length), low)
    scratch = [
        pltpu.VMEM(placed.get(name, operands[name].shape), operands[name].dtype) for name in FRONT_LOADS
    ]
    scratch += [pltpu.VMEM(split.get(name, shapes[name][0]), shapes[name][1]) for name in FRONT_OUTS]
    scratch += [rows] * 8 + [pltpu.VMEM((length, model_width), full)] + [wide] * 2 + [thin] * 3
    scratch += [half_rows] * 9
    scratch += [
        pltpu.VMEM((4 * width, model_width), low),
        pltpu.VMEM((8, model_width), full),
        pltpu.VMEM((24, width), full),
        pltpu.VMEM((8, 128), full),
        pltpu.VMEM((2, 1 << (length.bit_length() // 2), length), full),
        pltpu.VMEM((2, length >> (length.bit_length() // 2), length), full),
        pltpu.VMEM((model_width, model_width), low),
        pltpu.SemaphoreType.DMA((len(FRONT_LOADS),)),
        pltpu.SemaphoreType.DMA((len(STORES),)),
        pltpu.SemaphoreType.DMA((len(FRONT_PLAN),)),
        pltpu.SemaphoreType.DMA((len(FRONT_PLAN),)),
    ]
    results = pl.pallas_call(
        functools.partial(operator_front, dp_step),
        out_shape=tuple(jax.ShapeDtypeStruct(*shapes[name]) for name in FRONT_OUTS),
        in_specs=[pl.BlockSpec(memory_space=pl.ANY)] * len(FRONT_LOADS)
        + [pl.BlockSpec(memory_space=pltpu.SMEM)] * 2,
        out_specs=tuple(pl.BlockSpec(memory_space=pl.ANY) for name in FRONT_OUTS),
        scratch_shapes=scratch,
        compiler_params=pltpu.CompilerParams(
            vmem_limit_bytes=63 * 1024 * 1024, collective_id=1, has_side_effects=True
        ),
        name="operator_front",
    )(*(operands[name] for name in FRONT_LOADS), counts, lengths)
    return dict(zip(FRONT_OUTS, results))


PLAN = (N.resid, N.downy, N.peer_a, N.peer_b, N.y_a, N.y_b, N.chan, N.first) + tuple(
    (name, hop) for name in (N.up, N.down, N.a, N.b, N.chan) for hop in (1, 2, 3) if hop > 1 or name not in (N.up, N.down)
) + tuple((N.shared, hop) for hop in range(5))
LOADS = (N.resid, N.w_peer, N.up, N.up_r, N.down, N.down_r, N.w_in, N.w_out, N.streams, N.proj, N.conv, N.par,
         N.normed, N.table, N.factor, N.signal, N.filt, N.w_last, N.w_mid, N.feat, N.freq, N.tokens, N.gain,
         N.rgrad, N.extra, N.upb, N.residual, N.down_near, N.down_bias)
SPLIT = (N.streams, N.proj, N.conv, N.factor, N.signal)


def operator_back(dp_step, outs, *refs):
    sizes = len(LOADS)
    source = dict(zip(LOADS, refs[:sizes]))
    down_far, counts, lengths = refs[sizes : sizes + 3]
    refs = refs[:sizes] + refs[sizes + 3 :]
    out = dict(zip(outs, refs[sizes : sizes + len(outs)]))
    refs = refs[sizes + len(outs) :]
    held = dict(zip(LOADS, refs[: len(LOADS)]))
    refs = refs[len(LOADS) :]
    (grad, real, imag, pair_a, pair_b, pair_c, pair_d, stack, proj_low, h_grad, first, first_send, first_recv,
     peer_a, peer_b, beside_a, beside_b, send_a, send_b, recv_a, recv_b, sum_a, sum_b, recv_down, sums, chan_peer, chan_recv, chan, chan_hops,
     shared, shared_hops, w_own) = refs[:32]
    hops = dict(zip((N.up, N.down, N.a, N.b), (refs[32 + 5 * i : 37 + 5 * i] for i in range(4))))
    load_sem, send_sem, recv_sem = refs[52:]
    full, low = jnp.float32, jnp.bfloat16

    part = lax.axis_index(TENSOR)
    group = lax.axis_index(DP)
    side = part % 2
    bits = [(group // (dp_step << b)) % 2 for b in range(3)]
    across = {TENSOR: other_of(part, 1)}
    over = {TENSOR: other_of(part, 2)}
    flips = [{DP: other_of(group, dp_step << b)} for b in range(3)]

    def remote(name, src, dst, target):
        index = PLAN.index(name)
        return pltpu.make_async_remote_copy(
            src_ref=src,
            dst_ref=dst,
            send_sem=send_sem.at[index],
            recv_sem=recv_sem.at[index],
            device_id=target,
            device_id_type=pl.DeviceIdType.MESH,
        )

    width, length = grad.shape
    model_width = first.shape[1]
    half_rows = length // 2
    block_rows = model_width // BLOCKS
    mine = pl.ds(pl.multiple_of(side * half_rows, half_rows), half_rows)
    theirs = pl.ds(pl.multiple_of((1 - side) * half_rows, half_rows), half_rows)

    places = dict(held)
    places[N.resid] = held[N.resid].at[mine]
    places[N.w_in] = w_own.at[0 : 3 * width]
    places[N.w_out] = w_own.at[3 * width :]
    loads = {}

    def load(name, half):
        src, dst, index = source[name], places[name], LOADS.index(name)
        key = name
        if half is not None:
            span = slice(half * width, (half + 1) * width)
            if name == N.conv:
                src, dst = src.at[span], dst.at[span]
            else:
                src, dst = src.at[:, span], dst.at[:, span]
            key = (name, half)
            index = index if half == 1 else len(LOADS) + SPLIT.index(name)
        loads[key] = pltpu.make_async_copy(src, dst, load_sem.at[index])
        loads[key].start()

    late = LOADS.index(N.w_mid)
    for name in LOADS[:late]:
        load(name, 1 if name in SPLIT else None)
    for name in SPLIT:
        load(name, 0)
    for name in LOADS[late:]:
        load(name, None)

    barrier = pltpu.get_barrier_semaphore()
    for target in [across, over] + flips:
        pl.semaphore_signal(barrier, inc=1, device_id=target, device_id_type=pl.DeviceIdType.MESH)
    pl.semaphore_wait(barrier, 5)

    resid = held[N.resid]
    resid_copy = remote(N.resid, source[N.resid], resid.at[mine], across)
    resid_copy.start()
    loads[N.resid].wait()
    loads[N.w_peer].wait()
    resid_copy.wait()

    def spot(index, size):
        return pl.ds(pl.multiple_of(index * size, size), size)

    def order_of(name):
        return PATHS[1] if name == N.down else PATHS[0]

    def hop_one(name, grads):
        bit = order_of(name)[0]
        src = grads.at[spot(1 - bits[bit], 4 * block_rows)]
        copy = remote((name, 1), src, hops[name][0], flips[bit])
        copy.start()
        return copy

    def hop_two(name, grads, copy, recv_one):
        _, send_two, keep_two, recv_two, _ = hops[name]
        top, bit, _ = order_of(name)
        whole = copy is not None
        if whole:
            copy.wait()
        crossed = {N.a: recv_a, N.b: recv_b}.get(name)
        for keep in (0, 1):
            pick = bits[bit] if keep else 1 - bits[bit]
            first_place = 2 * bits[top] + pick if whole else pick
            total = (
                grads[spot(first_place, 2 * block_rows), :].astype(full)
                + recv_one[spot(pick, 2 * block_rows), :].astype(full)
            )
            if crossed is not None:
                total = total + crossed[spot(pick, 2 * block_rows), :].astype(full)
            if keep:
                keep_two[...] = total
            else:
                send_two[...] = total.astype(low)
                copy = remote((name, 2), send_two, recv_two, flips[bit])
                copy.start()
        return copy

    def hop_three(name, copy):
        recv_one, send_two, keep_two, recv_two, recv_three = hops[name]
        bit = order_of(name)[2]
        copy.wait()
        place = spot(1 - bits[bit], block_rows)
        send_two[0:block_rows, :] = (keep_two[place, :] + recv_two[place, :].astype(full)).astype(low)
        copy = remote((name, 3), send_two.at[0:block_rows], recv_three, flips[bit])
        copy.start()
        return copy

    def hop_last(name, copy):
        recv_one, send_two, keep_two, recv_two, recv_three = hops[name]
        copy.wait()
        place = spot(bits[order_of(name)[2]], block_rows)
        return keep_two[place, :] + recv_two[place, :].astype(full) + recv_three[...].astype(full)

    copies = {N.downy: remote(N.downy, down_far, recv_down, over)}
    copies[N.downy].start()
    for name in (N.up, N.up_r, N.down, N.down_r):
        loads[name].wait()
    for name, received in ((N.up, N.up_r), (N.down, N.down_r)):
        copies[name] = hop_two(name, held[name], None, held[received])

    lanes = lax.broadcasted_iota(jnp.int32, (CHUNK, length), 1)
    par, streams, proj, conv = held[N.par], held[N.streams], held[N.proj], held[N.conv]
    cos, sin = held[N.table].at[0], held[N.table].at[1]
    factor, signal, normed = held[N.factor], held[N.signal], held[N.normed]
    filt = held[N.filt]
    weights = (w_own, held[N.w_peer])

    def half_pass(half, loaded, early, middle):
        base = half * width
        weight = weights[half]
        own_w = 3 * width

        def at(index):
            return pl.ds(pl.multiple_of(index * CHUNK, CHUNK), CHUNK)

        def far(index):
            return pl.ds(pl.multiple_of(base + index * CHUNK, CHUNK), CHUNK)

        def stream_back(i, index, params, back):
            moved = [shifted(back, -j, lanes) for j in range(3)]
            out = sum(column(params, 3 * j + i) * moved[j] for j in range(3)).astype(low)
            line = proj[i, far(index), :].astype(full)
            start = pl.multiple_of(i * width + index * CHUNK, CHUNK)
            proj_low[pl.ds(start, CHUNK), :] = out
            found = [(3 * j + i, jnp.sum(moved[j] * line, axis=1, keepdims=True)) for j in range(3)]
            found.append((9 + i, jnp.sum(out.astype(full), axis=1, keepdims=True)))
            found.append((12 + i, jnp.sum(back, axis=1, keepdims=True)))
            return found

        grad[...] = dot_nt(weight[own_w:, :], resid[...])
        for name in (N.streams, N.proj, N.conv):
            loads[name, half].wait()
        if not loaded:
            loads[N.par].wait()

        def before(index, carry):
            rows = far(index)
            params = par[rows, :]
            gate_out, gate_in, values = streams[0, rows, :], streams[1, rows, :], streams[2, rows, :]
            mixed_grad = grad[at(index), :]
            conv_part = conv[rows, :]
            conv_grad = mixed_grad * gate_out
            grad[at(index), :] = conv_grad
            pair_a[at(index), :] = conv_grad.astype(low)
            pair_b[at(index), :] = (conv_part * gate_out).astype(low)
            found = stream_back(0, index, params, mixed_grad * conv_part)
            found.append((15, jnp.sum(conv_grad * values * gate_in, axis=1, keepdims=True)))
            sums[at(index), :] = pack_columns(found, CHUNK)
            return carry

        lax.fori_loop(0, width // CHUNK, before, 0)
        if not loaded:
            loads[N.normed].wait()
        stack[0:width, :] = dot_nn(proj_low[0:width, :], normed[...])
        stack[width : 2 * width, :] = dot_nn(pair_b[...], resid[...])
        early()
        if not loaded:
            loads[N.table].wait()
        real[...] = dot_nn(pair_a[...], cos[...])
        imag[...] = dot_nt(pair_a[...], sin[...])
        loads[N.factor, half].wait()
        loads[N.signal, half].wait()
        first_lane = lanes == 0
        scale = jnp.where(first_lane, 0.5 / length, 1.0 / length)

        def between(index, carry):
            rows, place = far(index), at(index)
            cos_part, sin_part = real[place, :] * scale, imag[place, :] * scale
            f_cos, f_sin = factor[0, rows, :], factor[1, rows, :]
            f_last = jnp.where(first_lane, f_sin, f_cos)
            f_sin = jnp.where(first_lane, 0.0, f_sin)
            pair_a[place, :] = (cos_part * f_cos + sin_part * f_sin).astype(low)
            pair_b[place, :] = (sin_part * f_last - cos_part * f_sin).astype(low)
            s_cos, s_sin = signal[0, rows, :], signal[1, rows, :]
            s_last = jnp.where(first_lane, s_sin, s_cos)
            s_sin = jnp.where(first_lane, 0.0, s_sin)
            pair_c[place, :] = (cos_part * s_cos + sin_part * s_sin).astype(low)
            pair_d[place, :] = (sin_part * s_last - cos_part * s_sin).astype(low)
            return carry

        lax.fori_loop(0, width // CHUNK, between, 0)
        middle()
        real[...] = dot_nn(pair_a[...], cos[...]) + dot_nn(pair_b[...], sin[...])
        imag[...] = dot_nn(pair_c[...], cos[...]) + dot_nn(pair_d[...], sin[...])

        def after(index, carry):
            rows = far(index)
            params = par[rows, :]
            gate_in, values = streams[1, rows, :], streams[2, rows, :]
            back = real[at(index), :] + grad[at(index), :] * column(params, 15)
            found = stream_back(1, index, params, back * values)
            found += stream_back(2, index, params, back * gate_in)
            sums[at(index), :] = sums[at(index), :] + pack_columns(found, CHUNK)
            window = jnp.exp(-lanes.astype(full) * column(params, 16))
            pair_a[at(index), :] = (imag[at(index), :] * window).astype(low)
            return carry

        lax.fori_loop(0, width // CHUNK, after, 0)
        if not loaded:
            for name in (N.filt, N.w_last):
                loads[name].wait()
        stack[2 * width :, :] = dot_nn(proj_low[width:, :], normed[...])
        target = chan_peer if half == 1 else chan
        target[0:16, :] = jnp.transpose(sums[...])[0:16, :]
        target[16:80, :] = dot_nt(filt[1].astype(low), pair_a[...])
        h_part = dot_nn(held[N.w_last][half].astype(low), pair_a[...])
        if half == 1:
            h_grad[...] = h_part
        else:
            h_grad[...] += h_part

    def turned(part_index, ref):
        middle = model_width // 2
        rows = slice(part_index * middle, (part_index + 1) * middle)
        for start in range(0, model_width, 128):
            block = jnp.transpose(stack[rows, start : start + 128]).astype(low)
            store_rows(ref, start, block, block_rows, PATHS[0])

    peers = ((N.peer_a, peer_a, beside_a, send_a), (N.peer_b, peer_b, beside_b, send_b))

    def peer_first(part_index):
        name, grads, beside, _ = peers[part_index]
        turned(part_index, grads)
        src = grads.at[spot(1 - bits[0], 4 * block_rows)]
        copies[name] = remote(name, src, beside, flips[0])
        copies[name].start()

    def peer_cross(part_index):
        name, grads, beside, sent = peers[part_index]
        across_name, crossed = ((N.y_a, recv_a), (N.y_b, recv_b))[part_index]
        copies[name].wait()
        kept = grads[spot(bits[0], 4 * block_rows), :].astype(full)
        sent[...] = (kept + beside[...].astype(full)).astype(low)
        copies[across_name] = remote(across_name, sent, crossed, over)
        copies[across_name].start()

    def first_part(half):
        for start in range(0, length, 256):
            product = dot_tn(proj_low[:, start : start + 256], weights[half][: 3 * width, :])
            if half == 1:
                first[start : start + 256, :] = product
            else:
                first[start : start + 256, :] += product

    def last_hops():
        for name in (N.up, N.down):
            copies[name] = hop_three(name, copies[name])

    half_pass(1, False, lambda: peer_first(0), last_hops)
    peer_first(1)
    chan_peer[80:88, :] = jnp.zeros((8, width), full)
    copies[N.chan] = remote(N.chan, chan_peer, chan_recv, over)
    copies[N.chan].start()
    first_part(1)
    loads[N.w_in].wait()
    loads[N.w_out].wait()
    peer_cross(0)

    def own_first():
        turned(0, sum_a)
        copies[N.a] = hop_one(N.a, sum_a)

    half_pass(0, True, own_first, lambda: peer_cross(1))
    first_part(0)
    first_send[...] = first[theirs, :].astype(low)
    first_copy = remote(N.first, first_send, first_recv, across)
    first_copy.start()
    turned(1, sum_b)
    copies[N.b] = hop_one(N.b, sum_b)
    copies[N.y_a].wait()
    copies[N.a] = hop_two(N.a, sum_a, copies[N.a], hops[N.a][0])

    copies[N.chan].wait()
    loads[N.upb].wait()
    chan[0:80, :] = chan[0:80, :] + chan_recv[0:80, :]
    chan[80:88, :] = jnp.zeros((8, width), full)
    for index in range(held[N.upb].shape[1] // width):
        chan[80 + index : 81 + index, :] = held[N.upb][0:1, index * width : (index + 1) * width]
    chan_copy = remote((N.chan, 1), chan, chan_hops.at[0], flips[0])
    chan_copy.start()

    for name in (N.w_mid, N.feat, N.freq):
        loads[name].wait()
    freq, w_mid = held[N.freq], held[N.w_mid]
    shared[...] = jnp.zeros_like(shared)
    units = w_mid.shape[0]
    feats = held[N.feat].shape[0]
    slope = h_grad[...] * filt[3]
    q_two = jnp.sum(slope * filt[5], axis=1, keepdims=True)
    slope = slope * column(freq[...], 1)
    b_two = jnp.sum(slope, axis=1, keepdims=True)
    slope_low = slope.astype(low)
    shared[80 : 80 + units, 0:units] = dot_nt(filt[0].astype(low), slope_low)
    slope = dot_nn(w_mid[...].astype(low), slope_low) * filt[2]
    q_one = jnp.sum(slope * filt[4], axis=1, keepdims=True)
    slope = slope * column(freq[...], 0)
    b_one = jnp.sum(slope, axis=1, keepdims=True)
    shared[40 : 40 + feats, 0:units] = dot_nt(held[N.feat][...].astype(low), slope.astype(low))
    vectors = pack_columns([(0, b_one), (1, q_one), (2, b_two), (3, q_two)], units)
    shared[144:152, 0:units] = jnp.transpose(vectors)[0:8, :]

    for name in (N.tokens, N.gain, N.rgrad, N.extra):
        loads[name].wait()
    first_copy.wait()
    gain = held[N.gain][...][None, :]

    def norm_rows(index, carry):
        rows = pl.ds(pl.multiple_of(index * ROWS, ROWS), ROWS)
        own = pl.ds(pl.multiple_of(side * half_rows + index * ROWS, ROWS), ROWS)
        normed_rows, inverse = normed_parts(held[N.tokens][rows, :].astype(full))
        back = first[own, :] + first_recv[rows, :].astype(full)
        grad_rows = norm_rows_back(back, normed_rows, inverse, gain)
        out[N.input_grad][rows, :] = held[N.rgrad][rows, :] + grad_rows
        return (
            carry[0] + jnp.sum(back * normed_rows, axis=0, keepdims=True),
            carry[1] + jnp.sum(back, axis=0, keepdims=True),
        )

    zero = jnp.zeros((1, model_width), full)
    found = lax.fori_loop(0, half_rows // ROWS, norm_rows, (zero, zero))
    extra = held[N.extra]
    vectors = list(found) + [extra[i : i + 1, :] for i in range(4)]
    for index, vector in enumerate(vectors):
        for piece in range(model_width // 128):
            row = index * (model_width // 128) + piece
            shared[row : row + 1, :] = vector[:, piece * 128 : (piece + 1) * 128]

    shared_targets = [across, over] + flips

    def share(hop):
        copy = remote((N.shared, hop), shared, shared_hops.at[hop], shared_targets[hop])
        copy.start()
        return copy

    def shared_next(hop, copy):
        copy.wait()
        shared[...] = shared[...] + shared_hops[hop]
        return share(hop + 1) if hop < 4 else None

    def chan_next(hop, copy):
        copy.wait()
        chan[...] = chan[...] + chan_hops[hop]
        if hop == 2:
            return None
        copy = remote((N.chan, hop + 2), chan, chan_hops.at[hop + 1], flips[hop + 1])
        copy.start()
        return copy

    shared_copy = share(0)
    chan_copy = chan_next(0, chan_copy)
    copies[N.a] = hop_three(N.a, copies[N.a])
    shared_copy = shared_next(0, shared_copy)
    copies[N.y_b].wait()
    copies[N.b] = hop_two(N.b, sum_b, copies[N.b], hops[N.b][0])

    for name in (N.residual, N.down_near, N.down_bias):
        loads[name].wait()
    copies[N.downy].wait()
    slot = part * half_rows // length
    mask_rows = jnp.where(slot < counts[0], lengths[0, slot], 0) - part * half_rows % length
    down_bias = held[N.down_bias][...][None, :]

    def result_rows(index, carry):
        rows = pl.ds(pl.multiple_of(index * ROWS, ROWS), ROWS)
        total = held[N.residual][rows, :] + held[N.down_near][rows, :] + recv_down[rows, :].astype(full)
        place = lax.broadcasted_iota(jnp.int32, (ROWS, model_width), 0) + index * ROWS
        out[N.activations][rows, :] = jnp.where(place < mask_rows, total + down_bias, 0.0).astype(low)
        return carry

    lax.fori_loop(0, half_rows // ROWS, result_rows, 0)
    shared_copy = shared_next(1, shared_copy)
    chan_copy = chan_next(1, chan_copy)
    copies[N.b] = hop_three(N.b, copies[N.b])
    shared_copy = shared_next(2, shared_copy)
    for name in (N.up, N.down, N.a):
        out[name][...] = hop_last(name, copies[name])
    chan_next(2, chan_copy)
    shared_copy = shared_next(3, shared_copy)
    out[N.b][...] = hop_last(N.b, copies[N.b])
    shared_next(4, shared_copy)
    out[N.shared][...] = shared[...]
    out[N.chan][...] = chan[...]


PASSED = (N.activations, N.input_grad, N.up, N.down)


def lay_out(group_units, *refs):
    sources = dict(zip(RAW, refs[: len(RAW)]))
    outs = dict(zip(RESULTS, refs[len(RAW) : len(RAW) + len(RESULTS)]))
    held = dict(zip(RAW, refs[len(RAW) + len(RESULTS) : -1]))
    sem = refs[-1]
    group = lax.axis_index(DP)
    loads, passes = {}, []
    for index, name in enumerate(RAW):
        if name in PASSED:
            passes.append(pltpu.make_async_copy(sources[name], outs[name], sem.at[index]))
            passes[-1].start()
        else:
            loads[name] = pltpu.make_async_copy(sources[name], held[name], sem.at[index])
            loads[name].start()
    for copy in loads.values():
        copy.wait()
    part_a, part_b = jnp.transpose(held[N.a][...]), jnp.transpose(held[N.b][...])
    width = outs[N.out].shape[0]
    outs[N.in_w][0] = part_a[0:width, :]
    outs[N.in_w][1] = part_b[0:width, :]
    outs[N.in_w][2] = part_b[width:, :]
    outs[N.out][...] = part_a[width:, :]
    shared, chan = held[N.shared], held[N.chan]
    model_width = outs[N.up].shape[1]
    units = outs[N.w2].shape[0]
    pieces = model_width // 128
    for index, name in enumerate(WIDES):
        row = index * pieces
        lines = [shared[row + piece : row + piece + 1, :] for piece in range(pieces)]
        outs[name][...] = jnp.concatenate(lines, axis=1).reshape(model_width)
    outs[N.w1][...] = shared[40 : 40 + outs[N.w1].shape[0], 0:units]
    outs[N.w2][...] = shared[80 : 80 + units, 0:units]
    for index, name in enumerate(VECTORS):
        outs[name][...] = shared[144 + index : 145 + index, 0:units].reshape(units)
    outs[N.conv_w][...] = chan[0:9, :].reshape(3, 3, width)
    outs[N.in_b][...] = chan[9:12, :]
    outs[N.conv_b][...] = chan[12:15, :]
    outs[N.f_bias][...] = chan[15:16, :].reshape(width)
    lines = [chan[80 + index : 81 + index, :] for index in range(model_width // width)]
    outs[N.up_b][...] = jnp.concatenate(lines, axis=1).reshape(model_width)
    outs[N.w3][...] = chan[pl.ds(pl.multiple_of(16 + group * group_units, 8), group_units), :]
    for copy in passes:
        copy.wait()


def call_lay_out(raw, inputs_count, units, width):
    full, low = jnp.float32, jnp.bfloat16
    rows, model_width = raw[N.input_grad].shape
    block = raw[N.up].shape[0]
    shapes = {name: raw[name].shape for name in PASSED}
    shapes.update({name: (model_width,) for name in WIDES + (N.up_b,)})
    shapes.update({name: (units,) for name in VECTORS})
    shapes.update(
        {
            N.in_w: (3, width, block),
            N.out: (width, block),
            N.w1: (inputs_count, units),
            N.w2: (units, units),
            N.w3: (units // BLOCKS, width),
            N.conv_w: (3, 3, width),
            N.in_b: (3, width),
            N.conv_b: (3, width),
            N.f_bias: (width,),
        }
    )
    results = pl.pallas_call(
        functools.partial(lay_out, units // BLOCKS),
        out_shape=tuple(
            jax.ShapeDtypeStruct(shapes[name], low if name == N.activations else full) for name in RESULTS
        ),
        in_specs=[pl.BlockSpec(memory_space=pl.ANY)] * len(RAW),
        out_specs=tuple(pl.BlockSpec(memory_space=pltpu.VMEM) for name in RESULTS),
        scratch_shapes=[
            pltpu.VMEM((8, 128) if name in PASSED else raw[name].shape, full) for name in RAW
        ]
        + [pltpu.SemaphoreType.DMA((len(RAW),))],
        name="lay_out",
    )(*(raw[name] for name in RAW))
    return results


def call_operator_back(operands, counts, lengths, width, length, model_width, dp_count):
    full, low = jnp.float32, jnp.bfloat16
    units = operands[N.w_mid].shape[0]
    half_rows = length // 2
    block = model_width // BLOCKS
    thin_grads = pltpu.VMEM((model_width, model_width // 2), low)
    part_grads = pltpu.VMEM((model_width // 2, model_width // 2), low)
    low_rows = pltpu.VMEM((half_rows, model_width), low)
    held = []
    for name in LOADS:
        shape = operands[name].shape
        if name == N.resid:
            shape = (length, model_width)
        elif name in (N.w_in, N.w_out):
            shape = (16, 128)
        held.append(pltpu.VMEM(shape, operands[name].dtype))
    wide, thin = pltpu.VMEM((width, length), full), pltpu.VMEM((width, length), low)
    chan = pltpu.VMEM((88, width), full)
    shared = pltpu.VMEM((152, 128), full)
    scratch = held + [wide] * 3 + [thin] * 4
    scratch += [
        pltpu.VMEM((4 * width, model_width), full),
        pltpu.VMEM((3 * width, length), low),
        pltpu.VMEM((units, length), full),
        pltpu.VMEM((length, model_width), full),
        low_rows,
        low_rows,
        thin_grads,
        thin_grads,
        part_grads,
        part_grads,
        part_grads,
        part_grads,
        part_grads,
        part_grads,
        thin_grads,
        thin_grads,
        low_rows,
        pltpu.VMEM((width, 128), full),
        chan,
        chan,
        chan,
        pltpu.VMEM((3, 88, width), full),
        shared,
        pltpu.VMEM((5, 152, 128), full),
        pltpu.VMEM((4 * width, model_width), low),
    ]
    for columns in (model_width, model_width, model_width // 2, model_width // 2):
        scratch += [
            pltpu.VMEM((4 * block, columns), low),
            pltpu.VMEM((2 * block, columns), low),
            pltpu.VMEM((2 * block, columns), full),
            pltpu.VMEM((2 * block, columns), low),
            pltpu.VMEM((block, columns), low),
        ]
    scratch += [
        pltpu.SemaphoreType.DMA((len(LOADS) + len(SPLIT),)),
        pltpu.SemaphoreType.DMA((len(PLAN),)),
        pltpu.SemaphoreType.DMA((len(PLAN),)),
    ]
    shapes = {N.activations: (half_rows, model_width), N.input_grad: (half_rows, model_width)}
    shapes.update({N.up: (block, model_width), N.down: (block, model_width)})
    shapes.update({N.a: (block, model_width // 2), N.b: (block, model_width // 2)})
    shapes.update({N.shared: (152, 128), N.chan: (88, width)})
    outs = tuple(shapes)
    results = pl.pallas_call(
        functools.partial(operator_back, dp_count // BLOCKS, outs),
        out_shape=tuple(
            jax.ShapeDtypeStruct(shapes[name], low if name == N.activations else full) for name in outs
        ),
        in_specs=[pl.BlockSpec(memory_space=pl.ANY)] * (len(LOADS) + 1)
        + [pl.BlockSpec(memory_space=pltpu.SMEM)] * 2,
        out_specs=tuple(pl.BlockSpec(memory_space=pltpu.VMEM) for out in outs),
        scratch_shapes=scratch,
        compiler_params=pltpu.CompilerParams(
            vmem_limit_bytes=63 * 1024 * 1024, collective_id=0, has_side_effects=True
        ),
        cost_estimate=pl.CostEstimate(
            flops=4 * width * length * (10 * length + 8 * model_width),
            bytes_accessed=40 * 1024 * 1024,
            transcendentals=0,
        ),
        name="operator_back",
    )(*(operands[name] for name in LOADS), operands[N.down_far], counts, lengths)
    return dict(zip(outs, results))


def local(
    tokens,
    seq_counts,
    seq_lengths,
    norm1_gain,
    norm1_bias,
    in_weight,
    in_bias,
    conv_weight,
    conv_bias,
    filter_w1,
    filter_b1,
    filter_freq1,
    filter_w2,
    filter_b2,
    filter_freq2,
    filter_w3,
    filter_bias,
    out_weight,
    out_bias,
    norm2_gain,
    norm2_bias,
    up_weight,
    up_bias,
    down_weight,
    down_bias,
    cotangent,
):
    low = jnp.bfloat16
    full = jnp.float32
    tensor_count = lax.axis_size(TENSOR)
    dp_count = lax.axis_size(DP)
    row_share, model_width = tokens.shape
    width = in_weight.shape[1]
    slot_count = seq_lengths.shape[1]
    length = row_share * tensor_count // slot_count
    part = lax.axis_index(TENSOR)
    group = lax.axis_index(DP)

    inputs_count = filter_w1.shape[0]
    units = filter_w2.shape[0]
    flat_in = in_weight.reshape(3 * width, model_width)
    front = call_operator_front(
        {
            N.w_in: flat_in,
            N.w_out: out_weight,
            N.tokens: tokens,
            N.g1: norm1_gain,
            N.b1: norm1_bias,
            N.cw: conv_weight,
            N.ib: in_bias,
            N.cb: conv_bias,
            N.fb: filter_bias,
            N.w3: filter_w3,
            N.cot: cotangent,
            N.seeds: jnp.asarray(turn_seeds(length)),
            N.fw1: filter_w1,
            N.fw2: filter_w2,
            N.fb1: filter_b1,
            N.ff1: filter_freq1,
            N.fb2: filter_b2,
            N.ff2: filter_freq2,
            N.ob: out_bias,
            N.g2: norm2_gain,
            N.b2: norm2_bias,
            N.upb: up_bias,
            N.up: up_weight,
            N.down: down_weight,
        },
        seq_counts,
        seq_lengths,
        width,
        length,
        model_width,
        dp_count // BLOCKS,
    )
    back = call_operator_back(
        {
            N.resid: front[N.resid],
            N.w_peer: front[N.w_peer],
            N.w_in: flat_in,
            N.w_out: out_weight,
            N.streams: front[N.streams],
            N.proj: front[N.proj],
            N.conv: front[N.conv],
            N.par: front[N.par],
            N.table: front[N.table],
            N.factor: front[N.factor],
            N.signal: front[N.signal],
            N.normed: front[N.normed],
            N.filt: front[N.filt],
            N.w_last: front[N.w_last],
            N.up: front[N.up_g],
            N.down: front[N.down_g],
            N.up_r: front[N.up_r],
            N.down_r: front[N.down_r],
            N.down_far: front[N.down_far],
            N.w_mid: filter_w2,
            N.feat: front[N.feat],
            N.freq: front[N.freq],
            N.tokens: tokens,
            N.gain: norm1_gain,
            N.rgrad: front[N.residual_grad],
            N.extra: front[N.extra],
            N.upb: front[N.upb_g],
            N.residual: front[N.residual],
            N.down_near: front[N.down_near],
            N.down_bias: down_bias,
        },
        seq_counts,
        seq_lengths,
        width,
        length,
        model_width,
        dp_count,
    )
    if dp_count == BLOCKS:
        results = list(call_lay_out(back, inputs_count, units, width))
        place = RESULTS.index(N.down)
        results[place] = jnp.transpose(results[place])
        return tuple(results)

    rest = dp_count.bit_length() - BLOCKS.bit_length()

    def flips(bit_index):
        return [(i, i ^ (1 << bit_index)) for i in range(dp_count)]

    def rest_scatter(grad):
        for bit_index in range(rest):
            bit = (group >> bit_index) & 1
            kept = grad.reshape(1 << (rest - 1 - bit_index), 2, model_width // dp_count, -1)
            mine = lax.dynamic_index_in_dim(kept, bit, 1, keepdims=False)
            sent = lax.dynamic_index_in_dim(kept, 1 - bit, 1, keepdims=False)
            grad = mine + lax.ppermute(sent.astype(low), DP, flips(bit_index)).astype(full)
        return grad.reshape(model_width // dp_count, -1)

    def rest_sum(values):
        for bit_index in range(rest):
            values = values + lax.ppermute(values, DP, flips(bit_index))
        return values

    part_a, part_b = rest_scatter(back[N.a]), rest_scatter(back[N.b])
    operator_grads = jnp.concatenate([part_a[:, :width], part_b, part_a[:, width:]], axis=1)
    shared, chan = rest_sum(back[N.shared]), rest_sum(back[N.chan])
    wide = shared[: 6 * (model_width // 128)].reshape(6, model_width)
    share = units // dp_count
    grad_in = operator_grads[:, : 3 * width].reshape(-1, 3, width)
    return (
        back[N.activations],
        back[N.input_grad],
        wide[0],
        wide[1],
        jnp.transpose(grad_in, (1, 2, 0)),
        chan[9:12],
        chan[0:9].reshape(3, 3, width),
        chan[12:15],
        shared[40 : 40 + inputs_count, :units],
        shared[144, :units],
        shared[145, :units],
        shared[80 : 80 + units, :units],
        shared[146, :units],
        shared[147, :units],
        lax.dynamic_slice_in_dim(chan[16 : 16 + units], group * share, share, 0),
        chan[15],
        jnp.transpose(operator_grads[:, 3 * width :]),
        wide[2],
        wide[3],
        wide[4],
        rest_scatter(back[N.up]),
        chan[80 : 80 + model_width // width].reshape(-1),
        jnp.transpose(rest_scatter(back[N.down])),
        wide[5],
    )


def solution(mesh):
    in_specs = (
        P((DP, TENSOR), None),
        P(DP),
        P(DP, None),
        P(),
        P(),
        P(None, TENSOR, None),
        P(None, TENSOR),
        P(None, None, TENSOR),
        P(None, TENSOR),
        P(),
        P(),
        P(),
        P(),
        P(),
        P(),
        P(None, TENSOR),
        P(TENSOR),
        P(TENSOR, None),
        P(),
        P(),
        P(),
        P(None, TENSOR),
        P(TENSOR),
        P(TENSOR, None),
        P(),
        P((DP, TENSOR), None),
    )
    out_specs = (
        P((DP, TENSOR), None),
        P((DP, TENSOR), None),
        P(),
        P(),
        P(None, TENSOR, DP),
        P(None, TENSOR),
        P(None, None, TENSOR),
        P(None, TENSOR),
        P(),
        P(),
        P(),
        P(),
        P(),
        P(),
        P(DP, TENSOR),
        P(TENSOR),
        P(TENSOR, DP),
        P(),
        P(),
        P(),
        P(DP, TENSOR),
        P(TENSOR),
        P(TENSOR, DP),
        P(),
    )
    return jax.shard_map(local, mesh=mesh, in_specs=in_specs, out_specs=out_specs, check_vma=False)
```

```python
import functools
import math

import jax
import jax.numpy as jnp
import numpy as np
from jax import lax
from jax.experimental import pallas as pl
from jax.experimental.pallas import tpu as pltpu
from jax.sharding import PartitionSpec as P

highest = lax.Precision.HIGHEST
norm_epsilon = 1e-05
slow_rate = math.log(100.0) / 1.5
fast_rate = math.log(100.0) / 0.3


def turn_seeds(length):
    levels = np.array(list(range(8)) + [1 << i for i in range(3, length.bit_length() - 1)])
    angle = (levels[:, None] * np.arange(length) % (2 * length)) * (math.pi / length)
    return np.stack([np.cos(angle), np.sin(angle)]).astype(np.float32)


def dot_nt(left, right):
    return lax.dot_general(
        left, right, (((1,), (1,)), ((), ())), preferred_element_type=jnp.float32
    )


def dot_nn(left, right):
    return jnp.dot(left, right, preferred_element_type=jnp.float32)


def dot_tn(left, right):
    return lax.dot_general(
        left, right, (((0,), (0,)), ((), ())), preferred_element_type=jnp.float32
    )


def shifted(values, shift, lanes):
    length = values.shape[1]
    if shift == 0:
        return values
    if shift > 0:
        return jnp.where(lanes >= shift, pltpu.roll(values, shift, 1), 0.0)
    return jnp.where(lanes < length + shift, pltpu.roll(values, length + shift, 1), 0.0)


def column(params, index):
    return params[:, index : index + 1]


def pack_columns(columns, rows):
    lanes = lax.broadcasted_iota(jnp.int32, (rows, 128), 1)
    packed = jnp.zeros((rows, 128), jnp.float32)
    for index, values in columns:
        packed = jnp.where(lanes == index, values, packed)
    return packed


BLOCKS = 8
CHUNK = 64
ROWS = 128


def other_of(index, step):
    return index + step * (1 - 2 * ((index // step) % 2))


TENSOR = "tensor"
DP = "dp"


class N:
    (
        a, activations, b, b1, b2, back, branch, cb, chan, conv, conv_b, conv_w, cot, cotf, cotn,
        coty, cw, down, down_b, down_bias, down_far, down_g, down_near, down_r, downf, downn, downy,
        extra, f_bias, factor, farx, fb, fb1, fb2, feat, ff1, ff2, filt, first, freq, fw1, fw2, g1,
        g2, gain, gain1, gain2, ib, in_b, in_w, input_grad, midf, midn, midy, near, norm, normed,
        ob, out, out_b, par, peer_a, peer_b, proj, resid, residual, residual_grad, rgrad, seeds,
        shared, shift1, shift2, signal, streams, table, tokens, up, up_b, up_g, up_r, upb, upb_g,
        w1, w2, w3, w_in, w_last, w_mid, w_out, w_peer, wx, wy, y_a, y_b,
    ) = range(94)


FRONT_PLAN = (N.up, N.down, (N.wy, 0), (N.wy, 1), (N.wy, 2), (N.wx, 0), (N.wx, 1), (N.wx, 2), N.norm, N.par, N.w3, N.cotn, N.coty, N.cotf, N.branch, N.midn, (N.midy, 0), (N.midy, 1),
              (N.midf, 0), (N.midf, 1), N.near, (N.farx, 0), (N.farx, 1), (N.back, 0), (N.back, 1), N.downn, N.downf)
FRONT_LOADS = (N.w_in, N.w_out, N.tokens, N.g1, N.b1, N.cw, N.ib, N.cb, N.fb, N.w3, N.cot, N.seeds, N.fw1,
               N.fw2, N.fb1, N.ff1, N.fb2, N.ff2, N.ob, N.g2, N.b2, N.upb, N.up, N.down)
FRONT_OUTS = (N.proj, N.streams, N.signal, N.factor, N.conv, N.normed, N.w_peer, N.par, N.table, N.filt, N.w_last,
              N.resid, N.residual_grad, N.residual, N.up_g, N.down_g, N.up_r, N.down_r, N.down_near, N.down_far, N.extra, N.upb_g, N.freq, N.feat)


def gelu_parts(values):
    cdf = 0.5 * (1.0 + lax.erf(values * (1.0 / math.sqrt(2.0))))
    density = jnp.exp(-0.5 * values * values) * (1.0 / math.sqrt(2.0 * math.pi))
    return (values * cdf, cdf + values * density)


def normed_parts(values):
    centred = values - jnp.mean(values, axis=-1, keepdims=True)
    inverse = lax.rsqrt(jnp.mean(centred * centred, axis=-1, keepdims=True) + norm_epsilon)
    return (centred * inverse, inverse)


def norm_rows_back(back, normed, inverse, gain):
    scaled = back * gain
    return inverse * (
        scaled
        - jnp.mean(scaled, axis=-1, keepdims=True)
        - normed * jnp.mean(scaled * normed, axis=-1, keepdims=True)
    )


def path_place(row, block_rows, order):
    index, offset = row // block_rows, row % block_rows
    bits = [(index >> b) & 1 for b in range(3)]
    return (bits[order[0]] * 4 + bits[order[1]] * 2 + bits[order[2]]) * block_rows + offset


def store_rows(ref, start, values, block_rows, order):
    stop, begin = start + values.shape[0], start
    while begin < stop:
        size = min(block_rows - begin % block_rows, stop - begin)
        place = path_place(begin, block_rows, order)
        ref[place : place + size, :] = values[begin - start : begin - start + size, :]
        begin += size


HALVES = (N.proj, N.streams, N.signal, N.factor, N.conv)
STORES = tuple((name, half) for name in HALVES for half in (0, 1)) + FRONT_OUTS[5:]
WIDES = (N.gain1, N.shift1, N.out_b, N.gain2, N.shift2, N.down_b)
VECTORS = (N.fb1, N.ff1, N.fb2, N.ff2)
RAW = (N.activations, N.input_grad, N.up, N.down, N.a, N.b, N.shared, N.chan)
RESULTS = (N.activations, N.input_grad, N.gain1, N.shift1, N.in_w, N.in_b, N.conv_w, N.conv_b, N.w1, N.fb1, N.ff1, N.w2,
           N.fb2, N.ff2, N.w3, N.f_bias, N.out, N.out_b, N.gain2, N.shift2, N.up, N.up_b, N.down, N.down_b)
PATHS = ((0, 1, 2), (1, 0, 2))


def operator_front(dp_step, *refs):
    full, low = jnp.float32, jnp.bfloat16
    n, m = len(FRONT_LOADS), len(FRONT_OUTS)
    source = dict(zip(FRONT_LOADS, refs[:n]))
    counts, lengths = refs[n], refs[n + 1]
    refs = refs[:n] + refs[n + 2 :]
    target = dict(zip(FRONT_OUTS, refs[n : n + m]))
    held = dict(zip(FRONT_LOADS, refs[n + m : 2 * n + m]))
    made = dict(zip(FRONT_OUTS, refs[2 * n + m : 2 * n + 2 * m]))
    (mid_near, mid_far, cot_near, cot_far, hid_near, hid_far, pg_near, pg_far, acc, inner, real,
     pair_a, pair_b, pair_c, send_row, recv_branch, recv_near, send_far, recv_far, send_back, recv_back,
     recv_down_near, recv_down_far, w_own, norms, lines, fcol, low_turns, high_turns, load_sem, store_sem, send_sem, recv_sem,
     ) = refs[2 * n + 2 * m :]

    part = lax.axis_index(TENSOR)
    group = lax.axis_index(DP)
    side = part % 2
    across = {TENSOR: other_of(part, 1)}
    over = {TENSOR: other_of(part, 2)}
    beside = {DP: other_of(group, 1)}
    bits = [(group // (dp_step << b)) % 2 for b in range(3)]
    flips = [{DP: other_of(group, dp_step << b)} for b in range(2)]
    greeted = [across, over] + flips + ([beside] if dp_step > 1 else [])
    width = inner.shape[0]
    length, model_width = acc.shape
    half = length // 2
    tile = half // 2
    mine = pl.ds(pl.multiple_of(side * half, half), half)
    theirs = pl.ds(pl.multiple_of((1 - side) * half, half), half)

    def mine_at(start, size):
        return pl.ds(pl.multiple_of(side * half + start, 16), size)

    def theirs_at(start, size):
        return pl.ds(pl.multiple_of((1 - side) * half + start, 16), size)

    def remote(name, src, dst, to):
        index = FRONT_PLAN.index(name)
        copy = pltpu.make_async_remote_copy(
            src_ref=src,
            dst_ref=dst,
            send_sem=send_sem.at[index],
            recv_sem=recv_sem.at[index],
            device_id=to,
            device_id_type=pl.DeviceIdType.MESH,
        )
        copy.start()
        return copy

    loads = {}
    for index, name in enumerate(FRONT_LOADS):
        place = held[name]
        if name == N.w_in:
            place = w_own.at[0 : 3 * width]
        elif name == N.w_out:
            place = w_own.at[3 * width :]
        elif name == N.w3:
            place = made[N.w_last].at[0]
        loads[name] = pltpu.make_async_copy(source[name], place, load_sem.at[index])
        loads[name].start()
    stores = {}

    def put(name, src, dst):
        stores[name] = pltpu.make_async_copy(src, dst, store_sem.at[STORES.index(name)])
        stores[name].start()

    barrier = pltpu.get_barrier_semaphore()
    for to in greeted:
        pl.semaphore_signal(barrier, inc=1, device_id=to, device_id_type=pl.DeviceIdType.MESH)
    pl.semaphore_wait(barrier, len(greeted))

    normed, w_peer, par = made[N.normed], made[N.w_peer], made[N.par]
    loads[N.w_in].wait()
    loads[N.w_out].wait()
    pieces = 3
    share = 4 * width // (2 * pieces)
    copies = {}

    def weight_rows(piece):
        return pl.ds(pl.multiple_of((2 * piece + group % 2) * share, 16), share)

    for piece in range(pieces):
        rows = weight_rows(piece)
        copies[N.wy, piece] = remote((N.wy, piece), w_own.at[rows], w_peer.at[rows], over)

    def pass_on(piece):
        copies[N.wy, piece].wait()
        rows = weight_rows(piece)
        copies[N.wx, piece] = remote((N.wx, piece), w_peer.at[rows], w_peer.at[rows], beside)

    for name in (N.tokens, N.g1, N.b1, N.ob, N.g2, N.b2, N.upb):
        loads[name].wait()
    for index, name in enumerate((N.g1, N.b1, N.ob, N.g2, N.b2, N.upb)):
        norms[index : index + 1, :] = held[name][...][None, :]

    def norm_one(index, carry):
        rows = pl.ds(pl.multiple_of(index * ROWS, ROWS), ROWS)
        values = normed_parts(held[N.tokens][rows, :].astype(full))[0]
        normed[mine_at(index * ROWS, ROWS), :] = (values * norms[0:1, :] + norms[1:2, :]).astype(low)
        return carry

    lax.fori_loop(0, half // ROWS, norm_one, 0)
    copies[N.norm] = remote(N.norm, normed.at[mine], normed.at[mine], across)

    for name in (N.cw, N.ib, N.cb, N.fb, N.w3):
        loads[name].wait()
    lines[...] = jnp.zeros_like(lines)
    lines[0:9, :] = held[N.cw][...].reshape(9, width)
    lines[9:12, :] = held[N.ib][...]
    lines[12:15, :] = held[N.cb][...]
    lines[15:16, :] = held[N.fb][...][None, :]
    channel = (part * width + lax.broadcasted_iota(jnp.int32, (1, width), 1)).astype(full)
    channels = 4 * width
    lines[16:17, :] = (slow_rate + (fast_rate - slow_rate) / (channels - 1) * channel) * (1.0 / (length - 1))
    par[0:width, 0:24] = jnp.transpose(lines[...])
    copies[N.par] = remote(N.par, par.at[0:width], par.at[width:], over)
    copies[N.w3] = remote(N.w3, made[N.w_last].at[0], made[N.w_last].at[1], over)

    loads[N.cot].wait()
    slot = part * half // length
    mask_rows = jnp.where(slot < counts[0], lengths[0, slot], 0) - part * half % length

    def mask_cot(index, carry):
        rows = pl.ds(pl.multiple_of(index * ROWS, ROWS), ROWS)
        place = lax.broadcasted_iota(jnp.int32, (ROWS, model_width), 0) + index * ROWS
        values = held[N.cot][rows, :]
        cot_near[mine_at(index * ROWS, ROWS), :] = jnp.where(
            place < mask_rows, values.astype(full), 0.0
        ).astype(low)
        return carry

    lax.fori_loop(0, half // ROWS, mask_cot, 0)
    copies[N.coty] = remote(N.coty, cot_near.at[mine], cot_far.at[mine], over)

    loads[N.seeds].wait()
    seeds, table = held[N.seeds], made[N.table]
    lows = low_turns.shape[1]

    def turn_by(turns, start, row):
        cos_row, sin_row = seeds[0, row : row + 1, :], seeds[1, row : row + 1, :]
        cos_part, sin_part = turns[0, 0:start, :], turns[1, 0:start, :]
        turns[0, start : 2 * start, :] = cos_part * cos_row - sin_part * sin_row
        turns[1, start : 2 * start, :] = sin_part * cos_row + cos_part * sin_row

    low_turns[:, 0:8, :] = seeds[:, 0:8, :]
    high_turns[:, 0:1, :] = seeds[:, 0:1, :]
    start, row = 8, 8
    while start < lows:
        turn_by(low_turns, start, row)
        start, row = 2 * start, row + 1
    start = 1
    while start < length // lows:
        turn_by(high_turns, start, row)
        start, row = 2 * start, row + 1
    feat = made[N.feat]
    bands = (feat.shape[0] - 1) // 2
    feat[0:1, :] = lax.broadcasted_iota(jnp.int32, (1, length), 1).astype(full) * (1.0 / (length - 1))
    for band in range(1, bands + 1):
        turns, index = (low_turns, 2 * band) if 2 * band < lows else (high_turns, 2 * band // lows)
        feat[band : band + 1, :] = turns[0, index : index + 1, :]
        feat[bands + band : bands + band + 1, :] = -turns[1, index : index + 1, :]
    put(N.feat, feat, target[N.feat])
    for high in range(length // lows):
        cos_high, sin_high = high_turns[0, high : high + 1, :], high_turns[1, high : high + 1, :]
        cos_low, sin_low = low_turns[0], low_turns[1]
        rows = slice(high * lows, (high + 1) * lows)
        table[0, rows, :] = (cos_high * cos_low - sin_high * sin_low).astype(low)
        sines = sin_high * cos_low + cos_high * sin_low
        if high == 0:
            place = lax.broadcasted_iota(jnp.int32, sines.shape, 1)
            first = lax.broadcasted_iota(jnp.int32, sines.shape, 0) == 0
            sines = jnp.where(first, (1 - 2 * (place % 2)).astype(full), sines)
        table[1, rows, :] = sines.astype(low)
    put(N.table, table, target[N.table])
    pass_on(0)
    cos, sin = table.at[0], table.at[1]

    for name in (N.fw1, N.fw2, N.fb1, N.ff1, N.fb2, N.ff2):
        loads[name].wait()

    def exact_tn(left, right):
        return lax.dot_general(
            left, right, (((0,), (0,)), ((), ())), precision=highest, preferred_element_type=full
        )

    filt = made[N.filt]
    units = held[N.fw2].shape[0]
    fcol[...] = jnp.zeros_like(fcol)
    for index, name in enumerate((N.ff1, N.ff2, N.fb1, N.fb2)):
        fcol[index : index + 1, 0:units] = held[name][...][None, :]
    freq = made[N.freq]
    freq[...] = jnp.zeros_like(freq)
    freq[:, 0:8] = jnp.transpose(fcol[...])[0:units, :]
    fcol = freq[...]
    put(N.freq, freq, target[N.freq])
    sum_one = exact_tn(held[N.fw1][...], feat[...]) + column(fcol, 2)
    angle = column(fcol, 0) * sum_one
    filt[0] = jnp.sin(angle)
    filt[2] = jnp.cos(angle)
    filt[4] = sum_one
    sum_two = exact_tn(held[N.fw2][...], filt[0]) + column(fcol, 3)
    angle = column(fcol, 1) * sum_two
    filt[1] = jnp.sin(angle)
    filt[3] = jnp.cos(angle)
    filt[5] = sum_two
    put(N.filt, filt, target[N.filt])
    pass_on(1)

    lanes = lax.broadcasted_iota(jnp.int32, (CHUNK, length), 1)
    first_lane = lanes == 0
    scale = jnp.where(first_lane, 0.5 / length, 1.0 / length)
    proj, signal, factor, conv = made[N.proj], made[N.signal], made[N.factor], made[N.conv]
    streams = made[N.streams]

    def forward(side_index, weight):
        base = side_index * width
        span = slice(base, base + width)

        def keep(name):
            place = target[name].at[span] if name == N.conv else target[name].at[:, span]
            put((name, side_index), made[name], place)

        def free(*names):
            if side_index == 1:
                for name in names:
                    stores.pop((name, 0)).wait()

        real[...] = exact_tn(made[N.w_last][side_index], filt[1])

        def windowed(index, carry):
            rows = pl.ds(pl.multiple_of(index * CHUNK, CHUNK), CHUNK)
            params = par[pl.ds(pl.multiple_of(base + index * CHUNK, CHUNK), CHUNK), :]
            pair_a[rows, :] = (
                real[rows, :] * jnp.exp(-lanes.astype(full) * column(params, 16))
            ).astype(low)
            return carry

        lax.fori_loop(0, width // CHUNK, windowed, 0)
        free(N.factor)
        factor[0] = dot_nn(pair_a[...], cos[...])
        factor[1] = dot_nt(pair_a[...], sin[...])
        keep(N.factor)
        if side_index == 0:
            pass_on(2)
        free(N.streams, N.proj)
        for i in range(3):
            streams[i] = dot_nt(weight[i * width : (i + 1) * width, :], normed[...]) + column(
                par[base : base + width, :], 9 + i
            )

        def mixing(index, carry):
            rows = pl.ds(pl.multiple_of(index * CHUNK, CHUNK), CHUNK)
            params = par[pl.ds(pl.multiple_of(base + index * CHUNK, CHUNK), CHUNK), :]

            def stream(i):
                line = streams[i, rows, :]
                proj[i, rows, :] = line.astype(low)
                total = column(params, 12 + i) + sum(
                    column(params, 3 * j + i) * shifted(line, j, lanes) for j in range(3)
                )
                streams[i, rows, :] = total
                return total

            stream(0)
            mixed_in = stream(1) * stream(2)
            inner[rows, :] = mixed_in
            pair_a[rows, :] = mixed_in.astype(low)
            return carry

        lax.fori_loop(0, width // CHUNK, mixing, 0)
        keep(N.streams)
        keep(N.proj)
        free(N.signal)
        signal[0] = dot_nn(pair_a[...], cos[...])
        signal[1] = dot_nt(pair_a[...], sin[...])
        keep(N.signal)

        def product(index, carry):
            rows = pl.ds(pl.multiple_of(index * CHUNK, CHUNK), CHUNK)
            s_cos, s_sin = signal[0, rows, :] * scale, signal[1, rows, :] * scale
            f_cos, f_sin = factor[0, rows, :], factor[1, rows, :]
            f_last = jnp.where(first_lane, f_sin, f_cos)
            f_sin = jnp.where(first_lane, 0.0, f_sin)
            pair_a[rows, :] = (s_cos * f_cos - s_sin * f_sin).astype(low)
            pair_b[rows, :] = (s_cos * f_sin + s_sin * f_last).astype(low)
            return carry

        lax.fori_loop(0, width // CHUNK, product, 0)
        real[...] = dot_nn(pair_a[...], cos[...])
        real[...] += dot_nn(pair_b[...], sin[...])

        free(N.conv)

        def gating(index, carry):
            rows = pl.ds(pl.multiple_of(index * CHUNK, CHUNK), CHUNK)
            params = par[pl.ds(pl.multiple_of(base + index * CHUNK, CHUNK), CHUNK), :]
            lines = real[rows, :] + inner[rows, :] * column(params, 15)
            conv[rows, :] = lines
            pair_c[rows, :] = (lines * streams[0, rows, :]).astype(low)
            return carry

        lax.fori_loop(0, width // CHUNK, gating, 0)
        keep(N.conv)
        for start in range(0, length, 256):
            piece = dot_tn(pair_c[:, start : start + 256], weight[3 * width :, :])
            if side_index == 0:
                acc[start : start + 256, :] = piece
            else:
                acc[start : start + 256, :] += piece

    copies[N.norm].wait()
    copies[N.cotn] = remote(N.cotn, cot_near.at[mine], cot_near.at[mine], across)
    put(N.normed, normed, target[N.normed])
    forward(0, w_own)
    for name in (N.par, N.w3) + tuple((N.wx, piece) for piece in range(pieces)):
        copies[name].wait()
    put(N.w_peer, w_peer, target[N.w_peer])
    put(N.par, par, target[N.par])
    put(N.w_last, made[N.w_last], target[N.w_last])
    forward(1, w_peer)

    send_row[...] = acc[theirs, :].astype(low)
    copies[N.branch] = remote(N.branch, send_row, recv_branch, across)
    copies[N.branch].wait()
    residual, residual_grad, resid = made[N.residual], made[N.residual_grad], made[N.resid]

    def norm_two(chunk):
        def body(index, carry):
            start = chunk * tile + index * ROWS
            rows = pl.ds(pl.multiple_of(start, ROWS), ROWS)
            place = mine_at(start, ROWS)
            lines = (
                held[N.tokens][rows, :].astype(full)
                + acc[place, :]
                + recv_branch[rows, :].astype(full)
                + norms[2:3, :]
            )
            residual[rows, :] = lines
            mid_near[place, :] = (normed_parts(lines)[0] * norms[3:4, :] + norms[4:5, :]).astype(low)
            return carry

        lax.fori_loop(0, tile // ROWS, body, 0)
        place = mine_at(chunk * tile, tile)
        copies[N.midy, chunk] = remote((N.midy, chunk), mid_near.at[place], mid_far.at[place], over)

    norm_two(0)
    norm_two(1)
    copies[N.midn] = remote(N.midn, mid_near.at[mine], mid_near.at[mine], across)
    put(N.residual, residual, target[N.residual])
    copies[N.cotn].wait()
    for name in (N.up, N.down):
        loads[name].wait()
    up, down = held[N.up], held[N.down]

    def units(rows, mid, cot, hid, pg):
        act, slope = gelu_parts(dot_nn(mid[rows, :], up[...]) + norms[5:6, :])
        hid[rows, :] = act.astype(low)
        back = (dot_nt(cot[rows, :], down[...]) * slope).astype(low)
        pg[rows, :] = back
        return (dot_nt(back, up[...]), jnp.sum(back.astype(full), axis=0, keepdims=True))

    copies[N.midn].wait()

    def near(index, total):
        rows = pl.ds(pl.multiple_of(index * tile, tile), tile)
        product, found = units(rows, mid_near, cot_near, hid_near, pg_near)
        acc[rows, :] = product
        return total + found

    total = lax.fori_loop(0, length // tile, near, jnp.zeros((1, model_width), full))
    send_row[...] = acc[theirs, :].astype(low)
    copies[N.near] = remote(N.near, send_row, recv_near, across)

    copies[N.coty].wait()
    copies[N.cotf] = remote(N.cotf, cot_far.at[mine], cot_far.at[mine], across)
    copies[N.midy, 0].wait()
    place = mine_at(0, tile)
    copies[N.midf, 0] = remote((N.midf, 0), mid_far.at[place], mid_far.at[place], across)
    copies[N.cotf].wait()
    for chunk in range(2):
        copies[N.midf, chunk].wait()
        product, found = units(theirs_at(chunk * tile, tile), mid_far, cot_far, hid_far, pg_far)
        total = total + found
        span = slice(chunk * tile, (chunk + 1) * tile)
        send_far[span, :] = product.astype(low)
        copies[N.farx, chunk] = remote((N.farx, chunk), send_far.at[span], recv_far.at[span], across)
        product, found = units(mine_at(chunk * tile, tile), mid_far, cot_far, hid_far, pg_far)
        total = total + found
        if chunk == 0:
            copies[N.midy, 1].wait()
            place = mine_at(tile, tile)
            copies[N.midf, 1] = remote((N.midf, 1), mid_far.at[place], mid_far.at[place], across)
        copies[N.farx, chunk].wait()
        send_back[span, :] = (product + recv_far[span, :].astype(full)).astype(low)
        copies[N.back, chunk] = remote((N.back, chunk), send_back.at[span], recv_back.at[span], over)

    part_rows = model_width // 2

    def weight_grads(name, recv, path, left, right):
        grads = made[name]
        for piece in range(model_width // 256):
            span = slice(piece * 256, (piece + 1) * 256)
            product = dot_tn(left[0][:, span], right[0][...]) + dot_tn(left[1][:, span], right[1][...])
            store_rows(grads, piece * 256, product.astype(low), model_width // BLOCKS, PATHS[path])
        bit = PATHS[path][0]
        sent = grads.at[pl.ds(pl.multiple_of((1 - bits[bit]) * part_rows, part_rows), part_rows)]
        kept = grads.at[pl.ds(pl.multiple_of(bits[bit] * part_rows, part_rows), part_rows)]
        short = N.up if path == 0 else N.down
        copies[short] = remote(short, sent, made[recv], flips[bit])
        put(name, kept, target[name])

    weight_grads(N.up_g, N.up_r, 0, (mid_near, mid_far), (pg_near, pg_far))
    weight_grads(N.down_g, N.down_r, 1, (cot_near, cot_far), (hid_near, hid_far))
    copies[N.near].wait()
    down_near, down_far = made[N.down_near], made[N.down_far]
    send_row[...] = dot_nn(hid_far[theirs, :], down[...]).astype(low)
    copies[N.downf] = remote(N.downf, send_row, recv_down_far, across)
    made[N.upb_g][0:1, :] = total
    down_near[...] = dot_nn(hid_near[mine, :], down[...])
    copies[N.downf].wait()
    down_far[...] = (dot_nn(hid_far[mine, :], down[...]) + recv_down_far[...].astype(full)).astype(low)
    put(N.down_far, down_far, target[N.down_far])
    send_row[...] = dot_nn(hid_near[theirs, :], down[...]).astype(low)
    copies[N.downn] = remote(N.downn, send_row, recv_down_near, across)
    copies[N.downn].wait()
    down_near[...] += recv_down_near[...].astype(full)
    put(N.down_near, down_near, target[N.down_near])

    sums = [jnp.zeros((1, model_width), full)] * 4
    sums = tuple(sums)
    for chunk in range(2):
        copies[N.back, chunk].wait()

        def body(index, carry):
            start = chunk * tile + index * ROWS
            rows = pl.ds(pl.multiple_of(start, ROWS), ROWS)
            place = mine_at(start, ROWS)
            normed_rows, inverse = normed_parts(residual[rows, :])
            back = acc[place, :] + recv_near[rows, :].astype(full) + recv_back[rows, :].astype(full)
            cots = cot_near[place, :].astype(full)
            grad = cots + norm_rows_back(back, normed_rows, inverse, norms[3:4, :])
            residual_grad[rows, :] = grad
            rounded = grad.astype(low)
            resid[rows, :] = rounded
            found = (rounded.astype(full), back * normed_rows, back, cots)
            return tuple(a + jnp.sum(b, axis=0, keepdims=True) for a, b in zip(carry, found))

        sums = lax.fori_loop(0, tile // ROWS, body, sums)
    extra = made[N.extra]
    for index in range(4):
        extra[index : index + 1, :] = sums[index]
    put(N.resid, resid, target[N.resid])
    put(N.residual_grad, residual_grad, target[N.residual_grad])
    put(N.extra, extra, target[N.extra])
    put(N.upb_g, made[N.upb_g], target[N.upb_g])
    for short, name in ((N.up, N.up_r), (N.down, N.down_r)):
        copies[short].wait()
        put(name, made[name], target[name])
    for copy in stores.values():
        copy.wait()


def call_operator_front(operands, counts, lengths, width, length, model_width, dp_step):
    full, low = jnp.float32, jnp.bfloat16
    half = length // 2
    channels = 2 * width
    units = operands[N.fw2].shape[0]
    shapes = {
        N.proj: ((3, channels, length), low),
        N.streams: ((3, channels, length), full),
        N.signal: ((2, channels, length), full),
        N.factor: ((2, channels, length), full),
        N.conv: ((channels, length), full),
        N.normed: ((length, model_width), low),
        N.w_peer: ((4 * width, model_width), low),
        N.par: ((channels, 128), full),
        N.table: ((2, length, length), low),
        N.filt: ((6, units, length), full),
        N.w_last: ((2, units, width), full),
        N.resid: ((half, model_width), low),
        N.residual_grad: ((half, model_width), full),
        N.residual: ((half, model_width), full),
        N.up_g: ((model_width // 2, model_width), low),
        N.down_g: ((model_width // 2, model_width), low),
        N.up_r: ((model_width // 2, model_width), low),
        N.down_r: ((model_width // 2, model_width), low),
        N.down_near: ((half, model_width), full),
        N.down_far: ((half, model_width), low),
        N.extra: ((8, model_width), full),
        N.upb_g: ((8, model_width), full),
        N.freq: ((units, 128), full),
        N.feat: ((operands[N.fw1].shape[0], length), full),
    }
    split = {
        N.proj: (3, width, length),
        N.streams: (3, width, length),
        N.signal: (2, width, length),
        N.factor: (2, width, length),
        N.conv: (width, length),
        N.up_g: (model_width, model_width),
        N.down_g: (model_width, model_width),
    }
    placed = {N.w_in: (16, 128), N.w_out: (16, 128), N.w3: (8, 128)}
    rows = pltpu.VMEM((length, model_width), low)
    half_rows = pltpu.VMEM((half, model_width), low)
    wide, thin = pltpu.VMEM((width, length), full), pltpu.VMEM((width, length), low)
    scratch = [
        pltpu.VMEM(placed.get(name, operands[name].shape), operands[name].dtype) for name in FRONT_LOADS
    ]
    scratch += [pltpu.VMEM(split.get(name, shapes[name][0]), shapes[name][1]) for name in FRONT_OUTS]
    scratch += [rows] * 8 + [pltpu.VMEM((length, model_width), full)] + [wide] * 2 + [thin] * 3
    scratch += [half_rows] * 9
    scratch += [
        pltpu.VMEM((4 * width, model_width), low),
        pltpu.VMEM((8, model_width), full),
        pltpu.VMEM((24, width), full),
        pltpu.VMEM((8, 128), full),
        pltpu.VMEM((2, 1 << (length.bit_length() // 2), length), full),
        pltpu.VMEM((2, length >> (length.bit_length() // 2), length), full),
        pltpu.SemaphoreType.DMA((len(FRONT_LOADS),)),
        pltpu.SemaphoreType.DMA((len(STORES),)),
        pltpu.SemaphoreType.DMA((len(FRONT_PLAN),)),
        pltpu.SemaphoreType.DMA((len(FRONT_PLAN),)),
    ]
    results = pl.pallas_call(
        functools.partial(operator_front, dp_step),
        out_shape=tuple(jax.ShapeDtypeStruct(*shapes[name]) for name in FRONT_OUTS),
        in_specs=[pl.BlockSpec(memory_space=pl.ANY)] * len(FRONT_LOADS)
        + [pl.BlockSpec(memory_space=pltpu.SMEM)] * 2,
        out_specs=tuple(pl.BlockSpec(memory_space=pl.ANY) for name in FRONT_OUTS),
        scratch_shapes=scratch,
        compiler_params=pltpu.CompilerParams(
            vmem_limit_bytes=63 * 1024 * 1024, collective_id=1, has_side_effects=True
        ),
        name="operator_front",
    )(*(operands[name] for name in FRONT_LOADS), counts, lengths)
    return dict(zip(FRONT_OUTS, results))


PLAN = (N.resid, N.downy, N.peer_a, N.peer_b, N.y_a, N.y_b, N.chan, N.first) + tuple(
    (name, hop) for name in (N.up, N.down, N.a, N.b, N.chan) for hop in (1, 2, 3) if hop > 1 or name not in (N.up, N.down)
) + tuple((N.shared, hop) for hop in range(5))
LOADS = (N.resid, N.w_peer, N.up, N.up_r, N.down, N.down_r, N.w_in, N.w_out, N.streams, N.proj, N.conv, N.par,
         N.normed, N.table, N.factor, N.signal, N.filt, N.w_last, N.w_mid, N.feat, N.freq, N.tokens, N.gain,
         N.rgrad, N.extra, N.upb, N.residual, N.down_near, N.down_bias)
SPLIT = (N.streams, N.proj, N.conv, N.factor, N.signal)


def operator_back(dp_step, outs, *refs):
    sizes = len(LOADS)
    source = dict(zip(LOADS, refs[:sizes]))
    down_far, counts, lengths = refs[sizes : sizes + 3]
    refs = refs[:sizes] + refs[sizes + 3 :]
    out = dict(zip(outs, refs[sizes : sizes + len(outs)]))
    refs = refs[sizes + len(outs) :]
    held = dict(zip(LOADS, refs[: len(LOADS)]))
    refs = refs[len(LOADS) :]
    (grad, real, imag, pair_a, pair_b, pair_c, pair_d, stack, proj_low, h_grad, first, first_send, first_recv,
     peer_a, peer_b, beside_a, beside_b, send_a, send_b, recv_a, recv_b, sum_a, sum_b, recv_down, sums, chan_peer, chan_recv, chan, chan_hops,
     shared, shared_hops, w_own) = refs[:32]
    hops = dict(zip((N.up, N.down, N.a, N.b), (refs[32 + 5 * i : 37 + 5 * i] for i in range(4))))
    load_sem, send_sem, recv_sem = refs[52:]
    full, low = jnp.float32, jnp.bfloat16

    part = lax.axis_index(TENSOR)
    group = lax.axis_index(DP)
    side = part % 2
    bits = [(group // (dp_step << b)) % 2 for b in range(3)]
    across = {TENSOR: other_of(part, 1)}
    over = {TENSOR: other_of(part, 2)}
    flips = [{DP: other_of(group, dp_step << b)} for b in range(3)]

    def remote(name, src, dst, target):
        index = PLAN.index(name)
        return pltpu.make_async_remote_copy(
            src_ref=src,
            dst_ref=dst,
            send_sem=send_sem.at[index],
            recv_sem=recv_sem.at[index],
            device_id=target,
            device_id_type=pl.DeviceIdType.MESH,
        )

    width, length = grad.shape
    model_width = first.shape[1]
    half_rows = length // 2
    block_rows = model_width // BLOCKS
    mine = pl.ds(pl.multiple_of(side * half_rows, half_rows), half_rows)
    theirs = pl.ds(pl.multiple_of((1 - side) * half_rows, half_rows), half_rows)

    places = dict(held)
    places[N.resid] = held[N.resid].at[mine]
    places[N.w_in] = w_own.at[0 : 3 * width]
    places[N.w_out] = w_own.at[3 * width :]
    loads = {}

    def load(name, half):
        src, dst, index = source[name], places[name], LOADS.index(name)
        key = name
        if half is not None:
            span = slice(half * width, (half + 1) * width)
            if name == N.conv:
                src, dst = src.at[span], dst.at[span]
            else:
                src, dst = src.at[:, span], dst.at[:, span]
            key = (name, half)
            index = index if half == 1 else len(LOADS) + SPLIT.index(name)
        loads[key] = pltpu.make_async_copy(src, dst, load_sem.at[index])
        loads[key].start()

    late = LOADS.index(N.w_mid)
    for name in LOADS[:late]:
        load(name, 1 if name in SPLIT else None)
    for name in SPLIT:
        load(name, 0)
    for name in LOADS[late:]:
        load(name, None)

    barrier = pltpu.get_barrier_semaphore()
    for target in [across, over] + flips:
        pl.semaphore_signal(barrier, inc=1, device_id=target, device_id_type=pl.DeviceIdType.MESH)
    pl.semaphore_wait(barrier, 5)

    resid = held[N.resid]
    resid_copy = remote(N.resid, source[N.resid], resid.at[mine], across)
    resid_copy.start()
    loads[N.resid].wait()
    loads[N.w_peer].wait()
    resid_copy.wait()

    def spot(index, size):
        return pl.ds(pl.multiple_of(index * size, size), size)

    def order_of(name):
        return PATHS[1] if name == N.down else PATHS[0]

    def hop_one(name, grads):
        bit = order_of(name)[0]
        src = grads.at[spot(1 - bits[bit], 4 * block_rows)]
        copy = remote((name, 1), src, hops[name][0], flips[bit])
        copy.start()
        return copy

    def hop_two(name, grads, copy, recv_one):
        _, send_two, keep_two, recv_two, _ = hops[name]
        top, bit, _ = order_of(name)
        whole = copy is not None
        if whole:
            copy.wait()
        crossed = {N.a: recv_a, N.b: recv_b}.get(name)
        for keep in (0, 1):
            pick = bits[bit] if keep else 1 - bits[bit]
            first_place = 2 * bits[top] + pick if whole else pick
            total = (
                grads[spot(first_place, 2 * block_rows), :].astype(full)
                + recv_one[spot(pick, 2 * block_rows), :].astype(full)
            )
            if crossed is not None:
                total = total + crossed[spot(pick, 2 * block_rows), :].astype(full)
            if keep:
                keep_two[...] = total
            else:
                send_two[...] = total.astype(low)
                copy = remote((name, 2), send_two, recv_two, flips[bit])
                copy.start()
        return copy

    def hop_three(name, copy):
        recv_one, send_two, keep_two, recv_two, recv_three = hops[name]
        bit = order_of(name)[2]
        copy.wait()
        place = spot(1 - bits[bit], block_rows)
        send_two[0:block_rows, :] = (keep_two[place, :] + recv_two[place, :].astype(full)).astype(low)
        copy = remote((name, 3), send_two.at[0:block_rows], recv_three, flips[bit])
        copy.start()
        return copy

    def hop_last(name, copy):
        recv_one, send_two, keep_two, recv_two, recv_three = hops[name]
        copy.wait()
        place = spot(bits[order_of(name)[2]], block_rows)
        return keep_two[place, :] + recv_two[place, :].astype(full) + recv_three[...].astype(full)

    copies = {N.downy: remote(N.downy, down_far, recv_down, over)}
    copies[N.downy].start()
    for name in (N.up, N.up_r, N.down, N.down_r):
        loads[name].wait()
    for name, received in ((N.up, N.up_r), (N.down, N.down_r)):
        copies[name] = hop_two(name, held[name], None, held[received])

    lanes = lax.broadcasted_iota(jnp.int32, (CHUNK, length), 1)
    par, streams, proj, conv = held[N.par], held[N.streams], held[N.proj], held[N.conv]
    cos, sin = held[N.table].at[0], held[N.table].at[1]
    factor, signal, normed = held[N.factor], held[N.signal], held[N.normed]
    filt = held[N.filt]
    weights = (w_own, held[N.w_peer])

    def half_pass(half, loaded, early, middle):
        base = half * width
        weight = weights[half]
        own_w = 3 * width

        def at(index):
            return pl.ds(pl.multiple_of(index * CHUNK, CHUNK), CHUNK)

        def far(index):
            return pl.ds(pl.multiple_of(base + index * CHUNK, CHUNK), CHUNK)

        def stream_back(i, index, params, back):
            moved = [shifted(back, -j, lanes) for j in range(3)]
            out = sum(column(params, 3 * j + i) * moved[j] for j in range(3)).astype(low)
            line = proj[i, far(index), :].astype(full)
            start = pl.multiple_of(i * width + index * CHUNK, CHUNK)
            proj_low[pl.ds(start, CHUNK), :] = out
            found = [(3 * j + i, jnp.sum(moved[j] * line, axis=1, keepdims=True)) for j in range(3)]
            found.append((9 + i, jnp.sum(out.astype(full), axis=1, keepdims=True)))
            found.append((12 + i, jnp.sum(back, axis=1, keepdims=True)))
            return found

        grad[...] = dot_nt(weight[own_w:, :], resid[...])
        for name in (N.streams, N.proj, N.conv):
            loads[name, half].wait()
        if not loaded:
            loads[N.par].wait()

        def before(index, carry):
            rows = far(index)
            params = par[rows, :]
            gate_out, gate_in, values = streams[0, rows, :], streams[1, rows, :], streams[2, rows, :]
            mixed_grad = grad[at(index), :]
            conv_part = conv[rows, :]
            conv_grad = mixed_grad * gate_out
            grad[at(index), :] = conv_grad
            pair_a[at(index), :] = conv_grad.astype(low)
            pair_b[at(index), :] = (conv_part * gate_out).astype(low)
            found = stream_back(0, index, params, mixed_grad * conv_part)
            found.append((15, jnp.sum(conv_grad * values * gate_in, axis=1, keepdims=True)))
            sums[at(index), :] = pack_columns(found, CHUNK)
            return carry

        lax.fori_loop(0, width // CHUNK, before, 0)
        if not loaded:
            loads[N.normed].wait()
        stack[0:width, :] = dot_nn(proj_low[0:width, :], normed[...])
        stack[width : 2 * width, :] = dot_nn(pair_b[...], resid[...])
        early()
        if not loaded:
            loads[N.table].wait()
        real[...] = dot_nn(pair_a[...], cos[...])
        imag[...] = dot_nt(pair_a[...], sin[...])
        loads[N.factor, half].wait()
        loads[N.signal, half].wait()
        first_lane = lanes == 0
        scale = jnp.where(first_lane, 0.5 / length, 1.0 / length)

        def between(index, carry):
            rows, place = far(index), at(index)
            cos_part, sin_part = real[place, :] * scale, imag[place, :] * scale
            f_cos, f_sin = factor[0, rows, :], factor[1, rows, :]
            f_last = jnp.where(first_lane, f_sin, f_cos)
            f_sin = jnp.where(first_lane, 0.0, f_sin)
            pair_a[place, :] = (cos_part * f_cos + sin_part * f_sin).astype(low)
            pair_b[place, :] = (sin_part * f_last - cos_part * f_sin).astype(low)
            s_cos, s_sin = signal[0, rows, :], signal[1, rows, :]
            s_last = jnp.where(first_lane, s_sin, s_cos)
            s_sin = jnp.where(first_lane, 0.0, s_sin)
            pair_c[place, :] = (cos_part * s_cos + sin_part * s_sin).astype(low)
            pair_d[place, :] = (sin_part * s_last - cos_part * s_sin).astype(low)
            return carry

        lax.fori_loop(0, width // CHUNK, between, 0)
        middle()
        real[...] = dot_nn(pair_a[...], cos[...]) + dot_nn(pair_b[...], sin[...])
        imag[...] = dot_nn(pair_c[...], cos[...]) + dot_nn(pair_d[...], sin[...])

        def after(index, carry):
            rows = far(index)
            params = par[rows, :]
            gate_in, values = streams[1, rows, :], streams[2, rows, :]
            back = real[at(index), :] + grad[at(index), :] * column(params, 15)
            found = stream_back(1, index, params, back * values)
            found += stream_back(2, index, params, back * gate_in)
            sums[at(index), :] = sums[at(index), :] + pack_columns(found, CHUNK)
            window = jnp.exp(-lanes.astype(full) * column(params, 16))
            pair_a[at(index), :] = (imag[at(index), :] * window).astype(low)
            return carry

        lax.fori_loop(0, width // CHUNK, after, 0)
        if not loaded:
            for name in (N.filt, N.w_last):
                loads[name].wait()
        stack[2 * width :, :] = dot_nn(proj_low[width:, :], normed[...])
        target = chan_peer if half == 1 else chan
        target[0:16, :] = jnp.transpose(sums[...])[0:16, :]
        target[16:80, :] = dot_nt(filt[1].astype(low), pair_a[...])
        h_part = dot_nn(held[N.w_last][half].astype(low), pair_a[...])
        if half == 1:
            h_grad[...] = h_part
        else:
            h_grad[...] += h_part

    def turned(part_index, ref):
        middle = model_width // 2
        rows = slice(part_index * middle, (part_index + 1) * middle)
        for start in range(0, model_width, 128):
            block = jnp.transpose(stack[rows, start : start + 128]).astype(low)
            store_rows(ref, start, block, block_rows, PATHS[0])

    peers = ((N.peer_a, peer_a, beside_a, send_a), (N.peer_b, peer_b, beside_b, send_b))

    def peer_first(part_index):
        name, grads, beside, _ = peers[part_index]
        turned(part_index, grads)
        src = grads.at[spot(1 - bits[0], 4 * block_rows)]
        copies[name] = remote(name, src, beside, flips[0])
        copies[name].start()

    def peer_cross(part_index):
        name, grads, beside, sent = peers[part_index]
        across_name, crossed = ((N.y_a, recv_a), (N.y_b, recv_b))[part_index]
        copies[name].wait()
        kept = grads[spot(bits[0], 4 * block_rows), :].astype(full)
        sent[...] = (kept + beside[...].astype(full)).astype(low)
        copies[across_name] = remote(across_name, sent, crossed, over)
        copies[across_name].start()

    def first_part(half):
        for start in range(0, length, 256):
            product = dot_tn(proj_low[:, start : start + 256], weights[half][: 3 * width, :])
            if half == 1:
                first[start : start + 256, :] = product
            else:
                first[start : start + 256, :] += product

    def last_hops():
        for name in (N.up, N.down):
            copies[name] = hop_three(name, copies[name])

    half_pass(1, False, lambda: peer_first(0), last_hops)
    peer_first(1)
    chan_peer[80:88, :] = jnp.zeros((8, width), full)
    copies[N.chan] = remote(N.chan, chan_peer, chan_recv, over)
    copies[N.chan].start()
    peer_cross(0)
    first_part(1)
    loads[N.w_in].wait()
    loads[N.w_out].wait()

    def own_first():
        turned(0, sum_a)
        copies[N.a] = hop_one(N.a, sum_a)

    half_pass(0, True, own_first, lambda: peer_cross(1))
    first_part(0)
    first_send[...] = first[theirs, :].astype(low)
    first_copy = remote(N.first, first_send, first_recv, across)
    first_copy.start()
    turned(1, sum_b)
    copies[N.b] = hop_one(N.b, sum_b)
    copies[N.y_a].wait()
    copies[N.a] = hop_two(N.a, sum_a, copies[N.a], hops[N.a][0])

    copies[N.chan].wait()
    loads[N.upb].wait()
    chan[0:80, :] = chan[0:80, :] + chan_recv[0:80, :]
    chan[80:88, :] = jnp.zeros((8, width), full)
    for index in range(held[N.upb].shape[1] // width):
        chan[80 + index : 81 + index, :] = held[N.upb][0:1, index * width : (index + 1) * width]
    chan_copy = remote((N.chan, 1), chan, chan_hops.at[0], flips[0])
    chan_copy.start()

    for name in (N.w_mid, N.feat, N.freq):
        loads[name].wait()
    freq, w_mid = held[N.freq], held[N.w_mid]
    shared[...] = jnp.zeros_like(shared)
    units = w_mid.shape[0]
    feats = held[N.feat].shape[0]
    slope = h_grad[...] * filt[3]
    q_two = jnp.sum(slope * filt[5], axis=1, keepdims=True)
    slope = slope * column(freq[...], 1)
    b_two = jnp.sum(slope, axis=1, keepdims=True)
    slope_low = slope.astype(low)
    shared[80 : 80 + units, 0:units] = dot_nt(filt[0].astype(low), slope_low)
    slope = dot_nn(w_mid[...].astype(low), slope_low) * filt[2]
    q_one = jnp.sum(slope * filt[4], axis=1, keepdims=True)
    slope = slope * column(freq[...], 0)
    b_one = jnp.sum(slope, axis=1, keepdims=True)
    shared[40 : 40 + feats, 0:units] = dot_nt(held[N.feat][...].astype(low), slope.astype(low))
    vectors = pack_columns([(0, b_one), (1, q_one), (2, b_two), (3, q_two)], units)
    shared[144:152, 0:units] = jnp.transpose(vectors)[0:8, :]

    for name in (N.tokens, N.gain, N.rgrad, N.extra):
        loads[name].wait()
    first_copy.wait()
    gain = held[N.gain][...][None, :]

    def norm_rows(index, carry):
        rows = pl.ds(pl.multiple_of(index * ROWS, ROWS), ROWS)
        own = pl.ds(pl.multiple_of(side * half_rows + index * ROWS, ROWS), ROWS)
        normed_rows, inverse = normed_parts(held[N.tokens][rows, :].astype(full))
        back = first[own, :] + first_recv[rows, :].astype(full)
        grad_rows = norm_rows_back(back, normed_rows, inverse, gain)
        out[N.input_grad][rows, :] = held[N.rgrad][rows, :] + grad_rows
        return (
            carry[0] + jnp.sum(back * normed_rows, axis=0, keepdims=True),
            carry[1] + jnp.sum(back, axis=0, keepdims=True),
        )

    zero = jnp.zeros((1, model_width), full)
    found = lax.fori_loop(0, half_rows // ROWS, norm_rows, (zero, zero))
    extra = held[N.extra]
    vectors = list(found) + [extra[i : i + 1, :] for i in range(4)]
    for index, vector in enumerate(vectors):
        for piece in range(model_width // 128):
            row = index * (model_width // 128) + piece
            shared[row : row + 1, :] = vector[:, piece * 128 : (piece + 1) * 128]

    shared_targets = [across, over] + flips

    def share(hop):
        copy = remote((N.shared, hop), shared, shared_hops.at[hop], shared_targets[hop])
        copy.start()
        return copy

    def shared_next(hop, copy):
        copy.wait()
        shared[...] = shared[...] + shared_hops[hop]
        return share(hop + 1) if hop < 4 else None

    def chan_next(hop, copy):
        copy.wait()
        chan[...] = chan[...] + chan_hops[hop]
        if hop == 2:
            return None
        copy = remote((N.chan, hop + 2), chan, chan_hops.at[hop + 1], flips[hop + 1])
        copy.start()
        return copy

    shared_copy = share(0)
    chan_copy = chan_next(0, chan_copy)
    copies[N.a] = hop_three(N.a, copies[N.a])
    shared_copy = shared_next(0, shared_copy)
    copies[N.y_b].wait()
    copies[N.b] = hop_two(N.b, sum_b, copies[N.b], hops[N.b][0])

    for name in (N.residual, N.down_near, N.down_bias):
        loads[name].wait()
    copies[N.downy].wait()
    slot = part * half_rows // length
    mask_rows = jnp.where(slot < counts[0], lengths[0, slot], 0) - part * half_rows % length
    down_bias = held[N.down_bias][...][None, :]

    def result_rows(index, carry):
        rows = pl.ds(pl.multiple_of(index * ROWS, ROWS), ROWS)
        total = held[N.residual][rows, :] + held[N.down_near][rows, :] + recv_down[rows, :].astype(full)
        place = lax.broadcasted_iota(jnp.int32, (ROWS, model_width), 0) + index * ROWS
        out[N.activations][rows, :] = jnp.where(place < mask_rows, total + down_bias, 0.0).astype(low)
        return carry

    lax.fori_loop(0, half_rows // ROWS, result_rows, 0)
    shared_copy = shared_next(1, shared_copy)
    chan_copy = chan_next(1, chan_copy)
    copies[N.b] = hop_three(N.b, copies[N.b])
    shared_copy = shared_next(2, shared_copy)
    for name in (N.up, N.down, N.a):
        out[name][...] = hop_last(name, copies[name])
    chan_next(2, chan_copy)
    shared_copy = shared_next(3, shared_copy)
    out[N.b][...] = hop_last(N.b, copies[N.b])
    shared_next(4, shared_copy)
    out[N.shared][...] = shared[...]
    out[N.chan][...] = chan[...]


PASSED = (N.activations, N.input_grad, N.up, N.down)


def lay_out(group_units, *refs):
    sources = dict(zip(RAW, refs[: len(RAW)]))
    outs = dict(zip(RESULTS, refs[len(RAW) : len(RAW) + len(RESULTS)]))
    held = dict(zip(RAW, refs[len(RAW) + len(RESULTS) : -1]))
    sem = refs[-1]
    group = lax.axis_index(DP)
    loads, passes = {}, []
    for index, name in enumerate(RAW):
        if name in PASSED:
            passes.append(pltpu.make_async_copy(sources[name], outs[name], sem.at[index]))
            passes[-1].start()
        else:
            loads[name] = pltpu.make_async_copy(sources[name], held[name], sem.at[index])
            loads[name].start()
    for copy in loads.values():
        copy.wait()
    part_a, part_b = jnp.transpose(held[N.a][...]), jnp.transpose(held[N.b][...])
    width = outs[N.out].shape[0]
    outs[N.in_w][0] = part_a[0:width, :]
    outs[N.in_w][1] = part_b[0:width, :]
    outs[N.in_w][2] = part_b[width:, :]
    outs[N.out][...] = part_a[width:, :]
    shared, chan = held[N.shared], held[N.chan]
    model_width = outs[N.up].shape[1]
    units = outs[N.w2].shape[0]
    pieces = model_width // 128
    for index, name in enumerate(WIDES):
        row = index * pieces
        lines = [shared[row + piece : row + piece + 1, :] for piece in range(pieces)]
        outs[name][...] = jnp.concatenate(lines, axis=1).reshape(model_width)
    outs[N.w1][...] = shared[40 : 40 + outs[N.w1].shape[0], 0:units]
    outs[N.w2][...] = shared[80 : 80 + units, 0:units]
    for index, name in enumerate(VECTORS):
        outs[name][...] = shared[144 + index : 145 + index, 0:units].reshape(units)
    outs[N.conv_w][...] = chan[0:9, :].reshape(3, 3, width)
    outs[N.in_b][...] = chan[9:12, :]
    outs[N.conv_b][...] = chan[12:15, :]
    outs[N.f_bias][...] = chan[15:16, :].reshape(width)
    lines = [chan[80 + index : 81 + index, :] for index in range(model_width // width)]
    outs[N.up_b][...] = jnp.concatenate(lines, axis=1).reshape(model_width)
    outs[N.w3][...] = chan[pl.ds(pl.multiple_of(16 + group * group_units, 8), group_units), :]
    for copy in passes:
        copy.wait()


def call_lay_out(raw, inputs_count, units, width):
    full, low = jnp.float32, jnp.bfloat16
    rows, model_width = raw[N.input_grad].shape
    block = raw[N.up].shape[0]
    shapes = {name: raw[name].shape for name in PASSED}
    shapes.update({name: (model_width,) for name in WIDES + (N.up_b,)})
    shapes.update({name: (units,) for name in VECTORS})
    shapes.update(
        {
            N.in_w: (3, width, block),
            N.out: (width, block),
            N.w1: (inputs_count, units),
            N.w2: (units, units),
            N.w3: (units // BLOCKS, width),
            N.conv_w: (3, 3, width),
            N.in_b: (3, width),
            N.conv_b: (3, width),
            N.f_bias: (width,),
        }
    )
    results = pl.pallas_call(
        functools.partial(lay_out, units // BLOCKS),
        out_shape=tuple(
            jax.ShapeDtypeStruct(shapes[name], low if name == N.activations else full) for name in RESULTS
        ),
        in_specs=[pl.BlockSpec(memory_space=pl.ANY)] * len(RAW),
        out_specs=tuple(pl.BlockSpec(memory_space=pltpu.VMEM) for name in RESULTS),
        scratch_shapes=[
            pltpu.VMEM((8, 128) if name in PASSED else raw[name].shape, full) for name in RAW
        ]
        + [pltpu.SemaphoreType.DMA((len(RAW),))],
        name="lay_out",
    )(*(raw[name] for name in RAW))
    return results


def call_operator_back(operands, counts, lengths, width, length, model_width, dp_count):
    full, low = jnp.float32, jnp.bfloat16
    units = operands[N.w_mid].shape[0]
    half_rows = length // 2
    block = model_width // BLOCKS
    thin_grads = pltpu.VMEM((model_width, model_width // 2), low)
    part_grads = pltpu.VMEM((model_width // 2, model_width // 2), low)
    low_rows = pltpu.VMEM((half_rows, model_width), low)
    held = []
    for name in LOADS:
        shape = operands[name].shape
        if name == N.resid:
            shape = (length, model_width)
        elif name in (N.w_in, N.w_out):
            shape = (16, 128)
        held.append(pltpu.VMEM(shape, operands[name].dtype))
    wide, thin = pltpu.VMEM((width, length), full), pltpu.VMEM((width, length), low)
    chan = pltpu.VMEM((88, width), full)
    shared = pltpu.VMEM((152, 128), full)
    scratch = held + [wide] * 3 + [thin] * 4
    scratch += [
        pltpu.VMEM((4 * width, model_width), full),
        pltpu.VMEM((3 * width, length), low),
        pltpu.VMEM((units, length), full),
        pltpu.VMEM((length, model_width), full),
        low_rows,
        low_rows,
        thin_grads,
        thin_grads,
        part_grads,
        part_grads,
        part_grads,
        part_grads,
        part_grads,
        part_grads,
        thin_grads,
        thin_grads,
        low_rows,
        pltpu.VMEM((width, 128), full),
        chan,
        chan,
        chan,
        pltpu.VMEM((3, 88, width), full),
        shared,
        pltpu.VMEM((5, 152, 128), full),
        pltpu.VMEM((4 * width, model_width), low),
    ]
    for columns in (model_width, model_width, model_width // 2, model_width // 2):
        scratch += [
            pltpu.VMEM((4 * block, columns), low),
            pltpu.VMEM((2 * block, columns), low),
            pltpu.VMEM((2 * block, columns), full),
            pltpu.VMEM((2 * block, columns), low),
            pltpu.VMEM((block, columns), low),
        ]
    scratch += [
        pltpu.SemaphoreType.DMA((len(LOADS) + len(SPLIT),)),
        pltpu.SemaphoreType.DMA((len(PLAN),)),
        pltpu.SemaphoreType.DMA((len(PLAN),)),
    ]
    shapes = {N.activations: (half_rows, model_width), N.input_grad: (half_rows, model_width)}
    shapes.update({N.up: (block, model_width), N.down: (block, model_width)})
    shapes.update({N.a: (block, model_width // 2), N.b: (block, model_width // 2)})
    shapes.update({N.shared: (152, 128), N.chan: (88, width)})
    outs = tuple(shapes)
    results = pl.pallas_call(
        functools.partial(operator_back, dp_count // BLOCKS, outs),
        out_shape=tuple(
            jax.ShapeDtypeStruct(shapes[name], low if name == N.activations else full) for name in outs
        ),
        in_specs=[pl.BlockSpec(memory_space=pl.ANY)] * (len(LOADS) + 1)
        + [pl.BlockSpec(memory_space=pltpu.SMEM)] * 2,
        out_specs=tuple(pl.BlockSpec(memory_space=pltpu.VMEM) for out in outs),
        scratch_shapes=scratch,
        compiler_params=pltpu.CompilerParams(
            vmem_limit_bytes=63 * 1024 * 1024, collective_id=0, has_side_effects=True
        ),
        cost_estimate=pl.CostEstimate(
            flops=4 * width * length * (10 * length + 8 * model_width),
            bytes_accessed=40 * 1024 * 1024,
            transcendentals=0,
        ),
        name="operator_back",
    )(*(operands[name] for name in LOADS), operands[N.down_far], counts, lengths)
    return dict(zip(outs, results))


def local(
    tokens,
    seq_counts,
    seq_lengths,
    norm1_gain,
    norm1_bias,
    in_weight,
    in_bias,
    conv_weight,
    conv_bias,
    filter_w1,
    filter_b1,
    filter_freq1,
    filter_w2,
    filter_b2,
    filter_freq2,
    filter_w3,
    filter_bias,
    out_weight,
    out_bias,
    norm2_gain,
    norm2_bias,
    up_weight,
    up_bias,
    down_weight,
    down_bias,
    cotangent,
):
    low = jnp.bfloat16
    full = jnp.float32
    tensor_count = lax.axis_size(TENSOR)
    dp_count = lax.axis_size(DP)
    row_share, model_width = tokens.shape
    width = in_weight.shape[1]
    slot_count = seq_lengths.shape[1]
    length = row_share * tensor_count // slot_count
    part = lax.axis_index(TENSOR)
    group = lax.axis_index(DP)

    inputs_count = filter_w1.shape[0]
    units = filter_w2.shape[0]
    flat_in = in_weight.reshape(3 * width, model_width)
    front = call_operator_front(
        {
            N.w_in: flat_in,
            N.w_out: out_weight,
            N.tokens: tokens,
            N.g1: norm1_gain,
            N.b1: norm1_bias,
            N.cw: conv_weight,
            N.ib: in_bias,
            N.cb: conv_bias,
            N.fb: filter_bias,
            N.w3: filter_w3,
            N.cot: cotangent,
            N.seeds: jnp.asarray(turn_seeds(length)),
            N.fw1: filter_w1,
            N.fw2: filter_w2,
            N.fb1: filter_b1,
            N.ff1: filter_freq1,
            N.fb2: filter_b2,
            N.ff2: filter_freq2,
            N.ob: out_bias,
            N.g2: norm2_gain,
            N.b2: norm2_bias,
            N.upb: up_bias,
            N.up: up_weight,
            N.down: down_weight,
        },
        seq_counts,
        seq_lengths,
        width,
        length,
        model_width,
        dp_count // BLOCKS,
    )
    back = call_operator_back(
        {
            N.resid: front[N.resid],
            N.w_peer: front[N.w_peer],
            N.w_in: flat_in,
            N.w_out: out_weight,
            N.streams: front[N.streams],
            N.proj: front[N.proj],
            N.conv: front[N.conv],
            N.par: front[N.par],
            N.table: front[N.table],
            N.factor: front[N.factor],
            N.signal: front[N.signal],
            N.normed: front[N.normed],
            N.filt: front[N.filt],
            N.w_last: front[N.w_last],
            N.up: front[N.up_g],
            N.down: front[N.down_g],
            N.up_r: front[N.up_r],
            N.down_r: front[N.down_r],
            N.down_far: front[N.down_far],
            N.w_mid: filter_w2,
            N.feat: front[N.feat],
            N.freq: front[N.freq],
            N.tokens: tokens,
            N.gain: norm1_gain,
            N.rgrad: front[N.residual_grad],
            N.extra: front[N.extra],
            N.upb: front[N.upb_g],
            N.residual: front[N.residual],
            N.down_near: front[N.down_near],
            N.down_bias: down_bias,
        },
        seq_counts,
        seq_lengths,
        width,
        length,
        model_width,
        dp_count,
    )
    if dp_count == BLOCKS:
        results = list(call_lay_out(back, inputs_count, units, width))
        place = RESULTS.index(N.down)
        results[place] = jnp.transpose(results[place])
        return tuple(results)

    rest = dp_count.bit_length() - BLOCKS.bit_length()

    def flips(bit_index):
        return [(i, i ^ (1 << bit_index)) for i in range(dp_count)]

    def rest_scatter(grad):
        for bit_index in range(rest):
            bit = (group >> bit_index) & 1
            kept = grad.reshape(1 << (rest - 1 - bit_index), 2, model_width // dp_count, -1)
            mine = lax.dynamic_index_in_dim(kept, bit, 1, keepdims=False)
            sent = lax.dynamic_index_in_dim(kept, 1 - bit, 1, keepdims=False)
            grad = mine + lax.ppermute(sent.astype(low), DP, flips(bit_index)).astype(full)
        return grad.reshape(model_width // dp_count, -1)

    def rest_sum(values):
        for bit_index in range(rest):
            values = values + lax.ppermute(values, DP, flips(bit_index))
        return values

    part_a, part_b = rest_scatter(back[N.a]), rest_scatter(back[N.b])
    operator_grads = jnp.concatenate([part_a[:, :width], part_b, part_a[:, width:]], axis=1)
    shared, chan = rest_sum(back[N.shared]), rest_sum(back[N.chan])
    wide = shared[: 6 * (model_width // 128)].reshape(6, model_width)
    share = units // dp_count
    grad_in = operator_grads[:, : 3 * width].reshape(-1, 3, width)
    return (
        back[N.activations],
        back[N.input_grad],
        wide[0],
        wide[1],
        jnp.transpose(grad_in, (1, 2, 0)),
        chan[9:12],
        chan[0:9].reshape(3, 3, width),
        chan[12:15],
        shared[40 : 40 + inputs_count, :units],
        shared[144, :units],
        shared[145, :units],
        shared[80 : 80 + units, :units],
        shared[146, :units],
        shared[147, :units],
        lax.dynamic_slice_in_dim(chan[16 : 16 + units], group * share, share, 0),
        chan[15],
        jnp.transpose(operator_grads[:, 3 * width :]),
        wide[2],
        wide[3],
        wide[4],
        rest_scatter(back[N.up]),
        chan[80 : 80 + model_width // width].reshape(-1),
        jnp.transpose(rest_scatter(back[N.down])),
        wide[5],
    )


def solution(mesh):
    in_specs = (
        P((DP, TENSOR), None),
        P(DP),
        P(DP, None),
        P(),
        P(),
        P(None, TENSOR, None),
        P(None, TENSOR),
        P(None, None, TENSOR),
        P(None, TENSOR),
        P(),
        P(),
        P(),
        P(),
        P(),
        P(),
        P(None, TENSOR),
        P(TENSOR),
        P(TENSOR, None),
        P(),
        P(),
        P(),
        P(None, TENSOR),
        P(TENSOR),
        P(TENSOR, None),
        P(),
        P((DP, TENSOR), None),
    )
    out_specs = (
        P((DP, TENSOR), None),
        P((DP, TENSOR), None),
        P(),
        P(),
        P(None, TENSOR, DP),
        P(None, TENSOR),
        P(None, None, TENSOR),
        P(None, TENSOR),
        P(),
        P(),
        P(),
        P(),
        P(),
        P(),
        P(DP, TENSOR),
        P(TENSOR),
        P(TENSOR, DP),
        P(),
        P(),
        P(),
        P(DP, TENSOR),
        P(TENSOR),
        P(TENSOR, DP),
        P(),
    )
    return jax.shard_map(local, mesh=mesh, in_specs=in_specs, out_specs=out_specs, check_vma=False)
```
